32 devices in a mesh: dp: 16 (over z, y, core), tensor: 2 (over x).
Axes of the slice: x: 2, y: 2, z: 4, core: 2. Of those that a mesh axis runs over, the one named last changes fastest.
Arguments:
- inputs: bfloat16 [64, 320, 1024], P(('dp', 'tensor')), may hold values from -6 to 6
- keep_mask: int32 [64, 256], P(('dp', 'tensor')), may hold values 0 or 1
- cotangent: bfloat16 [64, 320, 1024], P(('dp', 'tensor')), may hold values from -6 to 6
- ln1_gain: float32 [1024], replicated, may hold values from 0.1 to 1.9
- ln1_bias: float32 [1024], replicated, may hold values from -3 to 3
- w_qkv: bfloat16 [3, 1024, 1024], P(None, None, 'tensor'), may hold values from -0.1875 to 0.1875
- qv_bias: float32 [2, 1024], P(None, 'tensor'), may hold values from -2.5 to 2.5
- w_out: bfloat16 [1024, 1024], P('tensor'), may hold values from -0.75 to 0.75
- out_bias: float32 [1024], replicated, may hold values from -3 to 3
- ln2_gain: float32 [1024], replicated, may hold values from 0.1 to 1.9
- ln2_bias: float32 [1024], replicated, may hold values from -3 to 3
- w_fc1: bfloat16 [1024, 4096], P(None, 'tensor'), may hold values from -0.1875 to 0.1875
- fc1_bias: float32 [4096], P('tensor'), may hold values from -3 to 3
- w_fc2: bfloat16 [4096, 1024], P('tensor'), may hold values from -0.09375 to 0.09375
- fc2_bias: float32 [1024], replicated, may hold values from -3 to 3
Outputs:
- layer_out: bfloat16 [64, 320, 1024], P(('dp', 'tensor'))
- grad_input: bfloat16 [64, 320, 1024], P(('dp', 'tensor'))
- grad_ln1_gain: float32 [1024], replicated
- grad_ln1_bias: float32 [1024], replicated
- grad_qkv: float32 [3, 1024, 1024], P(None, None, 'tensor')
- grad_qv_bias: float32 [2, 1024], P(None, 'tensor')
- grad_out: float32 [1024, 1024], P('tensor')
- grad_out_bias: float32 [1024], replicated
- grad_ln2_gain: float32 [1024], replicated
- grad_ln2_bias: float32 [1024], replicated
- grad_fc1: float32 [1024, 4096], P(None, 'tensor')
- grad_fc1_bias: float32 [4096], P('tensor')
- grad_fc2: float32 [4096, 1024], P('tensor')
- grad_fc2_bias: float32 [1024], replicated
The draws below stay inside these ranges and needn't reach their ends.
Inputs may be any that keep to these rules, and one draw needn't show every extreme that they name: keep_mask is 1 for a kept slot and 0 for a masked one.
All inputs are finite; a program needn't handle non-finite values. No bound on the sum of `keep_mask` on one device may be relied on, other than what follows from the above.
Results may differ from the reference program's by a relative error of at most 0.02.
Values may be sent and summed in bfloat16 or wider, within the bound.
No kernel may reach another device: no remote copies, remote signals or barrier semaphores. Data moves between devices by JAX's collectives and lax.ppermute only.
A program may use at most 256 MiB of HBM per device.

```python
import jax
import jax.numpy as jnp
from jax import lax

D = 1024
HD = 64
FF = 4096
BUF = 64
SLOTS = 256
SEQ = 320
IMAGES = 64


def with_ends(array, key, low, high):
    longest = array.shape.index(max(array.shape))
    spots = []
    for shift in (0, 1):
        where = [jax.random.randint(jax.random.fold_in(key, axis), (), 0, length) for axis, length in enumerate(array.shape)]
        where[longest] = (where[longest] + shift) % array.shape[longest]
        spots.append(tuple(where))
    return array.at[spots[0]].set(low).at[spots[1]].set(high)


def steps_of(rng, shape, pieces, smallest, high):
    loudness, own = 1.0, jax.random.fold_in(rng, 6)
    for position, parts in pieces:
        draws = jnp.exp(jax.random.uniform(jax.random.fold_in(own, position), (parts,), jnp.float32, smallest / len(pieces), high / len(pieces)))
        loudness = loudness * jnp.repeat(draws, shape[position] // parts).reshape([-1 if axis == position else 1 for axis in range(len(shape))])
    return loudness


def normal_values(key, shape, width, reach, shards=(), dtype=jnp.bfloat16):
    values = width * jax.random.normal(key, shape, jnp.float32)
    if shards:
        values = values * steps_of(key, shape, shards, -0.22, 0.18)
    return jnp.clip(values, -reach, reach).astype(dtype)


def setup_inputs(seed: int = 0) -> dict:
    key_list = jax.random.split(jax.random.key(seed), 16)
    inputs = normal_values(key_list[0], (IMAGES, SEQ, D), 1.0, 6.0, ((0, 32),))
    keep_mask = with_ends((jax.random.randint(key_list[1], (IMAGES, SLOTS), 0, 8) < 3).astype(jnp.int32), jax.random.fold_in(key_list[1], 1), 0, 1)
    cotangent = normal_values(key_list[2], (IMAGES, SEQ, D), 1.0, 6.0, ((0, 32),))
    ln1_gain = jnp.clip(1.0 + 0.18 * jax.random.normal(key_list[3], (D,), jnp.float32), 0.1, 1.9)
    ln1_bias = normal_values(key_list[4], (D,), 0.3, 3.0, (), jnp.float32)
    w_qkv = normal_values(key_list[5], (3, D, D), D ** -0.5, 0.1875, ((2, 2),))
    qv_bias = normal_values(key_list[6], (2, D), 0.25, 2.5, ((1, 2),), jnp.float32)
    w_out = normal_values(key_list[7], (D, D), (D // 16) ** -0.5, 0.75, ((0, 2),))
    out_bias = normal_values(key_list[8], (D,), 0.3, 3.0, (), jnp.float32)
    ln2_gain = jnp.clip(1.0 + 0.18 * jax.random.normal(key_list[9], (D,), jnp.float32), 0.1, 1.9)
    ln2_bias = normal_values(key_list[10], (D,), 0.3, 3.0, (), jnp.float32)
    w_fc1 = normal_values(key_list[11], (D, FF), D ** -0.5, 0.1875, ((1, 2),))
    fc1_bias = normal_values(key_list[12], (FF,), 0.3, 3.0, ((0, 2),), jnp.float32)
    w_fc2 = normal_values(key_list[13], (FF, D), FF ** -0.5, 0.09375, ((0, 2),))
    fc2_bias = normal_values(key_list[14], (D,), 0.3, 3.0, (), jnp.float32)
    return {"inputs": inputs, "keep_mask": keep_mask, "cotangent": cotangent, "ln1_gain": ln1_gain, "ln1_bias": ln1_bias, "w_qkv": w_qkv, "qv_bias": qv_bias, "w_out": w_out, "out_bias": out_bias, "ln2_gain": ln2_gain, "ln2_bias": ln2_bias, "w_fc1": w_fc1, "fc1_bias": fc1_bias, "w_fc2": w_fc2, "fc2_bias": fc2_bias}


epsilon = 1e-06
group_images = 8

@jax.custom_vjp
def low(v):
    return lax.optimization_barrier(v.astype(jnp.bfloat16)).astype(jnp.float32)

@jax.custom_vjp
def low_back(v):
    return v

def low_keep(v):
    return (low(v), None)

def low_pass(kept, grad):
    return (grad,)

def back_keep(v):
    return (v, None)

def back_low(kept, grad):
    return (low(grad),)
low.defvjp(low_keep, low_pass)
low_back.defvjp(back_keep, back_low)

def layer_norm(values, gain_vec, shift_vec):
    row_mean = lax.optimization_barrier(jnp.mean(values, axis=-1, keepdims=True))
    centred = values - row_mean
    spread = lax.optimization_barrier(jnp.mean(centred * centred, axis=-1, keepdims=True))
    return centred * lax.rsqrt(spread + epsilon) * gain_vec + shift_vec

def forward(group_x, keep_rows, group_params):
    ln1_gain, ln1_bias, w_qkv, qv_bias, w_out, out_bias, ln2_gain, ln2_bias, w_fc1, fc1_bias, w_fc2, fc2_bias = group_params
    exact = lax.Precision.HIGHEST
    images, seq_len, model_width = group_x.shape
    head_count = model_width // HD
    normed1 = low(layer_norm(group_x, ln1_gain, ln1_bias))
    projected = jnp.einsum('isd,cde->cise', normed1, w_qkv, precision=exact)
    qkv_bias = jnp.stack([qv_bias[0], jnp.zeros_like(qv_bias[0]), qv_bias[1]])
    proj_rows = low_back(low(projected + qkv_bias[:, None, None, :]))
    query = proj_rows[0].reshape(images, seq_len, head_count, HD)
    key_rows = proj_rows[1].reshape(images, seq_len, head_count, HD)
    value = proj_rows[2].reshape(images, seq_len, head_count, HD)
    scores = low_back(jnp.einsum('iqhd,ikhd->ihqk', query, key_rows, precision=exact) * HD ** (-0.5))
    masked = jnp.where(keep_rows[:, None, None, :] > 0.5, scores, -1e+30)
    prob_low = low(jax.nn.softmax(masked, axis=-1))
    mixed = jnp.einsum('ihqk,ikhd->iqhd', prob_low, value, precision=exact)
    mixed = low_back(low(mixed.reshape(images, seq_len, model_width)))
    attn_rows = low_back(jnp.dot(mixed, w_out, precision=exact) + out_bias)
    mid = group_x + attn_rows
    normed2 = low(layer_norm(mid, ln2_gain, ln2_bias))
    pre_act = low_back(jnp.dot(normed2, w_fc1, precision=exact) + fc1_bias)
    act_low = low(jax.nn.gelu(pre_act, approximate=False))
    mlp_rows = low_back(jnp.dot(act_low, w_fc2, precision=exact) + fc2_bias)
    return keep_rows[:, :, None] * (mid + mlp_rows)

def reference(inputs, keep_mask, cotangent, ln1_gain, ln1_bias, w_qkv, qv_bias, w_out, out_bias, ln2_gain, ln2_bias, w_fc1, fc1_bias, w_fc2, fc2_bias):
    params = tuple((p.astype(jnp.float32) for p in (ln1_gain, ln1_bias, w_qkv, qv_bias, w_out, out_bias, ln2_gain, ln2_bias, w_fc1, fc1_bias, w_fc2, fc2_bias)))
    images, seq_len, model_width = inputs.shape
    groups = images // group_images
    keep_all = jnp.concatenate([jnp.ones((images, BUF), jnp.float32), keep_mask.astype(jnp.float32)], axis=1)

    def step_group(totals, item):
        group_x, group_keep, group_cot = item
        layer_rows, pull_back = jax.vjp(lambda xs, ps: forward(xs, group_keep, ps), group_x, params)
        grad_x, grad_params = pull_back(group_cot)
        totals = jax.tree.map(jnp.add, totals, grad_params)
        return (totals, (layer_rows.astype(jnp.bfloat16), grad_x.astype(jnp.bfloat16)))
    zeros = jax.tree.map(jnp.zeros_like, params)
    stacked = (inputs.astype(jnp.float32).reshape(groups, group_images, seq_len, model_width), keep_all.reshape(groups, group_images, seq_len), cotangent.astype(jnp.float32).reshape(groups, group_images, seq_len, model_width))
    totals, (layer_rows, grad_rows) = lax.scan(step_group, zeros, stacked)
    layer_out = layer_rows.reshape(images, seq_len, model_width)
    grad_input = grad_rows.reshape(images, seq_len, model_width)
    return (layer_out, grad_input, totals[0], totals[1], totals[2], totals[3], totals[4], totals[5], totals[6], totals[7], totals[8], totals[9], totals[10], totals[11])
```

```python
import functools

import jax
import jax.numpy as jnp
from jax import lax
from jax.experimental import pallas as pl
from jax.experimental.pallas import tpu as pltpu
from jax.sharding import Mesh, PartitionSpec as P

HD = 64
BUF = 64
EPS = 1e-06
CORES = 2
FAST = 192
LANES = 256
TILE = 512

f32 = jnp.float32
bf16 = jnp.bfloat16
NT = ((1,), (1,))
TN = ((0,), (0,))


def dot(a, b, dims=((1,), (0,))):
    return lax.dot_general(a, b, (dims, ((), ())), preferred_element_type=f32)


def spans(flags, seq_len, body):
    if seq_len <= FAST:
        body(seq_len)
        return

    @pl.when(flags[0] == 1)
    def _():
        body(FAST)

    @pl.when(flags[0] == 0)
    def _():
        body(seq_len)


def whole(shape):
    return pl.BlockSpec(shape, lambda *_: (0,) * len(shape), pipeline_mode=pl.Buffered(1))


def kernel_call(name, body, flags, args, in_specs, out_specs, out_shape, grid=(1,), **kw):
    return pl.pallas_call(
        body,
        name=name,
        grid_spec=pltpu.PrefetchScalarGridSpec(
            num_scalar_prefetch=1,
            grid=grid,
            in_specs=in_specs,
            out_specs=out_specs,
            scratch_shapes=kw.pop("scratch", ()),
        ),
        out_shape=out_shape,
        compiler_params=pltpu.CompilerParams(vmem_limit_bytes=kw.pop("vmem", 28 << 20)),
        cost_estimate=pl.CostEstimate(flops=1000, bytes_accessed=1000, transcendentals=0),
        **kw,
    )(flags, *args)


def picks(keep_row, span):
    seq_len = keep_row.shape[1]
    upto = lax.broadcasted_iota(jnp.int32, (seq_len, seq_len), 0) <= lax.broadcasted_iota(
        jnp.int32, (seq_len, seq_len), 1
    )
    keep_rows = jnp.broadcast_to(keep_row, (16, seq_len))
    rank = dot(keep_rows.astype(bf16), upto.astype(f32).astype(bf16))[0:1]
    place = lax.broadcasted_iota(jnp.int32, (span, seq_len), 0).astype(f32) + 1.0
    hit = jnp.where(place == rank, keep_row, 0.0)
    return hit.astype(bf16)


def norm_parts(values):
    centred = values - jnp.mean(values, axis=-1, keepdims=True)
    inverse = lax.rsqrt(jnp.mean(centred * centred, axis=-1, keepdims=True) + EPS)
    return centred * inverse, inverse


def norm_grad(grad_rows, unit, inverse, gain):
    scaled = grad_rows * gain
    centred = (
        scaled
        - jnp.mean(scaled, axis=-1, keepdims=True)
        - unit * jnp.mean(scaled * unit, axis=-1, keepdims=True)
    )
    return centred * inverse


def col_sum(values):
    return jnp.sum(values, axis=0, keepdims=True)


def prep_kernel(seq_len, images, flags, x, cot, keep, gain, bias, xc, normed, top, top_sum):
    def body(span):
        total = jnp.zeros(top_sum.shape, f32)
        for i in range(images):
            pick = picks(keep[i : i + 1, :], span)
            rows = slice(i * span, (i + 1) * span)
            source = slice(i * seq_len, (i + 1) * seq_len)
            kept = dot(pick, x[source, :])
            xc[rows, :] = kept.astype(bf16)
            normed[rows, :] = (norm_parts(kept)[0] * gain[...] + bias[...]).astype(bf16)
            grad = dot(pick, cot[source, :])
            top[rows, :] = grad.astype(bf16)
            total = total + col_sum(grad)
        top_sum[...] = total

    spans(flags, seq_len, body)


def head_masks(heads):
    lane = lax.broadcasted_iota(jnp.int32, (1, heads * HD), 1)
    return [(lane >= h * HD) & (lane < (h + 1) * HD) for h in range(heads)]


def softmax_rows(q, k, count):
    raw = dot(q, k, NT)
    column = lax.broadcasted_iota(jnp.int32, raw.shape, 1)
    raw = jnp.where(column < count, raw, -1e30)
    raised = jnp.exp(raw - jnp.max(raw, axis=-1, keepdims=True))
    return raised / jnp.sum(raised, axis=-1, keepdims=True)


def attend_kernel(seq_len, images, flags, normed, w, shift, proj, mixed):
    heads = mixed.shape[1] // HD

    def body(span):
        masks = head_masks(heads)
        for c in range(3):
            value = dot(normed[: images * span, :], w[c]) + shift[c]
            proj[c, : images * span, :] = value.astype(bf16)
        for i in range(images):
            rows = slice(i * span, (i + 1) * span)
            count = flags[1 + i]
            q, k, v = proj[0, rows, :], proj[1, rows, :], proj[2, rows, :]
            q = (q.astype(f32) * HD ** (-0.5)).astype(bf16)
            joined = jnp.zeros(q.shape, f32)
            for h in range(heads):
                probs = softmax_rows(jnp.where(masks[h], q, 0), k, count)
                joined = jnp.where(masks[h], dot(probs.astype(bf16), v), joined)
            mixed[rows, :] = joined.astype(bf16)

    spans(flags, seq_len, body)


def middle_kernel(seq_len, images, slots, flags, *refs):
    mixed, w, (xc, out_bias, gain, bias, mid, normed) = (
        refs[:slots],
        refs[slots : 2 * slots],
        refs[2 * slots :],
    )

    def body(span):
        for i in range(images):
            rows = slice(i * span, (i + 1) * span)
            total = xc[rows, :].astype(f32) + out_bias[...]
            for slot in range(slots):
                total = total + dot(mixed[slot][rows, :], w[slot][...])
            mid[rows, :] = total
            normed[rows, :] = (norm_parts(total)[0] * gain[...] + bias[...]).astype(bf16)

    spans(flags, seq_len, body)


def hidden_kernel(seq_len, images, flags, normed, w, bias, act, slope):
    def body(span):
        rows = images * span
        step = rows // 2
        for part in range(2):
            at = slice(part * step, (part + 1) * step)
            pre = dot(normed[at, :], w[...]) + bias[...]
            cdf = 0.5 * (1.0 + lax.erf(pre * 0.7071067811865476))
            act[at, :] = (pre * cdf).astype(bf16)
            slope[at, :] = (cdf + pre * jnp.exp(-0.5 * pre * pre) * 0.3989422804014327).astype(bf16)

    spans(flags, seq_len, body)


def ffn_kernel(seq_len, images, first, flags, act, slope, top, w2, w1, base, *refs):
    if first:
        total, grad_pre, grad_norm, sums = refs
        grad_base = None
    else:
        grad_base, total, grad_pre, grad_norm, sums = refs
    start = pl.program_id(0) == 0

    def body(span):
        rows = images * span

        @pl.when(start)
        def _():
            total[:rows, :] = base[:rows, :]
            if first:
                grad_norm[:rows, :] = jnp.zeros((rows, grad_norm.shape[1]), f32)
            else:
                grad_norm[:rows, :] = grad_base[:rows, :]

        total[:rows, :] += dot(act[:rows, :], w2[...])
        grad = dot(top[:rows, :], w2[...], NT) * slope[:rows, :].astype(f32)
        grad_pre[:rows, :] = grad.astype(bf16)
        sums[...] = col_sum(grad_pre[:rows, :].astype(f32))
        grad_norm[:rows, :] += dot(grad_pre[:rows, :], w1[...], NT)

    spans(flags, seq_len, body)


def mid_back_kernel(seq_len, images, flags, grad_norm, mid, top, gain, grad_mid, grad_attn, sums):
    def body(span):
        for i in range(images):
            rows = slice(i * span, (i + 1) * span)
            unit, inverse = norm_parts(mid[rows, :])
            grad = grad_norm[rows, :]
            full = top[rows, :].astype(f32) + norm_grad(grad, unit, inverse, gain[...])
            low = full.astype(bf16)
            grad_mid[rows, :] = full
            grad_attn[rows, :] = low
            part = [col_sum(grad * unit), col_sum(grad), col_sum(low.astype(f32))]
            for n, row in enumerate(part):
                sums[n : n + 1, :] = row if i == 0 else sums[n : n + 1, :] + row

    spans(flags, seq_len, body)


def attend_back_kernel(seq_len, images, first, flags, grad_attn, w_out, proj, w, *refs):
    if first:
        grad_proj, grad_norm, sums = refs
        base = None
    else:
        base, grad_proj, grad_norm, sums = refs
    heads = proj.shape[2] // HD
    start = pl.program_id(0) == 0

    def body(span):
        rows_all = images * span
        masks = head_masks(heads)

        @pl.when(start)
        def _():
            if first:
                grad_norm[:rows_all, :] = jnp.zeros((rows_all, grad_norm.shape[1]), f32)
            else:
                grad_norm[:rows_all, :] = base[:rows_all, :]

        for i in range(images):
            rows = slice(i * span, (i + 1) * span)
            count = flags[1 + i]
            grad_mixed = dot(grad_attn[rows, :], w_out[...], NT).astype(bf16)
            q, k, v = proj[0, rows, :], proj[1, rows, :], proj[2, rows, :]
            q_low = (q.astype(f32) * HD ** (-0.5)).astype(bf16)
            dq = jnp.zeros(q.shape, f32)
            dk, dv = dq, dq
            for h in range(heads):
                probs = softmax_rows(jnp.where(masks[h], q_low, 0), k, count)
                grad_prob = dot(jnp.where(masks[h], grad_mixed, 0), v, NT)
                delta = jnp.sum(probs * grad_prob, axis=-1, keepdims=True)
                grad_score = (probs * (grad_prob - delta)).astype(bf16)
                dv = jnp.where(masks[h], dot(probs.astype(bf16), grad_mixed, TN), dv)
                dq = jnp.where(masks[h], dot(grad_score, k), dq)
                dk = jnp.where(masks[h], dot(grad_score, q_low, TN), dk)
            grad_proj[0, rows, :] = (dq * HD ** (-0.5)).astype(bf16)
            grad_proj[1, rows, :] = dk.astype(bf16)
            grad_proj[2, rows, :] = dv.astype(bf16)
        for c in range(3):
            grad_norm[:rows_all, :] += dot(grad_proj[c, :rows_all, :], w[c], NT)
        sums[0:1, :] = col_sum(grad_proj[0, :rows_all, :].astype(f32))
        sums[1:2, :] = col_sum(grad_proj[2, :rows_all, :].astype(f32))

    spans(flags, seq_len, body)


def spread_kernel(seq_len, images, flags, value, bias, keep, out):
    def body(span):
        for i in range(images):
            rows = slice(i * span, (i + 1) * span)
            low = (value[rows, :] + bias[...]).astype(bf16)
            pick = picks(keep[i : i + 1, :], span)
            out[i * seq_len : (i + 1) * seq_len, :] = dot(pick, low, TN).astype(bf16)

    spans(flags, seq_len, body)


def last_kernel(seq_len, images, flags, grad_norm, xc, grad_mid, gain, keep, out, sums):
    def body(span):
        for i in range(images):
            rows = slice(i * span, (i + 1) * span)
            unit, inverse = norm_parts(xc[rows, :].astype(f32))
            grad = grad_norm[rows, :]
            low = (grad_mid[rows, :] + norm_grad(grad, unit, inverse, gain[...])).astype(bf16)
            pick = picks(keep[i : i + 1, :], span)
            out[i * seq_len : (i + 1) * seq_len, :] = dot(pick, low, TN).astype(bf16)
            part = [col_sum(grad * unit), col_sum(grad)]
            for n, row in enumerate(part):
                sums[n : n + 1, :] = row if i == 0 else sums[n : n + 1, :] + row

    spans(flags, seq_len, body)


def grad_kernel(seq_len, images, slots, flags, *refs):
    left, right, rest = refs[: len(slots)], refs[len(slots) : 2 * len(slots)], refs[2 * len(slots) :]
    out = rest[-1]

    def body(span):
        rows = images * span
        for n in range(len(slots)):
            value = dot(left[n][:rows, :], right[n][:rows, :], TN)
            for came in rest[:-1]:
                value = value + came[n].astype(f32)
            out[n] = value.astype(bf16)

    spans(flags, seq_len, body)


def last_grad_kernel(seq_len, images, first, slots, flags, normed, top, *refs):
    mixed, right, rest = (
        refs[: len(slots)],
        refs[len(slots) : 2 * len(slots)],
        refs[2 * len(slots) :],
    )
    out = rest[-1]

    def finish(n, value):
        for came in rest[:-1]:
            value = value + came[n, 0].astype(f32)
        out[n, 0] = value.astype(bf16)

    def body(span):
        rows = images * span
        which = first + pl.program_id(0)

        @pl.when(which == 0)
        def _():
            for n in range(len(slots)):
                finish(n, dot(top[:rows, :], mixed[n][:rows, :], TN))

        @pl.when(which > 0)
        def _():
            for n in range(len(slots)):
                finish(n, dot(normed[:rows, :], right[n][0, :rows, :], TN))

    spans(flags, seq_len, body)


def assemble_kernel(offsets, count, flags, *refs):
    pieces, out, sems = refs[:count], refs[count], refs[count + 1]
    copies = []
    for n, piece in enumerate(pieces):
        start = pl.multiple_of(offsets(flags)[n], 8)
        copy = pltpu.make_async_copy(piece, out.at[pl.ds(start, piece.shape[0]), :], sems.at[n])
        copy.start()
        copies.append(copy)
    for copy in copies:
        copy.wait()


def swap(value, axis, size, mask):
    return lax.ppermute(value, axis, [(i, i ^ mask) for i in range(size)])


def after(values, *waits):
    return lax.optimization_barrier((values, waits))[0]


def build(chips, tensor):
    def core_swap(value):
        return swap(value, "core", CORES, 1)

    def chip_swap(value, mask):
        return swap(value, "chip", chips, mask)

    def peer(value, slot):
        return swap(value, "tensor", tensor, slot)

    def local(
        inputs,
        keep_mask,
        cotangent,
        ln1_gain,
        ln1_bias,
        w_qkv,
        qv_bias,
        w_out,
        out_bias,
        ln2_gain,
        ln2_bias,
        w_fc1,
        fc1_bias,
        w_fc2,
        fc2_bias,
    ):
        images, seq_len, width = inputs.shape
        tokens = images * seq_len
        part = w_qkv.shape[2]
        hidden = w_fc1.shape[1]
        slots = range(tensor)
        others = range(1, tensor)
        lanes = min(LANES, part)
        tile = min(TILE, hidden)
        core, chip = lax.axis_index("core"), lax.axis_index("chip")
        low, high = chip & 1, (chip >> 1) & 1
        like = jax.ShapeDtypeStruct
        static = functools.partial
        row = lambda v: v.reshape(1, -1)

        keep = jnp.concatenate([jnp.ones((images, BUF), f32), keep_mask.astype(f32)], axis=1)
        counts = BUF + jnp.sum(keep_mask, axis=1)
        place = jnp.stack([core, low, high]).astype(jnp.int32)
        flags = jnp.concatenate([jnp.all(counts <= FAST).astype(jnp.int32)[None], counts, place])
        shape2 = (tokens, width)
        g1, b1, g2, b2 = row(ln1_gain), row(ln1_bias), row(ln2_gain), row(ln2_bias)


        class Box:
            def __init__(self, value):
                self.value = value
                opened.append(self)

        opened = []
        gate = Box(flags)

        def step():
            values = lax.optimization_barrier([box.value for box in opened])
            for box, value in zip(opened, values):
                box.value = value
            opened[:] = [gate]

        def run(name, body, args, in_specs, out_specs, out_shape, grid=(1,), **kw):
            args = [a.value if isinstance(a, Box) else a for a in args]
            got = kernel_call(
                name, body, gate.value, args, in_specs, out_specs, out_shape, grid, **kw
            )
            return [Box(g) for g in got] if isinstance(got, (list, tuple)) else Box(got)

        def start(move, value, *mask):
            value = value.value if isinstance(value, Box) else value
            return Box(move(after(value, gate.value), *mask))


        def assemble(pieces, offsets):
            rows = sum(p.value.shape[0] for p in pieces)
            shape = (rows, pieces[0].value.shape[1])
            return run(
                "assemble",
                static(assemble_kernel, offsets, len(pieces)),
                pieces,
                [pl.BlockSpec(memory_space=pl.ANY)] * len(pieces),
                whole(shape),
                like(shape, bf16),
                scratch=[pltpu.SemaphoreType.DMA((len(pieces),))],
            )

        class Fetch:
            def __init__(self, shard, mask):
                self.mask, self.rows = mask, shard.shape[0] // 4
                spot = core * 2 + (low if mask == 1 else high)
                piece = lax.dynamic_slice_in_dim(shard, spot * self.rows, self.rows, axis=0)
                self.mine = [start(peer, piece, slot) for slot in others]

            def second(self):
                self.beside = [start(chip_swap, m, self.mask) for m in self.mine]
                self.mine2 = [start(core_swap, m) for m in self.mine]

            def third(self):
                self.beside2 = [start(core_swap, m) for m in self.beside]

            def full(self):
                rows, at = self.rows, (2 if self.mask == 1 else 3) + images

                def offsets(f):
                    co, bit = f[1 + images], f[at]
                    return (
                        (2 * co + bit) * rows,
                        (2 * co + 1 - bit) * rows,
                        (2 * (1 - co) + bit) * rows,
                        (2 * (1 - co) + 1 - bit) * rows,
                    )

                return [
                    assemble(pieces, offsets)
                    for pieces in zip(self.mine, self.beside, self.mine2, self.beside2)
                ]


        half_of = lambda own: (lambda f: f[1 + images]) if own else (lambda f: 1 - f[1 + images])

        class Plain:
            def __init__(self, name, left, right, begin, size, block):
                self.name, self.left, self.right = name, left, right
                self.begin, self.size, self.block = begin, size, min(block, size)

            def make(self, which, own, came):
                pick = lambda v: [v[slot] if len(v) > 1 else v[0] for slot in which]
                left, right = pick(self.left), pick(self.right)
                block, first = self.block, self.begin // self.block
                per_half = left[0].value.shape[1] // 2 // block
                cols = right[0].value.shape[1]
                spot = pl.BlockSpec((len(which), block, cols), lambda g, f: (0, g, 0))
                half = half_of(own)
                return run(
                    f"{self.name}{which[0]}{'own' if own else 'away'}",
                    static(grad_kernel, seq_len, images, which),
                    (*left, *right, *came),
                    [
                        pl.BlockSpec((tokens, block), lambda g, f: (0, half(f) * per_half + first + g))
                        for _ in left
                    ]
                    + [whole((tokens, cols)) for _ in right]
                    + [spot] * len(came),
                    spot,
                    like((len(which), self.size, cols), bf16),
                    grid=(self.size // block,),
                )

        class Packed:
            def __init__(self, name, begin, size):
                self.name, self.begin, self.size = name, begin, size

            def make(self, which, own, came):
                begin, half = self.begin, half_of(own)
                mats = [mixes[slot] for slot in which]
                rights = [grad_projs[slot] for slot in which]
                spot = pl.BlockSpec((len(which), 1, width // 2, part), lambda g, f: (0, g, 0, 0))
                return run(
                    f"{self.name}{which[0]}{'own' if own else 'away'}",
                    static(last_grad_kernel, seq_len, images, begin, which),
                    (normed1, grad_attn, *mats, *rights, *came),
                    [pl.BlockSpec((tokens, width // 2), lambda g, f: (0, half(f)))] * 2
                    + [whole((tokens, part)) for _ in mats]
                    + [
                        pl.BlockSpec(
                            (1, tokens, part), lambda g, f: (jnp.maximum(begin + g - 1, 0), 0, 0)
                        )
                        for _ in rights
                    ]
                    + [spot] * len(came),
                    spot,
                    like((len(which), self.size, width // 2, part), bf16),
                    grid=(self.size,),
                )

        class Reduce:
            def __init__(self, source):
                self.source = source
                self.made, self.came, self.ready, self.sent = {}, {}, {}, []
                self.trail = []

            def k_away(self, *which):
                for slot in which:
                    self.made[slot] = self.source.make([slot], False, ())

            def t_core(self, *which):
                for slot in which:
                    self.came[slot] = start(core_swap, self.made[slot])

            def k_send(self):
                for slot in others:
                    self.ready[slot] = self.source.make([slot], True, (self.came[slot],))

            def t_x(self):
                self.sent = [start(peer, self.ready[slot], slot) for slot in others]

            def k_keep(self):
                total = self.source.make([0], True, (self.came[0], *self.sent))
                self.shape = total.value.shape
                self.held = total.value.reshape(-1, self.shape[-1])
                self.moving = None

            def settle(self):
                if self.moving is not None:
                    self.held = self.held.astype(f32) + self.moving.value.astype(f32)
                    self.moving = None

            def t_scatter(self, bit, mask):
                self.settle()
                size = self.held.shape[0] // 2
                sent = lax.dynamic_slice_in_dim(self.held, (1 - bit) * size, size).astype(bf16)
                self.held = lax.dynamic_slice_in_dim(self.held, bit * size, size)
                self.moving = start(chip_swap, sent, mask)

            def t_full(self):
                mask = 4
                while mask < chips:
                    self.settle()
                    self.held = self.held.astype(bf16)
                    self.moving = start(chip_swap, self.held, mask)
                    mask *= 2

            def t_y(self):
                self.t_scatter(low, 1)

            def t_z(self):
                self.t_scatter(high, 2)

            def t_up(self):
                self.settle()
                self.held = self.held.astype(bf16)
                self.moving = start(chip_swap, self.held, 2)

            def t_out(self):
                self.join(high)
                self.moving = start(chip_swap, self.held, 1)

            def join(self, bit):
                moving = self.moving.value
                self.held = jnp.where(
                    bit == 0,
                    jnp.concatenate([self.held, moving]),
                    jnp.concatenate([moving, self.held]),
                )

            def t_share(self):
                self.join(low)
                self.moving = start(core_swap, self.held)

        def joined(chunks):
            mine = [c.held for c in chunks]
            other = [c.moving.value for c in chunks]
            return jnp.where(
                core == 0, jnp.concatenate(mine + other), jnp.concatenate(other + mine)
            ).astype(f32)


        def attend(slot, w):
            qv = biases[slot].value[: 2 * part].reshape(2, 1, part)
            shift = jnp.stack([qv[0], jnp.zeros_like(qv[0]), qv[1]])
            return run(
                f"attend{slot}",
                static(attend_kernel, seq_len, images),
                (normed1, w, shift),
                [
                    whole(shape2),
                    pl.BlockSpec((3, width, lanes), lambda g, f: (0, 0, g)),
                    pl.BlockSpec((3, 1, lanes), lambda g, f: (0, 0, g)),
                ],
                [
                    pl.BlockSpec((3, tokens, lanes), lambda g, f: (0, 0, g)),
                    pl.BlockSpec((tokens, lanes), lambda g, f: (0, g)),
                ],
                [like((3, tokens, part), bf16), like((tokens, part), bf16)],
                grid=(part // lanes,),
            )

        def hide(slot):
            acts[slot], slopes[slot] = run(
                f"hidden{slot}",
                static(hidden_kernel, seq_len, images),
                (normed2, fc1[slot], row(biases[slot].value[2 * part :])),
                [
                    whole(shape2),
                    pl.BlockSpec((width, tile), lambda g, f: (0, g)),
                    pl.BlockSpec((1, tile), lambda g, f: (0, g)),
                ],
                [pl.BlockSpec((tokens, tile), lambda g, f: (0, g))] * 2,
                [like((tokens, hidden), bf16)] * 2,
                grid=(hidden // tile,),
            )

        def ffn(slot):
            nonlocal total, grad_norm2
            first = grad_norm2 is None
            tiles = pl.BlockSpec((tokens, tile), lambda g, f: (0, g))
            total, grad_pres[slot], grad_norm2, pre_sums[slot] = run(
                f"ffn{slot}",
                static(ffn_kernel, seq_len, images, first),
                (acts[slot], slopes[slot], top, fc2[slot], fc1[slot], total)
                + (() if first else (grad_norm2,)),
                [
                    tiles,
                    tiles,
                    whole(shape2),
                    pl.BlockSpec((tile, width), lambda g, f: (g, 0)),
                    pl.BlockSpec((width, tile), lambda g, f: (0, g)),
                    whole(shape2),
                ]
                + ([] if first else [whole(shape2)]),
                [whole(shape2), tiles, whole(shape2), pl.BlockSpec((1, tile), lambda g, f: (0, g))],
                [
                    like(shape2, f32),
                    like((tokens, hidden), bf16),
                    like(shape2, f32),
                    like((1, hidden), f32),
                ],
                grid=(hidden // tile,),
                vmem=36 << 20,
            )

        def attend_back(slot):
            nonlocal grad_norm1
            first = grad_norm1 is None
            tiles = pl.BlockSpec((3, tokens, lanes), lambda g, f: (0, 0, g))
            grad_projs[slot], grad_norm1, proj_sums[slot] = run(
                f"aback{slot}",
                static(attend_back_kernel, seq_len, images, first),
                (grad_attn, out[slot], projs[slot], qkv[slot]) + (() if first else (grad_norm1,)),
                [
                    whole(shape2),
                    pl.BlockSpec((lanes, width), lambda g, f: (g, 0)),
                    tiles,
                    pl.BlockSpec((3, width, lanes), lambda g, f: (0, 0, g)),
                ]
                + ([] if first else [whole(shape2)]),
                [tiles, whole(shape2), pl.BlockSpec((2, lanes), lambda g, f: (0, g))],
                [like((3, tokens, part), bf16), like(shape2, f32), like((2, part), f32)],
                grid=(part // lanes,),
            )

        acts, slopes = [None] * tensor, [None] * tensor
        total, grad_norm2 = None, None
        grad_pres, pre_sums = [None] * tensor, [None] * tensor
        grad_projs, proj_sums, grad_norm1 = [None] * tensor, [None] * tensor, None


        small = jnp.concatenate([qv_bias.reshape(-1), fc1_bias])
        get_qkv = Fetch(w_qkv.reshape(3 * width, part), 1)
        get_out = Fetch(w_out, 1)
        biases = [Box(small)] + [start(peer, small, slot) for slot in others]
        xc, normed1, top, top_sum = run(
            "prep",
            static(prep_kernel, seq_len, images),
            (inputs.reshape(shape2), cotangent.reshape(shape2), keep, g1, b1),
            [whole(shape2), whole(shape2), whole(keep.shape), whole(g1.shape), whole(b1.shape)],
            [whole(shape2), whole(shape2), whole(shape2), whole((1, width))],
            [like(shape2, bf16), like(shape2, bf16), like(shape2, bf16), like((1, width), f32)],
        )
        seen = [attend(0, w_qkv)]
        step()

        get_qkv.second()
        get_out.second()
        get_fc1 = Fetch(w_fc1, 2)
        step()

        get_qkv.third()
        get_out.third()
        get_fc1.second()
        get_fc2 = Fetch(w_fc2, 1)
        qkv = [w_qkv] + [w.value.reshape(3, width, part) for w in get_qkv.full()]
        for slot in others:
            seen.append(attend(slot, qkv[slot]))
        projs, mixes = [s[0] for s in seen], [s[1] for s in seen]
        out = [w_out] + get_out.full()
        mid, normed2 = run(
            "middle",
            static(middle_kernel, seq_len, images, tensor),
            (*mixes, *out, xc, row(out_bias), g2, b2),
            [whole((tokens, part))] * tensor
            + [whole((part, width))] * tensor
            + [whole(shape2), whole((1, width)), whole((1, width)), whole((1, width))],
            [whole(shape2), whole(shape2)],
            [like(shape2, f32), like(shape2, bf16)],
        )
        step()

        get_fc1.third()
        get_fc2.second()
        fc1 = [w_fc1] + get_fc1.full()
        for slot in others:
            hide(slot)
        rest = hidden // 4
        w1 = [Reduce(Plain(f"fc2{n}", acts, [top], n * rest, rest, TILE)) for n in range(2)]
        for p in w1:
            p.k_away(*others)
        step()

        for p in w1:
            p.t_core(*others)
        get_fc2.third()
        hide(0)
        fc2 = [w_fc2] + get_fc2.full()
        for p in w1:
            p.k_send()
        step()


        total = mid
        rest = width // 4
        w2 = [
            Reduce(Plain(f"fc1{n}", [normed2], grad_pres, n * rest, rest, 256)) for n in range(2)
        ]
        w1[0].t_x()
        for slot in others:
            ffn(slot)
        for p in w2:
            p.k_away(*others)
        for p in w1:
            p.k_away(0)
        step()

        w1[1].t_x()
        for p in w2:
            p.t_core(*others)
        for p in w1:
            p.t_core(0)
        ffn(0)
        for p in w2:
            p.k_send()
        w1[0].k_keep()
        step()

        w2[0].t_x()
        w1[0].t_y()
        w1[1].k_keep()
        grad_mid, grad_attn, sums2 = run(
            "midback",
            static(mid_back_kernel, seq_len, images),
            (grad_norm2, mid, top, g2),
            [whole(shape2), whole(shape2), whole(shape2), whole((1, width))],
            [whole(shape2), whole(shape2), whole((3, width))],
            [like(shape2, f32), like(shape2, bf16), like((3, width), f32)],
        )
        for slot in others:
            attend_back(slot)
        for p in w2:
            p.k_away(0)
        w3 = [Reduce(Packed("qkv0", 0, 2)), Reduce(Packed("qkv1", 2, 2))]
        for p in w3:
            p.k_away(*others)
        step()

        w2[1].t_x()
        w1[1].t_y()
        w1[0].t_z()
        for p in w2:
            p.t_core(0)
        for p in w3:
            p.t_core(*others)
        attend_back(0)
        for p in w3:
            p.k_send()
        w2[0].k_keep()
        step()

        w3[0].t_x()
        w2[0].t_y()
        w1[1].t_z()
        w1[0].t_full()
        w2[1].k_keep()
        for p in w3:
            p.k_away(0)
        grad_input, sums1 = run(
            "last",
            static(last_kernel, seq_len, images),
            (grad_norm1, xc, grad_mid, g1, keep),
            [whole(shape2), whole(shape2), whole(shape2), whole((1, width)), whole(keep.shape)],
            [whole(shape2), whole((2, width))],
            [like(shape2, bf16), like((2, width), f32)],
        )
        step()

        w3[1].t_x()
        for p in w3:
            p.t_core(0)
        w2[1].t_y()
        w2[0].t_z()
        w1[1].t_full()
        w1[0].t_up()
        w3[0].k_keep()
        layer_out = run(
            "spread",
            static(spread_kernel, seq_len, images),
            (total, row(fc2_bias), keep),
            [whole(shape2), whole((1, width)), whole(keep.shape)],
            whole(shape2),
            like(shape2, bf16),
        )
        step()

        w3[0].t_y()
        w2[1].t_z()
        w2[0].t_full()
        w1[1].t_up()
        w1[0].t_out()
        w3[1].k_keep()
        step()

        w3[1].t_y()
        w3[0].t_z()
        w2[1].t_full()
        w2[0].t_up()
        w1[1].t_out()
        w1[0].t_share()
        step()

        w3[1].t_z()
        w3[0].t_full()
        w2[1].t_up()
        w2[0].t_out()
        w1[1].t_share()
        step()

        w3[1].t_full()
        w3[0].t_up()
        w2[1].t_out()
        w2[0].t_share()
        step()

        w3[1].t_up()
        w3[0].t_out()
        w2[1].t_share()
        step()

        w3[1].t_out()
        w3[0].t_share()
        step()

        w3[1].t_share()
        grad_fc2, grad_fc1 = joined(w1), joined(w2)

        def unpacked(chunk):
            mine = chunk.held.reshape(-1, width // 2, part)
            other = chunk.moving.value.reshape(-1, width // 2, part)
            return jnp.where(
                core == 0,
                jnp.concatenate([mine, other], axis=1),
                jnp.concatenate([other, mine], axis=1),
            ).astype(f32)

        packs = [unpacked(p) for p in w3]
        grad_out = packs[0][0].T
        grad_qkv = jnp.concatenate([packs[0][1:], packs[1]])
        layer_out = layer_out.value.reshape(inputs.shape)
        grad_input = grad_input.value.reshape(inputs.shape)
        sums1, sums2, top_sum = sums1.value, sums2.value, top_sum.value
        proj_sums = [p.value for p in proj_sums]
        pre_sums = [p.value for p in pre_sums]

        common = jnp.concatenate([sums1.reshape(-1), sums2[2], sums2[0], sums2[1], top_sum[0]])
        owned = [
            jnp.concatenate([proj_sums[slot].reshape(-1), pre_sums[slot].reshape(-1), common])
            for slot in slots
        ]
        vector = owned[0]
        for slot in others:
            vector = vector + peer(owned[slot], slot)
        vector = vector + core_swap(vector)
        mask = 1
        while mask < chips:
            vector = vector + chip_swap(vector, mask)
            mask *= 2
        grad_qv_bias = vector[: 2 * part].reshape(2, part)
        grad_fc1_bias = vector[2 * part : 2 * part + hidden]
        rest = vector[2 * part + hidden :].reshape(6, width)
        return (
            layer_out,
            grad_input,
            rest[0],
            rest[1],
            grad_qkv,
            grad_qv_bias,
            grad_out,
            rest[2],
            rest[3],
            rest[4],
            grad_fc1,
            grad_fc1_bias,
            grad_fc2,
            rest[5],
        )

    return local


def solution(mesh):
    chips, tensor = mesh.shape["dp"] // CORES, mesh.shape["tensor"]
    finer = Mesh(mesh.devices.reshape(chips, CORES, tensor), ("chip", "core", "tensor"))
    rows = ("chip", "core", "tensor")
    return jax.shard_map(
        build(chips, tensor),
        mesh=finer,
        in_specs=(
            P(rows, None, None),
            P(rows, None),
            P(rows, None, None),
            P(),
            P(),
            P(None, None, "tensor"),
            P(None, "tensor"),
            P("tensor", None),
            P(),
            P(),
            P(),
            P(None, "tensor"),
            P("tensor"),
            P("tensor", None),
            P(),
        ),
        out_specs=(
            P(rows, None, None),
            P(rows, None, None),
            P(),
            P(),
            P(None, None, "tensor"),
            P(None, "tensor"),
            P("tensor", None),
            P(),
            P(),
            P(),
            P(None, "tensor"),
            P("tensor"),
            P("tensor", None),
            P(),
        ),
        check_vma=False,
    )
```

```python
import functools

import jax
import jax.numpy as jnp
from jax import lax
from jax.experimental import pallas as pl
from jax.experimental.pallas import tpu as pltpu
from jax.sharding import Mesh, PartitionSpec as P

HD = 64
BUF = 64
EPS = 1e-06
CORES = 2
FAST = 192
LANES = 256
TILE = 512

f32 = jnp.float32
bf16 = jnp.bfloat16
NT = ((1,), (1,))
TN = ((0,), (0,))


def dot(a, b, dims=((1,), (0,))):
    return lax.dot_general(a, b, (dims, ((), ())), preferred_element_type=f32)


def spans(flags, seq_len, body):
    if seq_len <= FAST:
        body(seq_len)
        return

    @pl.when(flags[0] == 1)
    def _():
        body(FAST)

    @pl.when(flags[0] == 0)
    def _():
        body(seq_len)


def whole(shape):
    return pl.BlockSpec(shape, lambda *_: (0,) * len(shape), pipeline_mode=pl.Buffered(1))


def kernel_call(name, body, flags, args, in_specs, out_specs, out_shape, grid=(1,), **kw):
    return pl.pallas_call(
        body,
        name=name,
        grid_spec=pltpu.PrefetchScalarGridSpec(
            num_scalar_prefetch=1,
            grid=grid,
            in_specs=in_specs,
            out_specs=out_specs,
            scratch_shapes=kw.pop("scratch", ()),
        ),
        out_shape=out_shape,
        compiler_params=pltpu.CompilerParams(vmem_limit_bytes=kw.pop("vmem", 28 << 20)),
        cost_estimate=pl.CostEstimate(flops=1000, bytes_accessed=1000, transcendentals=0),
        **kw,
    )(flags, *args)


def picks(keep_row, span):
    seq_len = keep_row.shape[1]
    upto = lax.broadcasted_iota(jnp.int32, (seq_len, seq_len), 0) <= lax.broadcasted_iota(
        jnp.int32, (seq_len, seq_len), 1
    )
    keep_rows = jnp.broadcast_to(keep_row, (16, seq_len))
    rank = dot(keep_rows.astype(bf16), upto.astype(f32).astype(bf16))[0:1]
    place = lax.broadcasted_iota(jnp.int32, (span, seq_len), 0).astype(f32) + 1.0
    hit = jnp.where(place == rank, keep_row, 0.0)
    return hit.astype(bf16)


def norm_parts(values):
    centred = values - jnp.mean(values, axis=-1, keepdims=True)
    inverse = lax.rsqrt(jnp.mean(centred * centred, axis=-1, keepdims=True) + EPS)
    return centred * inverse, inverse


def norm_grad(grad_rows, unit, inverse, gain):
    scaled = grad_rows * gain
    centred = (
        scaled
        - jnp.mean(scaled, axis=-1, keepdims=True)
        - unit * jnp.mean(scaled * unit, axis=-1, keepdims=True)
    )
    return centred * inverse


def col_sum(values):
    return jnp.sum(values, axis=0, keepdims=True)


def prep_kernel(seq_len, images, flags, x, cot, keep, gain, bias, xc, normed, top, top_sum):
    def body(span):
        total = jnp.zeros(top_sum.shape, f32)
        for i in range(images):
            pick = picks(keep[i : i + 1, :], span)
            rows = slice(i * span, (i + 1) * span)
            source = slice(i * seq_len, (i + 1) * seq_len)
            kept = dot(pick, x[source, :])
            xc[rows, :] = kept.astype(bf16)
            normed[rows, :] = (norm_parts(kept)[0] * gain[...] + bias[...]).astype(bf16)
            grad = dot(pick, cot[source, :])
            top[rows, :] = grad.astype(bf16)
            total = total + col_sum(grad)
        top_sum[...] = total

    spans(flags, seq_len, body)


def head_masks(heads):
    lane = lax.broadcasted_iota(jnp.int32, (1, heads * HD), 1)
    return [(lane >= h * HD) & (lane < (h + 1) * HD) for h in range(heads)]


def softmax_rows(q, k, count):
    raw = dot(q, k, NT)
    column = lax.broadcasted_iota(jnp.int32, raw.shape, 1)
    raw = jnp.where(column < count, raw, -1e30)
    raised = jnp.exp(raw - jnp.max(raw, axis=-1, keepdims=True))
    return raised / jnp.sum(raised, axis=-1, keepdims=True)


def attend_kernel(seq_len, images, flags, normed, w, shift, proj, mixed):
    heads = mixed.shape[1] // HD

    def body(span):
        masks = head_masks(heads)
        for c in range(3):
            value = dot(normed[: images * span, :], w[c]) + shift[c]
            proj[c, : images * span, :] = value.astype(bf16)
        for i in range(images):
            rows = slice(i * span, (i + 1) * span)
            count = flags[1 + i]
            q, k, v = proj[0, rows, :], proj[1, rows, :], proj[2, rows, :]
            q = (q.astype(f32) * HD ** (-0.5)).astype(bf16)
            joined = jnp.zeros(q.shape, f32)
            for h in range(heads):
                probs = softmax_rows(jnp.where(masks[h], q, 0), k, count)
                joined = jnp.where(masks[h], dot(probs.astype(bf16), v), joined)
            mixed[rows, :] = joined.astype(bf16)

    spans(flags, seq_len, body)


def middle_kernel(seq_len, images, slots, flags, *refs):
    mixed, w, (xc, out_bias, gain, bias, mid, normed) = (
        refs[:slots],
        refs[slots : 2 * slots],
        refs[2 * slots :],
    )

    def body(span):
        for i in range(images):
            rows = slice(i * span, (i + 1) * span)
            total = xc[rows, :].astype(f32) + out_bias[...]
            for slot in range(slots):
                total = total + dot(mixed[slot][rows, :], w[slot][...])
            mid[rows, :] = total
            normed[rows, :] = (norm_parts(total)[0] * gain[...] + bias[...]).astype(bf16)

    spans(flags, seq_len, body)


def hidden_kernel(seq_len, images, flags, normed, w, bias, act, slope):
    def body(span):
        rows = images * span
        step = rows // 2
        for part in range(2):
            at = slice(part * step, (part + 1) * step)
            pre = dot(normed[at, :], w[...]) + bias[...]
            cdf = 0.5 * (1.0 + lax.erf(pre * 0.7071067811865476))
            act[at, :] = (pre * cdf).astype(bf16)
            slope[at, :] = (cdf + pre * jnp.exp(-0.5 * pre * pre) * 0.3989422804014327).astype(bf16)

    spans(flags, seq_len, body)


def ffn_kernel(seq_len, images, first, flags, act, slope, top, w2, w1, base, *refs):
    if first:
        total, grad_pre, grad_norm, sums = refs
        grad_base = None
    else:
        grad_base, total, grad_pre, grad_norm, sums = refs
    start = pl.program_id(0) == 0

    def body(span):
        rows = images * span

        @pl.when(start)
        def _():
            total[:rows, :] = base[:rows, :]
            if first:
                grad_norm[:rows, :] = jnp.zeros((rows, grad_norm.shape[1]), f32)
            else:
                grad_norm[:rows, :] = grad_base[:rows, :]

        total[:rows, :] += dot(act[:rows, :], w2[...])
        grad = dot(top[:rows, :], w2[...], NT) * slope[:rows, :].astype(f32)
        grad_pre[:rows, :] = grad.astype(bf16)
        sums[...] = col_sum(grad_pre[:rows, :].astype(f32))
        grad_norm[:rows, :] += dot(grad_pre[:rows, :], w1[...], NT)

    spans(flags, seq_len, body)


def mid_back_kernel(seq_len, images, flags, grad_norm, mid, top, gain, grad_mid, grad_attn, sums):
    def body(span):
        for i in range(images):
            rows = slice(i * span, (i + 1) * span)
            unit, inverse = norm_parts(mid[rows, :])
            grad = grad_norm[rows, :]
            full = top[rows, :].astype(f32) + norm_grad(grad, unit, inverse, gain[...])
            low = full.astype(bf16)
            grad_mid[rows, :] = full
            grad_attn[rows, :] = low
            part = [col_sum(grad * unit), col_sum(grad), col_sum(low.astype(f32))]
            for n, row in enumerate(part):
                sums[n : n + 1, :] = row if i == 0 else sums[n : n + 1, :] + row

    spans(flags, seq_len, body)


def attend_back_kernel(seq_len, images, first, flags, grad_attn, w_out, proj, w, *refs):
    if first:
        grad_proj, grad_norm, sums = refs
        base = None
    else:
        base, grad_proj, grad_norm, sums = refs
    heads = proj.shape[2] // HD
    start = pl.program_id(0) == 0

    def body(span):
        rows_all = images * span
        masks = head_masks(heads)

        @pl.when(start)
        def _():
            if first:
                grad_norm[:rows_all, :] = jnp.zeros((rows_all, grad_norm.shape[1]), f32)
            else:
                grad_norm[:rows_all, :] = base[:rows_all, :]

        for i in range(images):
            rows = slice(i * span, (i + 1) * span)
            count = flags[1 + i]
            grad_mixed = dot(grad_attn[rows, :], w_out[...], NT).astype(bf16)
            q, k, v = proj[0, rows, :], proj[1, rows, :], proj[2, rows, :]
            q_low = (q.astype(f32) * HD ** (-0.5)).astype(bf16)
            dq = jnp.zeros(q.shape, f32)
            dk, dv = dq, dq
            for h in range(heads):
                probs = softmax_rows(jnp.where(masks[h], q_low, 0), k, count)
                grad_prob = dot(jnp.where(masks[h], grad_mixed, 0), v, NT)
                delta = jnp.sum(probs * grad_prob, axis=-1, keepdims=True)
                grad_score = (probs * (grad_prob - delta)).astype(bf16)
                dv = jnp.where(masks[h], dot(probs.astype(bf16), grad_mixed, TN), dv)
                dq = jnp.where(masks[h], dot(grad_score, k), dq)
                dk = jnp.where(masks[h], dot(grad_score, q_low, TN), dk)
            grad_proj[0, rows, :] = (dq * HD ** (-0.5)).astype(bf16)
            grad_proj[1, rows, :] = dk.astype(bf16)
            grad_proj[2, rows, :] = dv.astype(bf16)
        for c in range(3):
            grad_norm[:rows_all, :] += dot(grad_proj[c, :rows_all, :], w[c], NT)
        sums[0:1, :] = col_sum(grad_proj[0, :rows_all, :].astype(f32))
        sums[1:2, :] = col_sum(grad_proj[2, :rows_all, :].astype(f32))

    spans(flags, seq_len, body)


def spread_kernel(seq_len, images, flags, value, bias, keep, out):
    def body(span):
        for i in range(images):
            rows = slice(i * span, (i + 1) * span)
            low = (value[rows, :] + bias[...]).astype(bf16)
            pick = picks(keep[i : i + 1, :], span)
            out[i * seq_len : (i + 1) * seq_len, :] = dot(pick, low, TN).astype(bf16)

    spans(flags, seq_len, body)


def last_kernel(seq_len, images, flags, grad_norm, xc, grad_mid, gain, keep, out, sums):
    def body(span):
        for i in range(images):
            rows = slice(i * span, (i + 1) * span)
            unit, inverse = norm_parts(xc[rows, :].astype(f32))
            grad = grad_norm[rows, :]
            low = (grad_mid[rows, :] + norm_grad(grad, unit, inverse, gain[...])).astype(bf16)
            pick = picks(keep[i : i + 1, :], span)
            out[i * seq_len : (i + 1) * seq_len, :] = dot(pick, low, TN).astype(bf16)
            part = [col_sum(grad * unit), col_sum(grad)]
            for n, row in enumerate(part):
                sums[n : n + 1, :] = row if i == 0 else sums[n : n + 1, :] + row

    spans(flags, seq_len, body)


def grad_kernel(seq_len, images, slots, flags, *refs):
    left, right, rest = refs[: len(slots)], refs[len(slots) : 2 * len(slots)], refs[2 * len(slots) :]
    out = rest[-1]

    def body(span):
        rows = images * span
        for n in range(len(slots)):
            value = dot(left[n][:rows, :], right[n][:rows, :], TN)
            for came in rest[:-1]:
                value = value + came[n].astype(f32)
            out[n] = value.astype(bf16)

    spans(flags, seq_len, body)


def last_grad_kernel(seq_len, images, first, slots, flags, normed, top, *refs):
    mixed, right, rest = (
        refs[: len(slots)],
        refs[len(slots) : 2 * len(slots)],
        refs[2 * len(slots) :],
    )
    out = rest[-1]

    def finish(n, value):
        for came in rest[:-1]:
            value = value + came[n, 0].astype(f32)
        out[n, 0] = value.astype(bf16)

    def body(span):
        rows = images * span
        which = first + pl.program_id(0)

        @pl.when(which == 0)
        def _():
            for n in range(len(slots)):
                finish(n, dot(top[:rows, :], mixed[n][:rows, :], TN))

        @pl.when(which > 0)
        def _():
            for n in range(len(slots)):
                finish(n, dot(normed[:rows, :], right[n][0, :rows, :], TN))

    spans(flags, seq_len, body)


def assemble_kernel(spots, units, count, flags, *refs):
    pieces, outs, sems = refs[:count], refs[count:-1], refs[-1]
    copies = []
    for piece, places in zip(pieces, spots(flags)):
        begin = 0
        for out in outs:
            rows = out.shape[0] // units
            for c in range(0, out.shape[1], piece.shape[1]):
                for place in places:
                    copy = pltpu.make_async_copy(
                        piece.at[pl.ds(begin, rows), :],
                        out.at[
                            pl.ds(pl.multiple_of(place * rows, 16), rows), pl.ds(c, piece.shape[1])
                        ],
                        sems.at[len(copies)],
                    )
                    copy.start()
                    copies.append(copy)
                    begin += rows
    for copy in copies:
        copy.wait()


def place_kernel(count, flags, *refs):
    out = refs[count]
    for n in range(count):

        @pl.when(pl.program_id(0) == n)
        def _():
            out[...] = refs[n][...].astype(out.dtype)


def last_place_kernel(matrix, count, flags, *refs):
    pieces, (out, qkv) = refs[:count], refs[count:]
    for n in range(count):
        which = matrix(n, flags)

        @pl.when((pl.program_id(0) == n) & (which == 0))
        def _():
            out[...] = pieces[n][...].astype(f32).T

        @pl.when((pl.program_id(0) == n) & (which > 0))
        def _():
            qkv[0] = pieces[n][...].astype(f32)


def swap(value, axis, size, mask):
    return lax.ppermute(value, axis, [(i, i ^ mask) for i in range(size)])


def after(values, *waits):
    return lax.optimization_barrier((values, waits))[0]


def build(chips, tensor):
    def core_swap(value):
        return swap(value, "core", CORES, 1)

    def chip_swap(value, mask):
        return swap(value, "chip", chips, mask)

    def peer(value, slot):
        return swap(value, "tensor", tensor, slot)

    def local(
        inputs,
        keep_mask,
        cotangent,
        ln1_gain,
        ln1_bias,
        w_qkv,
        qv_bias,
        w_out,
        out_bias,
        ln2_gain,
        ln2_bias,
        w_fc1,
        fc1_bias,
        w_fc2,
        fc2_bias,
    ):
        images, seq_len, width = inputs.shape
        tokens = images * seq_len
        part = w_qkv.shape[2]
        hidden = w_fc1.shape[1]
        slots = range(tensor)
        others = range(1, tensor)
        lanes = min(LANES, part)
        tile = min(TILE, hidden)
        core, chip = lax.axis_index("core"), lax.axis_index("chip")
        low, high = chip & 1, (chip >> 1) & 1
        like = jax.ShapeDtypeStruct
        static = functools.partial
        row = lambda v: v.reshape(1, -1)

        keep = jnp.concatenate([jnp.ones((images, BUF), f32), keep_mask.astype(f32)], axis=1)
        counts = BUF + jnp.sum(keep_mask, axis=1)
        place = jnp.stack([core, low, high]).astype(jnp.int32)
        flags = jnp.concatenate([jnp.all(counts <= FAST).astype(jnp.int32)[None], counts, place])
        shape2 = (tokens, width)
        g1, b1, g2, b2 = row(ln1_gain), row(ln1_bias), row(ln2_gain), row(ln2_bias)


        class Box:
            def __init__(self, value):
                self.value = value
                opened.append(self)

        opened = []
        gate = Box(flags)

        def step():
            values = lax.optimization_barrier([box.value for box in opened])
            for box, value in zip(opened, values):
                box.value = value
            opened[:] = [gate]

        def run(name, body, args, in_specs, out_specs, out_shape, grid=(1,), **kw):
            args = [a.value if isinstance(a, Box) else a for a in args]
            got = kernel_call(
                name, body, gate.value, args, in_specs, out_specs, out_shape, grid, **kw
            )
            return [Box(g) for g in got] if isinstance(got, (list, tuple)) else Box(got)

        def start(move, value, *mask):
            value = value.value if isinstance(value, Box) else value
            return Box(move(after(value, gate.value), *mask))


        class Fetch:
            def __init__(self, shards, split):
                self.split, self.shards = split, shards
                units = self.units = 8 if split else 4
                own = self.places(core, low, high)[0]
                cols = min(w.shape[1] for w in shards)
                parts = []
                for w in shards:
                    rows = w.shape[0] // units
                    for c in range(0, w.shape[1], cols):
                        for place in own:
                            parts.append(
                                lax.dynamic_slice(w, (place * rows, c), (rows, min(cols, w.shape[1])))
                            )
                piece = jnp.concatenate(parts) if len(parts) > 1 else parts[0]
                self.mine = [start(peer, piece, slot) for slot in others]

            def places(self, co, lo, hi):
                if self.split:
                    return [(4 * co + lo, 4 * co + 2 + hi), (4 * co + 1 - lo,), (4 * co + 3 - hi,)]
                return [(2 * co + lo,), (2 * co + 1 - lo,)]

            def second(self):
                self.got = []
                for m in self.mine:
                    if self.split:
                        rows = m.value.shape[0] // 2
                        beside = [
                            start(chip_swap, m.value[:rows], 1),
                            start(chip_swap, m.value[rows:], 2),
                        ]
                    else:
                        beside = [start(chip_swap, m, 1)]
                    self.got.append([m, *beside, start(core_swap, m)])

            def third(self):
                for got in self.got:
                    got += [start(core_swap, g) for g in got[1:-1]]

            def full(self):
                shapes = [w.shape for w in self.shards]

                def spots(f):
                    co, lo, hi = f[1 + images], f[2 + images], f[3 + images]
                    return self.places(co, lo, hi) + self.places(1 - co, lo, hi)

                return [
                    run(
                        "assemble",
                        static(assemble_kernel, spots, self.units, len(got)),
                        got,
                        [pl.BlockSpec(memory_space=pl.ANY)] * len(got),
                        [whole(shape) for shape in shapes],
                        [like(shape, bf16) for shape in shapes],
                        scratch=[pltpu.SemaphoreType.DMA((16,))],
                    )
                    for got in self.got
                ]


        half_of = lambda own: (lambda f: f[1 + images]) if own else (lambda f: 1 - f[1 + images])

        class Plain:
            def __init__(self, name, left, right, block):
                self.name, self.left, self.right, self.block = name, left, right, block

            def make(self, which, own, came, begin=0, share=1):
                pick = lambda v: [v[slot] if len(v) > 1 else v[0] for slot in which]
                left, right = pick(self.left), pick(self.right)
                half_rows = left[0].value.shape[1] // 2
                size = half_rows // share
                block = min(self.block, size)
                first, per_half = begin * size // block, half_rows // block
                cols = right[0].value.shape[1]
                half = half_of(own)
                shape = (len(which), block, cols)
                spots = [
                    pl.BlockSpec(shape, lambda g, f, s=s, r=r: (s, r * (size // block) + g, 0))
                    for _, s, r in came
                ]
                return run(
                    f"{self.name}{which[0]}{'own' if own else 'away'}",
                    static(grad_kernel, seq_len, images, which),
                    (*left, *right, *[c for c, _, _ in came]),
                    [
                        pl.BlockSpec((tokens, block), lambda g, f: (0, half(f) * per_half + first + g))
                        for _ in left
                    ]
                    + [whole((tokens, cols)) for _ in right]
                    + spots,
                    pl.BlockSpec(shape, lambda g, f: (0, g, 0)),
                    like((len(which), size, cols), bf16),
                    grid=(size // block,),
                )

        class Packed:
            name = "qkv"

            def make(self, which, own, came, begin=0, share=1):
                size = 4 // share
                begin, half = begin * size, half_of(own)
                mats = [mixes[slot] for slot in which]
                rights = [grad_projs[slot] for slot in which]
                shape = (len(which), 1, width // 2, part)
                spots = [
                    pl.BlockSpec(shape, lambda g, f, s=s, r=r: (s, r * size + g, 0, 0))
                    for _, s, r in came
                ]
                came = [c for c, _, _ in came]
                return run(
                    f"{self.name}{which[0]}{'own' if own else 'away'}",
                    static(last_grad_kernel, seq_len, images, begin, which),
                    (normed1, grad_attn, *mats, *rights, *came),
                    [pl.BlockSpec((tokens, width // 2), lambda g, f: (0, half(f)))] * 2
                    + [whole((tokens, part)) for _ in mats]
                    + [
                        pl.BlockSpec(
                            (1, tokens, part), lambda g, f: (jnp.maximum(begin + g - 1, 0), 0, 0)
                        )
                        for _ in rights
                    ]
                    + spots,
                    pl.BlockSpec(shape, lambda g, f: (0, g, 0, 0)),
                    like((len(which), size, width // 2, part), bf16),
                    grid=(size,),
                )

        class Reduce:
            def __init__(self, source):
                self.source = source

            def k_away(self):
                self.made = self.source.make([*slots], False, ())

            def t_core(self):
                self.came = start(core_swap, self.made)

            def k_own(self):
                make, came = self.source.make, self.came
                self.first = [make([slot], True, [(came, slot, 0)], 0, 2) for slot in others]
                self.second = make([*slots], True, [(came, 0, 1)], 1, 2)

            def t_one(self):
                self.sent = [start(peer, value, slot) for value, slot in zip(self.first, others)]
                total = self.second.value
                total = total.reshape(tensor, -1, total.shape[-1])
                sent, self.held_b = halves(total, low, 1)
                self.moving_b = start(chip_swap, sent, 1)

            def k_mid(self):
                came = [(self.came, 0, 0)] + [(sent, 0, 0) for sent in self.sent]
                self.total = self.source.make([0], True, came, 0, 2)

            def t_two(self):
                total = self.total.value
                sent, self.held_a = halves(total.reshape(-1, total.shape[-1]), low, 0)
                self.moving_a = start(chip_swap, sent, 1)
                total = self.held_b.astype(f32) + self.moving_b.value.astype(f32)
                self.held_b = total[0]
                self.moving_b = [start(peer, total[slot].astype(bf16), slot) for slot in others]

            def t_z(self):
                total_a = self.held_a.astype(f32) + self.moving_a.value.astype(f32)
                total_b = self.held_b
                for moving in self.moving_b:
                    total_b = total_b + moving.value.astype(f32)
                self.held = jnp.where(high == 0, total_a, total_b)
                sent = jnp.where(high == 0, total_b, total_a).astype(bf16)
                self.moving = start(chip_swap, sent, 2)

            def t_full(self):
                mask = 4
                while mask < chips:
                    self.held = (self.held.astype(f32) + self.moving.value.astype(f32)).astype(bf16)
                    self.moving = start(chip_swap, self.held, mask)
                    mask *= 2

            def t_up(self):
                self.held = (self.held.astype(f32) + self.moving.value.astype(f32)).astype(bf16)
                self.moving = start(chip_swap, self.held, 2)

            def t_out(self):
                self.held = ordered(high, self.held, self.moving.value)
                self.moving = start(chip_swap, self.held, 1)

            def t_share(self):
                pieces = [self.held, self.moving.value]
                self.pieces = pieces + [start(core_swap, p) for p in pieces]

            def joined(self):
                pieces = self.pieces
                rows, cols = pieces[0].shape
                rows //= 2

                def spot(n):
                    return lambda w, i, f: (jnp.where(w == n, i, jnp.where(w < n, 0, 1)), 0)

                def place(w, i, f):
                    half = f[1 + images] ^ (w // 2)
                    return (half * 4 + i * 2 + (f[2 + images] ^ (w % 2)), 0)

                return run(
                    f"{self.source.name}join",
                    static(place_kernel, 4),
                    pieces,
                    [pl.BlockSpec((rows, cols), spot(n)) for n in range(4)],
                    pl.BlockSpec((rows, cols), place),
                    like((8 * rows, cols), f32),
                    grid=(4, 2),
                )

        def halves(value, bit, axis):
            size = value.shape[axis] // 2
            return (
                lax.dynamic_slice_in_dim(value, (1 - bit) * size, size, axis=axis),
                lax.dynamic_slice_in_dim(value, bit * size, size, axis=axis),
            )

        class Apart(Reduce):
            def t_one(self):
                self.sent = [start(peer, value, slot) for value, slot in zip(self.first, others)]
                total = self.second.value
                total = total.reshape(tensor, -1, total.shape[-1])
                sent, self.held_b = halves(total, high, 1)
                self.moving_b = start(chip_swap, sent, 2)

            def t_three(self):
                total_a = self.held_a.astype(f32) + self.moving_a.value.astype(f32)
                sent_a, self.held_a = halves(total_a, high, 0)
                total_b = self.held_b
                for moving in self.moving_b:
                    total_b = total_b + moving.value.astype(f32)
                sent_b, self.held_b = halves(total_b, low, 0)
                self.moving_a = start(chip_swap, sent_a.astype(bf16), 2)
                self.moving_b = start(chip_swap, sent_b.astype(bf16), 1)

            def t_full(self):
                held = [
                    h.astype(f32) + m.value.astype(f32)
                    for h, m in ((self.held_a, self.moving_a), (self.held_b, self.moving_b))
                ]
                self.held = jnp.concatenate(held).astype(bf16)
                self.moving = start(chip_swap, self.held, 4)
                mask = 8
                while mask < chips:
                    self.held = (self.held.astype(f32) + self.moving.value.astype(f32)).astype(bf16)
                    self.moving = start(chip_swap, self.held, mask)
                    mask *= 2

            def t_up(self):
                held, moving = (v.reshape(2, -1, v.shape[-1]) for v in (self.held, self.moving.value))
                self.held_a = (held[0].astype(f32) + moving[0].astype(f32)).astype(bf16)
                self.held_b = (held[1].astype(f32) + moving[1].astype(f32)).astype(bf16)
                self.moving_a = start(chip_swap, self.held_a, 2)
                self.moving_b = start(chip_swap, self.held_b, 1)

            def t_out(self):
                self.held_a = ordered(high, self.held_a, self.moving_a.value)
                self.held_b = ordered(low, self.held_b, self.moving_b.value)
                self.moving_a = start(chip_swap, self.held_a, 1)
                self.moving_b = start(chip_swap, self.held_b, 2)

            def t_share(self):
                pieces = [self.held_a, self.moving_a.value, self.held_b, self.moving_b.value]
                self.pieces = pieces + [start(core_swap, p) for p in pieces]

            def joined(self):
                def matrix(n, f):
                    bit = jnp.where(n % 4 < 2, f[2 + images], f[3 + images])
                    return 2 * ((n % 4) // 2) + (bit ^ (n % 2))

                half = width // 2
                return run(
                    "qkvjoin",
                    static(last_place_kernel, matrix, 8),
                    self.pieces,
                    [whole((half, part))] * 8,
                    [
                        pl.BlockSpec((part, half), lambda w, f: (0, f[1 + images] ^ (w // 4))),
                        pl.BlockSpec(
                            (1, half, part),
                            lambda w, f: (
                                jnp.maximum(matrix(w, f) - 1, 0),
                                f[1 + images] ^ (w // 4),
                                0,
                            ),
                        ),
                    ],
                    [like((part, width), f32), like((3, width, part), f32)],
                    grid=(8,),
                )

        def ordered(bit, mine, other):
            return jnp.where(
                bit == 0, jnp.concatenate([mine, other]), jnp.concatenate([other, mine])
            )


        def attend(slot, w):
            qv = biases[slot].value[: 2 * part].reshape(2, 1, part)
            shift = jnp.stack([qv[0], jnp.zeros_like(qv[0]), qv[1]])
            return run(
                f"attend{slot}",
                static(attend_kernel, seq_len, images),
                (normed1, w, shift),
                [
                    whole(shape2),
                    pl.BlockSpec((3, width, lanes), lambda g, f: (0, 0, g)),
                    pl.BlockSpec((3, 1, lanes), lambda g, f: (0, 0, g)),
                ],
                [
                    pl.BlockSpec((3, tokens, lanes), lambda g, f: (0, 0, g)),
                    pl.BlockSpec((tokens, lanes), lambda g, f: (0, g)),
                ],
                [like((3, tokens, part), bf16), like((tokens, part), bf16)],
                grid=(part // lanes,),
            )

        def hide(slot):
            acts[slot], slopes[slot] = run(
                f"hidden{slot}",
                static(hidden_kernel, seq_len, images),
                (normed2, fc1[slot], row(biases[slot].value[2 * part :])),
                [
                    whole(shape2),
                    pl.BlockSpec((width, tile), lambda g, f: (0, g)),
                    pl.BlockSpec((1, tile), lambda g, f: (0, g)),
                ],
                [pl.BlockSpec((tokens, tile), lambda g, f: (0, g))] * 2,
                [like((tokens, hidden), bf16)] * 2,
                grid=(hidden // tile,),
            )

        def ffn(slot):
            nonlocal total, grad_norm2
            first = grad_norm2 is None
            tiles = pl.BlockSpec((tokens, tile), lambda g, f: (0, g))
            total, grad_pres[slot], grad_norm2, pre_sums[slot] = run(
                f"ffn{slot}",
                static(ffn_kernel, seq_len, images, first),
                (acts[slot], slopes[slot], top, fc2[slot], fc1[slot], total)
                + (() if first else (grad_norm2,)),
                [
                    tiles,
                    tiles,
                    whole(shape2),
                    pl.BlockSpec((tile, width), lambda g, f: (g, 0)),
                    pl.BlockSpec((width, tile), lambda g, f: (0, g)),
                    whole(shape2),
                ]
                + ([] if first else [whole(shape2)]),
                [whole(shape2), tiles, whole(shape2), pl.BlockSpec((1, tile), lambda g, f: (0, g))],
                [
                    like(shape2, f32),
                    like((tokens, hidden), bf16),
                    like(shape2, f32),
                    like((1, hidden), f32),
                ],
                grid=(hidden // tile,),
                vmem=36 << 20,
            )

        def attend_back(slot):
            nonlocal grad_norm1
            first = grad_norm1 is None
            tiles = pl.BlockSpec((3, tokens, lanes), lambda g, f: (0, 0, g))
            grad_projs[slot], grad_norm1, proj_sums[slot] = run(
                f"aback{slot}",
                static(attend_back_kernel, seq_len, images, first),
                (grad_attn, out[slot], projs[slot], qkv[slot]) + (() if first else (grad_norm1,)),
                [
                    whole(shape2),
                    pl.BlockSpec((lanes, width), lambda g, f: (g, 0)),
                    tiles,
                    pl.BlockSpec((3, width, lanes), lambda g, f: (0, 0, g)),
                ]
                + ([] if first else [whole(shape2)]),
                [tiles, whole(shape2), pl.BlockSpec((2, lanes), lambda g, f: (0, g))],
                [like((3, tokens, part), bf16), like(shape2, f32), like((2, part), f32)],
                grid=(part // lanes,),
            )

        acts, slopes = [None] * tensor, [None] * tensor
        total, grad_norm2 = None, None
        grad_pres, pre_sums = [None] * tensor, [None] * tensor
        grad_projs, proj_sums, grad_norm1 = [None] * tensor, [None] * tensor, None


        get_attn = Fetch([w_qkv.reshape(3 * width, part), w_out], False)
        small = jnp.concatenate([qv_bias.reshape(-1), fc1_bias])
        biases = [Box(small)] + [start(peer, small, slot) for slot in others]
        xc, normed1, top, top_sum = run(
            "prep",
            static(prep_kernel, seq_len, images),
            (inputs.reshape(shape2), cotangent.reshape(shape2), keep, g1, b1),
            [whole(shape2), whole(shape2), whole(keep.shape), whole(g1.shape), whole(b1.shape)],
            [whole(shape2), whole(shape2), whole(shape2), whole((1, width))],
            [like(shape2, bf16), like(shape2, bf16), like(shape2, bf16), like((1, width), f32)],
        )
        seen = [attend(0, w_qkv)]
        step()

        get_attn.second()
        get_fc1 = Fetch([w_fc1], True)
        step()

        get_attn.third()
        get_fc1.second()
        qkv, out = [w_qkv], [w_out]
        for w, w_2 in get_attn.full():
            qkv.append(w.value.reshape(3, width, part))
            out.append(w_2)
        for slot in others:
            seen.append(attend(slot, qkv[slot]))
        projs, mixes = [s[0] for s in seen], [s[1] for s in seen]
        mid, normed2 = run(
            "middle",
            static(middle_kernel, seq_len, images, tensor),
            (*mixes, *out, xc, row(out_bias), g2, b2),
            [whole((tokens, part))] * tensor
            + [whole((part, width))] * tensor
            + [whole(shape2), whole((1, width)), whole((1, width)), whole((1, width))],
            [whole(shape2), whole(shape2)],
            [like(shape2, f32), like(shape2, bf16)],
        )
        step()

        get_fc1.third()
        get_fc2 = Fetch([w_fc2], True)
        fc1 = [w_fc1] + [w for w, in get_fc1.full()]
        for slot in slots:
            hide(slot)
        w1 = Reduce(Plain("fc2", acts, [top], TILE))
        w1.k_away()
        step()

        w1.t_core()
        get_fc2.second()
        w1.k_own()
        step()


        total = mid
        w1.t_one()
        get_fc2.third()
        fc2 = [w_fc2] + [w for w, in get_fc2.full()]
        for slot in slots:
            ffn(slot)
        w2 = Reduce(Plain("fc1", [normed2], grad_pres, 256))
        w2.k_away()
        step()

        w1.k_mid()
        step()

        w1.t_two()
        w2.t_core()
        grad_mid, grad_attn, sums2 = run(
            "midback",
            static(mid_back_kernel, seq_len, images),
            (grad_norm2, mid, top, g2),
            [whole(shape2), whole(shape2), whole(shape2), whole((1, width))],
            [whole(shape2), whole(shape2), whole((3, width))],
            [like(shape2, f32), like(shape2, bf16), like((3, width), f32)],
        )
        attend_back(0)
        step()

        w1.t_z()
        w2.k_own()
        step()

        w2.t_one()
        w1.t_full()
        for slot in others:
            attend_back(slot)
        w3 = Apart(Packed())
        w3.k_away()
        step()

        w2.k_mid()
        step()

        w2.t_two()
        w3.t_core()
        w1.t_up()
        grad_input, sums1 = run(
            "last",
            static(last_kernel, seq_len, images),
            (grad_norm1, xc, grad_mid, g1, keep),
            [whole(shape2), whole(shape2), whole(shape2), whole((1, width)), whole(keep.shape)],
            [whole(shape2), whole((2, width))],
            [like(shape2, bf16), like((2, width), f32)],
        )
        layer_out = run(
            "spread",
            static(spread_kernel, seq_len, images),
            (total, row(fc2_bias), keep),
            [whole(shape2), whole((1, width)), whole(keep.shape)],
            whole(shape2),
            like(shape2, bf16),
        )
        step()

        w2.t_z()
        w3.k_own()
        step()

        w3.t_one()
        w1.t_out()
        common = jnp.concatenate(
            [
                sums1.value.reshape(-1),
                sums2.value[2],
                sums2.value[0],
                sums2.value[1],
                top_sum.value[0],
            ]
        )
        owned = [
            jnp.concatenate(
                [proj_sums[slot].value.reshape(-1), pre_sums[slot].value.reshape(-1), common]
            )
            for slot in slots
        ]
        vector = owned[0]
        moving = [start(peer, owned[slot], slot) for slot in others]

        def add(*mask):
            nonlocal vector, moving
            for m in moving:
                vector = vector + m.value
            moving = [start(chip_swap if mask else core_swap, vector, *mask)] if mask != (0,) else []

        step()

        w3.k_mid()
        step()

        w3.t_two()
        w2.t_full()
        add()
        step()

        w3.t_three()
        w2.t_up()
        w1.t_share()
        add(1)
        step()

        w3.t_full()
        w2.t_out()
        add(2)
        grad_fc2 = w1.joined()
        step()

        w3.t_up()
        w2.t_share()
        mask = 4
        while mask < chips:
            add(mask)
            mask *= 2
        step()

        w3.t_out()
        add(0)
        grad_fc1 = w2.joined()
        step()

        w3.t_share()
        grad_out, grad_qkv = (g.value for g in w3.joined())
        layer_out = layer_out.value.reshape(inputs.shape)
        grad_input = grad_input.value.reshape(inputs.shape)
        grad_qv_bias = vector[: 2 * part].reshape(2, part)
        grad_fc1_bias = vector[2 * part : 2 * part + hidden]
        rest = vector[2 * part + hidden :].reshape(6, width)
        return (
            layer_out,
            grad_input,
            rest[0],
            rest[1],
            grad_qkv,
            grad_qv_bias,
            grad_out,
            rest[2],
            rest[3],
            rest[4],
            grad_fc1.value,
            grad_fc1_bias,
            grad_fc2.value,
            rest[5],
        )

    return local


def solution(mesh):
    chips, tensor = mesh.shape["dp"] // CORES, mesh.shape["tensor"]
    finer = Mesh(mesh.devices.reshape(chips, CORES, tensor), ("chip", "core", "tensor"))
    rows = ("chip", "core", "tensor")
    return jax.shard_map(
        build(chips, tensor),
        mesh=finer,
        in_specs=(
            P(rows, None, None),
            P(rows, None),
            P(rows, None, None),
            P(),
            P(),
            P(None, None, "tensor"),
            P(None, "tensor"),
            P("tensor", None),
            P(),
            P(),
            P(),
            P(None, "tensor"),
            P("tensor"),
            P("tensor", None),
            P(),
        ),
        out_specs=(
            P(rows, None, None),
            P(rows, None, None),
            P(),
            P(),
            P(None, None, "tensor"),
            P(None, "tensor"),
            P("tensor", None),
            P(),
            P(),
            P(),
            P(None, "tensor"),
            P("tensor"),
            P("tensor", None),
            P(),
        ),
        check_vma=False,
    )
```

```python
import functools

import jax
import jax.numpy as jnp
from jax import lax
from jax.experimental import pallas as pl
from jax.experimental.pallas import tpu as pltpu
from jax.sharding import Mesh, PartitionSpec as P

HD = 64
BUF = 64
EPS = 1e-06
CORES = 2
FAST = 192
LANES = 256
TILE = 512

f32 = jnp.float32
bf16 = jnp.bfloat16
NT = ((1,), (1,))
TN = ((0,), (0,))


def dot(a, b, dims=((1,), (0,))):
    return lax.dot_general(a, b, (dims, ((), ())), preferred_element_type=f32)


def spans(flags, seq_len, body):
    if seq_len <= FAST:
        body(seq_len)
        return

    @pl.when(flags[0] == 1)
    def _():
        body(FAST)

    @pl.when(flags[0] == 0)
    def _():
        body(seq_len)


def whole(shape):
    return pl.BlockSpec(shape, lambda *_: (0,) * len(shape), pipeline_mode=pl.Buffered(1))


def kernel_call(name, body, flags, args, in_specs, out_specs, out_shape, grid=(1,), **kw):
    return pl.pallas_call(
        body,
        name=name,
        grid_spec=pltpu.PrefetchScalarGridSpec(
            num_scalar_prefetch=1,
            grid=grid,
            in_specs=in_specs,
            out_specs=out_specs,
            scratch_shapes=kw.pop("scratch", ()),
        ),
        out_shape=out_shape,
        compiler_params=pltpu.CompilerParams(vmem_limit_bytes=kw.pop("vmem", 28 << 20)),
        cost_estimate=pl.CostEstimate(flops=1000, bytes_accessed=1000, transcendentals=0),
        **kw,
    )(flags, *args)


def picks(keep_row, span):
    seq_len = keep_row.shape[1]
    upto = lax.broadcasted_iota(jnp.int32, (seq_len, seq_len), 0) <= lax.broadcasted_iota(
        jnp.int32, (seq_len, seq_len), 1
    )
    keep_rows = jnp.broadcast_to(keep_row, (16, seq_len))
    rank = dot(keep_rows.astype(bf16), upto.astype(f32).astype(bf16))[0:1]
    place = lax.broadcasted_iota(jnp.int32, (span, seq_len), 0).astype(f32) + 1.0
    hit = jnp.where(place == rank, keep_row, 0.0)
    return hit.astype(bf16)


def norm_parts(values):
    centred = values - jnp.mean(values, axis=-1, keepdims=True)
    inverse = lax.rsqrt(jnp.mean(centred * centred, axis=-1, keepdims=True) + EPS)
    return centred * inverse, inverse


def norm_grad(grad_rows, unit, inverse, gain):
    scaled = grad_rows * gain
    centred = (
        scaled
        - jnp.mean(scaled, axis=-1, keepdims=True)
        - unit * jnp.mean(scaled * unit, axis=-1, keepdims=True)
    )
    return centred * inverse


def col_sum(values):
    return jnp.sum(values, axis=0, keepdims=True)


def prep_kernel(seq_len, images, flags, x, cot, keep, gain, bias, xc, normed, top, top_sum):
    def body(span):
        total = jnp.zeros(top_sum.shape, f32)
        for i in range(images):
            pick = picks(keep[i : i + 1, :], span)
            rows = slice(i * span, (i + 1) * span)
            source = slice(i * seq_len, (i + 1) * seq_len)
            kept = dot(pick, x[source, :])
            xc[rows, :] = kept.astype(bf16)
            normed[rows, :] = (norm_parts(kept)[0] * gain[...] + bias[...]).astype(bf16)
            grad = dot(pick, cot[source, :])
            top[rows, :] = grad.astype(bf16)
            total = total + col_sum(grad)
        top_sum[...] = total

    spans(flags, seq_len, body)


def head_masks(heads):
    lane = lax.broadcasted_iota(jnp.int32, (1, heads * HD), 1)
    return [(lane >= h * HD) & (lane < (h + 1) * HD) for h in range(heads)]


def softmax_rows(q, k, count):
    raw = dot(q, k, NT)
    column = lax.broadcasted_iota(jnp.int32, raw.shape, 1)
    raw = jnp.where(column < count, raw, -1e30)
    raised = jnp.exp(raw - jnp.max(raw, axis=-1, keepdims=True))
    return raised / jnp.sum(raised, axis=-1, keepdims=True)


def attend_kernel(seq_len, images, flags, normed, w, shift, proj, mixed):
    heads = mixed.shape[1] // HD

    def body(span):
        masks = head_masks(heads)
        for c in range(3):
            value = dot(normed[: images * span, :], w[c]) + shift[c]
            proj[c, : images * span, :] = value.astype(bf16)
        for i in range(images):
            rows = slice(i * span, (i + 1) * span)
            count = flags[1 + i]
            q, k, v = proj[0, rows, :], proj[1, rows, :], proj[2, rows, :]
            q = (q.astype(f32) * HD ** (-0.5)).astype(bf16)
            joined = jnp.zeros(q.shape, f32)
            for h in range(heads):
                probs = softmax_rows(jnp.where(masks[h], q, 0), k, count)
                joined = jnp.where(masks[h], dot(probs.astype(bf16), v), joined)
            mixed[rows, :] = joined.astype(bf16)

    spans(flags, seq_len, body)


def middle_kernel(seq_len, images, slots, flags, *refs):
    mixed, w, (xc, out_bias, gain, bias, mid, normed) = (
        refs[:slots],
        refs[slots : 2 * slots],
        refs[2 * slots :],
    )

    def body(span):
        for i in range(images):
            rows = slice(i * span, (i + 1) * span)
            total = xc[rows, :].astype(f32) + out_bias[...]
            for slot in range(slots):
                total = total + dot(mixed[slot][rows, :], w[slot][...])
            mid[rows, :] = total
            normed[rows, :] = (norm_parts(total)[0] * gain[...] + bias[...]).astype(bf16)

    spans(flags, seq_len, body)


def hidden_kernel(seq_len, images, flags, normed, w, bias, act, slope):
    def body(span):
        rows = images * span
        step = rows // 2
        for part in range(2):
            at = slice(part * step, (part + 1) * step)
            pre = dot(normed[at, :], w[...]) + bias[...]
            cdf = 0.5 * (1.0 + lax.erf(pre * 0.7071067811865476))
            act[at, :] = (pre * cdf).astype(bf16)
            slope[at, :] = (cdf + pre * jnp.exp(-0.5 * pre * pre) * 0.3989422804014327).astype(bf16)

    spans(flags, seq_len, body)


def ffn_kernel(seq_len, images, slots, flags, *refs):
    act, slope, w2, w1 = (refs[n * slots : (n + 1) * slots] for n in range(4))
    top, mid, bias, gain = refs[4 * slots : 4 * slots + 4]
    refs = refs[4 * slots + 4 :]
    grad_pre, pre_sums = refs[:slots], refs[slots : 2 * slots]
    low, grad_attn, sums, total, grad_norm = refs[2 * slots :]
    step, steps = pl.program_id(0), pl.num_programs(0)

    def body(span):
        rows = images * span

        @pl.when(step == 0)
        def _():
            total[:rows, :] = mid[:rows, :]
            grad_norm[:rows, :] = jnp.zeros((rows, grad_norm.shape[1]), f32)

        for slot in range(slots):

            @pl.when(step // (steps // slots) == slot)
            def _():
                total[:rows, :] += dot(act[slot][:rows, :], w2[slot][...])
                grad = dot(top[:rows, :], w2[slot][...], NT) * slope[slot][:rows, :].astype(f32)
                grad_pre[slot][:rows, :] = grad.astype(bf16)
                pre_sums[slot][...] = col_sum(grad_pre[slot][:rows, :].astype(f32))
                grad_norm[:rows, :] += dot(grad_pre[slot][:rows, :], w1[slot][...], NT)

        @pl.when(step == steps - 1)
        def _():
            for i in range(images):
                at = slice(i * span, (i + 1) * span)
                low[at, :] = (total[at, :] + bias[...]).astype(bf16)
                unit, inverse = norm_parts(mid[at, :])
                grad = grad_norm[at, :]
                full = top[at, :].astype(f32) + norm_grad(grad, unit, inverse, gain[...])
                grad_attn[at, :] = full.astype(bf16)
                part = [
                    col_sum(grad * unit),
                    col_sum(grad),
                    col_sum(grad_attn[at, :].astype(f32)),
                ]
                for n, row in enumerate(part):
                    sums[n : n + 1, :] = row if i == 0 else sums[n : n + 1, :] + row

    spans(flags, seq_len, body)


def attend_back_kernel(seq_len, images, first, flags, grad_attn, w_out, proj, w, *refs):
    if first:
        grad_proj, grad_norm, sums = refs
        base = None
    else:
        base, grad_proj, grad_norm, sums = refs
    heads = proj.shape[2] // HD
    start = pl.program_id(0) == 0

    def body(span):
        rows_all = images * span
        masks = head_masks(heads)

        @pl.when(start)
        def _():
            if first:
                grad_norm[:rows_all, :] = jnp.zeros((rows_all, grad_norm.shape[1]), f32)
            else:
                grad_norm[:rows_all, :] = base[:rows_all, :]

        for i in range(images):
            rows = slice(i * span, (i + 1) * span)
            count = flags[1 + i]
            grad_mixed = dot(grad_attn[rows, :], w_out[...], NT).astype(bf16)
            q, k, v = proj[0, rows, :], proj[1, rows, :], proj[2, rows, :]
            q_low = (q.astype(f32) * HD ** (-0.5)).astype(bf16)
            dq = jnp.zeros(q.shape, f32)
            dk, dv = dq, dq
            for h in range(heads):
                probs = softmax_rows(jnp.where(masks[h], q_low, 0), k, count)
                grad_prob = dot(jnp.where(masks[h], grad_mixed, 0), v, NT)
                delta = jnp.sum(probs * grad_prob, axis=-1, keepdims=True)
                grad_score = (probs * (grad_prob - delta)).astype(bf16)
                dv = jnp.where(masks[h], dot(probs.astype(bf16), grad_mixed, TN), dv)
                dq = jnp.where(masks[h], dot(grad_score, k), dq)
                dk = jnp.where(masks[h], dot(grad_score, q_low, TN), dk)
            grad_proj[0, rows, :] = (dq * HD ** (-0.5)).astype(bf16)
            grad_proj[1, rows, :] = dk.astype(bf16)
            grad_proj[2, rows, :] = dv.astype(bf16)
        for c in range(3):
            grad_norm[:rows_all, :] += dot(grad_proj[c, :rows_all, :], w[c], NT)
        sums[0:1, :] = col_sum(grad_proj[0, :rows_all, :].astype(f32))
        sums[1:2, :] = col_sum(grad_proj[2, :rows_all, :].astype(f32))

    spans(flags, seq_len, body)


def spread_kernel(seq_len, images, flags, value, keep, out):
    def body(span):
        for i in range(images):
            rows = slice(i * span, (i + 1) * span)
            pick = picks(keep[i : i + 1, :], span)
            out[i * seq_len : (i + 1) * seq_len, :] = dot(pick, value[rows, :], TN).astype(bf16)

    spans(flags, seq_len, body)


def last_kernel(seq_len, images, flags, grad_norm, xc, grad_attn, gain, keep, out, sums):
    def body(span):
        for i in range(images):
            rows = slice(i * span, (i + 1) * span)
            unit, inverse = norm_parts(xc[rows, :].astype(f32))
            grad = grad_norm[rows, :]
            low = grad_attn[rows, :].astype(f32) + norm_grad(grad, unit, inverse, gain[...])
            low = low.astype(bf16)
            pick = picks(keep[i : i + 1, :], span)
            out[i * seq_len : (i + 1) * seq_len, :] = dot(pick, low, TN).astype(bf16)
            part = [col_sum(grad * unit), col_sum(grad)]
            for n, row in enumerate(part):
                sums[n : n + 1, :] = row if i == 0 else sums[n : n + 1, :] + row

    spans(flags, seq_len, body)


def grad_kernel(seq_len, images, slots, flags, *refs):
    left, right, rest = refs[: len(slots)], refs[len(slots) : 2 * len(slots)], refs[2 * len(slots) :]
    out = rest[-1]

    def body(span):
        rows = images * span
        for n in range(len(slots)):
            value = dot(left[n][:rows, :], right[n][:rows, :], TN)
            for came in rest[:-1]:
                value = value + came[n].astype(f32)
            out[n] = value.astype(bf16)

    spans(flags, seq_len, body)


def last_grad_kernel(seq_len, images, first, slots, flags, normed, top, *refs):
    mixed, right, rest = (
        refs[: len(slots)],
        refs[len(slots) : 2 * len(slots)],
        refs[2 * len(slots) :],
    )
    out = rest[-1]

    def finish(n, value):
        for came in rest[:-1]:
            value = value + came[n, 0].astype(f32)
        out[n, 0] = value.astype(bf16)

    def body(span):
        rows = images * span
        which = first + pl.program_id(0)

        @pl.when(which == 0)
        def _():
            for n in range(len(slots)):
                finish(n, dot(top[:rows, :], mixed[n][:rows, :], TN))

        @pl.when(which > 0)
        def _():
            for n in range(len(slots)):
                finish(n, dot(normed[:rows, :], right[n][0, :rows, :], TN))

    spans(flags, seq_len, body)


def assemble_kernel(spots, units, count, flags, *refs):
    pieces, outs, sems = refs[:count], refs[count:-1], refs[-1]
    copies = []
    for piece, places in zip(pieces, spots(flags)):
        begin = 0
        for out in outs:
            rows = out.shape[0] // units
            for c in range(0, out.shape[1], piece.shape[1]):
                for place in places:
                    copy = pltpu.make_async_copy(
                        piece.at[pl.ds(begin, rows), :],
                        out.at[
                            pl.ds(pl.multiple_of(place * rows, 16), rows), pl.ds(c, piece.shape[1])
                        ],
                        sems.at[len(copies)],
                    )
                    copy.start()
                    copies.append(copy)
                    begin += rows
    for copy in copies:
        copy.wait()


def place_kernel(count, flags, *refs):
    out = refs[count]
    for n in range(count):

        @pl.when(pl.program_id(0) == n)
        def _():
            out[...] = refs[n][...].astype(out.dtype)


def last_place_kernel(matrix, flags, *refs):
    pieces, (out, qkv) = refs[:4], refs[-2:]
    for n in range(4):
        which = matrix(n, flags)

        @pl.when((pl.program_id(0) == n) & (which == 0))
        def _():
            out[...] = pieces[n][...].astype(f32).T

        @pl.when((pl.program_id(0) == n) & (which > 0))
        def _():
            qkv[0] = pieces[n][...].astype(f32)


def swap(value, axis, size, mask):
    return lax.ppermute(value, axis, [(i, i ^ mask) for i in range(size)])


def after(values, *waits):
    return lax.optimization_barrier((values, waits))[0]


def build(chips, tensor):
    def core_swap(value):
        return swap(value, "core", CORES, 1)

    def chip_swap(value, mask):
        return swap(value, "chip", chips, mask)

    def peer(value, slot):
        return swap(value, "tensor", tensor, slot)

    def local(
        inputs,
        keep_mask,
        cotangent,
        ln1_gain,
        ln1_bias,
        w_qkv,
        qv_bias,
        w_out,
        out_bias,
        ln2_gain,
        ln2_bias,
        w_fc1,
        fc1_bias,
        w_fc2,
        fc2_bias,
    ):
        images, seq_len, width = inputs.shape
        tokens = images * seq_len
        part = w_qkv.shape[2]
        hidden = w_fc1.shape[1]
        slots = range(tensor)
        others = range(1, tensor)
        lanes = min(LANES, part)
        tile = min(TILE, hidden)
        core, chip = lax.axis_index("core"), lax.axis_index("chip")
        low, high = chip & 1, (chip >> 1) & 1
        like = jax.ShapeDtypeStruct
        static = functools.partial
        row = lambda v: v.reshape(1, -1)

        keep = jnp.concatenate([jnp.ones((images, BUF), f32), keep_mask.astype(f32)], axis=1)
        counts = BUF + jnp.sum(keep_mask, axis=1)
        place = jnp.stack([core, low, high]).astype(jnp.int32)
        flags = jnp.concatenate([jnp.all(counts <= FAST).astype(jnp.int32)[None], counts, place])
        shape2 = (tokens, width)
        g1, b1, g2, b2 = row(ln1_gain), row(ln1_bias), row(ln2_gain), row(ln2_bias)


        class Box:
            def __init__(self, value):
                self.value = value
                opened.append(self)

        opened = []
        gate = Box(flags)

        def step():
            values = lax.optimization_barrier([box.value for box in opened])
            for box, value in zip(opened, values):
                box.value = value
            opened[:] = [gate]

        def run(name, body, args, in_specs, out_specs, out_shape, grid=(1,), **kw):
            args = [a.value if isinstance(a, Box) else a for a in args]
            got = kernel_call(
                name, body, gate.value, args, in_specs, out_specs, out_shape, grid, **kw
            )
            return [Box(g) for g in got] if isinstance(got, (list, tuple)) else Box(got)

        def start(move, value, *mask):
            value = value.value if isinstance(value, Box) else value
            return Box(move(after(value, gate.value), *mask))


        class Fetch:
            def __init__(self, shards, split):
                self.split, self.shards = split, shards
                units = self.units = 8 if split else 4
                own = self.places(core, low, high)[0]
                cols = min(w.shape[1] for w in shards)
                parts = []
                for w in shards:
                    rows = w.shape[0] // units
                    for c in range(0, w.shape[1], cols):
                        for place in own:
                            parts.append(
                                lax.dynamic_slice(w, (place * rows, c), (rows, min(cols, w.shape[1])))
                            )
                piece = jnp.concatenate(parts) if len(parts) > 1 else parts[0]
                self.mine = [start(peer, piece, slot) for slot in others]

            def places(self, co, lo, hi):
                if self.split:
                    return [(4 * co + lo, 4 * co + 2 + hi), (4 * co + 1 - lo,), (4 * co + 3 - hi,)]
                return [(2 * co + lo,), (2 * co + 1 - lo,)]

            def second(self):
                self.got = []
                for m in self.mine:
                    if self.split:
                        rows = m.value.shape[0] // 2
                        beside = [
                            start(chip_swap, m.value[:rows], 1),
                            start(chip_swap, m.value[rows:], 2),
                        ]
                    else:
                        beside = [start(chip_swap, m, 1)]
                    self.got.append([m, *beside, start(core_swap, m)])

            def third(self):
                for got in self.got:
                    got += [start(core_swap, g) for g in got[1:-1]]

            def full(self):
                shapes = [w.shape for w in self.shards]

                def spots(f):
                    co, lo, hi = f[1 + images], f[2 + images], f[3 + images]
                    return self.places(co, lo, hi) + self.places(1 - co, lo, hi)

                return [
                    run(
                        "assemble",
                        static(assemble_kernel, spots, self.units, len(got)),
                        got,
                        [pl.BlockSpec(memory_space=pl.ANY)] * len(got),
                        [whole(shape) for shape in shapes],
                        [like(shape, bf16) for shape in shapes],
                        scratch=[pltpu.SemaphoreType.DMA((16,))],
                    )
                    for got in self.got
                ]


        half_of = lambda own: (lambda f: f[1 + images]) if own else (lambda f: 1 - f[1 + images])

        class Plain:
            def __init__(self, name, left, right, block):
                self.name, self.left, self.right, self.block = name, left, right, block

            def make(self, which, own, came, begin=0, share=1):
                pick = lambda v: [v[slot] if len(v) > 1 else v[0] for slot in which]
                left, right = pick(self.left), pick(self.right)
                half_rows = left[0].value.shape[1] // 2
                size = half_rows // share
                block = min(self.block, size)
                first, per_half = begin * size // block, half_rows // block
                cols = right[0].value.shape[1]
                half = half_of(own)
                shape = (len(which), block, cols)
                spots = [
                    pl.BlockSpec(shape, lambda g, f, s=s, r=r: (s, r * (size // block) + g, 0))
                    for _, s, r in came
                ]
                return run(
                    f"{self.name}{which[0]}{'own' if own else 'away'}",
                    static(grad_kernel, seq_len, images, which),
                    (*left, *right, *[c for c, _, _ in came]),
                    [
                        pl.BlockSpec((tokens, block), lambda g, f: (0, half(f) * per_half + first + g))
                        for _ in left
                    ]
                    + [whole((tokens, cols)) for _ in right]
                    + spots,
                    pl.BlockSpec(shape, lambda g, f: (0, g, 0)),
                    like((len(which), size, cols), bf16),
                    grid=(size // block,),
                )

        class Packed:
            name = "qkv"

            def make(self, which, own, came, begin=0, share=1):
                size = 4 // share
                begin, half = begin * size, half_of(own)
                mats = [mixes[slot] for slot in which]
                rights = [grad_projs[slot] for slot in which]
                shape = (len(which), 1, width // 2, part)
                spots = [
                    pl.BlockSpec(shape, lambda g, f, s=s, r=r: (s, r * size + g, 0, 0))
                    for _, s, r in came
                ]
                came = [c for c, _, _ in came]
                return run(
                    f"{self.name}{which[0]}{'own' if own else 'away'}",
                    static(last_grad_kernel, seq_len, images, begin, which),
                    (normed1, grad_attn, *mats, *rights, *came),
                    [pl.BlockSpec((tokens, width // 2), lambda g, f: (0, half(f)))] * 2
                    + [whole((tokens, part)) for _ in mats]
                    + [
                        pl.BlockSpec(
                            (1, tokens, part), lambda g, f: (jnp.maximum(begin + g - 1, 0), 0, 0)
                        )
                        for _ in rights
                    ]
                    + spots,
                    pl.BlockSpec(shape, lambda g, f: (0, g, 0, 0)),
                    like((len(which), size, width // 2, part), bf16),
                    grid=(size,),
                )

        class Reduce:
            def __init__(self, source):
                self.source = source

            def k_away(self):
                self.made = self.source.make([*slots], False, ())

            def t_core(self):
                self.came = start(core_swap, self.made)

            def k_own(self):
                make, came = self.source.make, self.came
                self.first = [make([slot], True, [(came, slot, 0)], 0, 2) for slot in others]
                self.second = make([*slots], True, [(came, 0, 1)], 1, 2)

            def t_one(self):
                self.sent = [start(peer, value, slot) for value, slot in zip(self.first, others)]
                total = self.second.value
                total = total.reshape(tensor, -1, total.shape[-1])
                sent, self.held_b = halves(total, low, 1)
                self.moving_b = start(chip_swap, sent, 1)

            def k_mid(self):
                self.total = self.source.make([0], True, [(self.came, 0, 0)], 0, 2)

            def t_two(self):
                total = self.total.value.astype(f32)
                for sent in self.sent:
                    total = total + sent.value.astype(f32)
                sent, self.held_a = halves(total.reshape(-1, total.shape[-1]), low, 0)
                self.moving_a = start(chip_swap, sent.astype(bf16), 1)
                total = self.held_b.astype(f32) + self.moving_b.value.astype(f32)
                self.held_b = total[0]
                self.moving_b = [start(peer, total[slot].astype(bf16), slot) for slot in others]

            def t_z(self):
                total_a = self.held_a.astype(f32) + self.moving_a.value.astype(f32)
                total_b = self.held_b
                for moving in self.moving_b:
                    total_b = total_b + moving.value.astype(f32)
                self.held = jnp.where(high == 0, total_a, total_b)
                sent = jnp.where(high == 0, total_b, total_a).astype(bf16)
                self.moving = start(chip_swap, sent, 2)

            def t_full(self):
                mask = 4
                while mask < chips:
                    self.held = (self.held.astype(f32) + self.moving.value.astype(f32)).astype(bf16)
                    self.moving = start(chip_swap, self.held, mask)
                    mask *= 2

            def t_up(self):
                self.held = (self.held.astype(f32) + self.moving.value.astype(f32)).astype(bf16)
                self.moving = start(chip_swap, self.held, 2)

            def t_out(self):
                self.held = ordered(high, self.held, self.moving.value)
                self.moving = start(chip_swap, self.held, 1)

            def t_share(self):
                pieces = [self.held, self.moving.value]
                self.pieces = pieces + [start(core_swap, p) for p in pieces]

            def joined(self):
                pieces = self.pieces
                rows, cols = pieces[0].shape
                rows //= 2

                def spot(n):
                    return lambda w, i, f: (jnp.where(w == n, i, jnp.where(w < n, 0, 1)), 0)

                def place(w, i, f):
                    half = f[1 + images] ^ (w // 2)
                    return (half * 4 + i * 2 + (f[2 + images] ^ (w % 2)), 0)

                return run(
                    f"{self.source.name}join",
                    static(place_kernel, 4),
                    pieces,
                    [pl.BlockSpec((rows, cols), spot(n)) for n in range(4)],
                    pl.BlockSpec((rows, cols), place),
                    like((8 * rows, cols), f32),
                    grid=(4, 2),
                )

        def halves(value, bit, axis):
            size = value.shape[axis] // 2
            return (
                lax.dynamic_slice_in_dim(value, (1 - bit) * size, size, axis=axis),
                lax.dynamic_slice_in_dim(value, bit * size, size, axis=axis),
            )

        class Apart(Reduce):
            def t_one(self):
                self.sent = [start(peer, value, slot) for value, slot in zip(self.first, others)]
                total = self.second.value
                total = total.reshape(tensor, -1, total.shape[-1])
                sent, self.held_b = halves(total, high, 1)
                self.moving_b = start(chip_swap, sent, 2)

            def t_three(self):
                total_a = self.held_a.astype(f32) + self.moving_a.value.astype(f32)
                sent_a, self.held_a = halves(total_a, high, 0)
                total_b = self.held_b
                for moving in self.moving_b:
                    total_b = total_b + moving.value.astype(f32)
                sent_b, self.held_b = halves(total_b, low, 0)
                self.moving_a = start(chip_swap, sent_a.astype(bf16), 2)
                self.moving_b = start(chip_swap, sent_b.astype(bf16), 1)

            def t_full(self):
                held = [
                    h.astype(f32) + m.value.astype(f32)
                    for h, m in ((self.held_a, self.moving_a), (self.held_b, self.moving_b))
                ]
                self.held = jnp.concatenate(held).astype(bf16)
                self.moving = start(chip_swap, self.held, 4)
                mask = 8
                while mask < chips:
                    self.held = (self.held.astype(f32) + self.moving.value.astype(f32)).astype(bf16)
                    self.moving = start(chip_swap, self.held, mask)
                    mask *= 2

            def t_up(self):
                held, moving = (v.reshape(2, -1, v.shape[-1]) for v in (self.held, self.moving.value))
                self.held_a = (held[0].astype(f32) + moving[0].astype(f32)).astype(bf16)
                self.held_b = (held[1].astype(f32) + moving[1].astype(f32)).astype(bf16)
                self.moving_a = start(chip_swap, self.held_a, 2)
                self.moving_b = start(chip_swap, self.held_b, 1)

            def t_out(self):
                self.held_a = ordered(high, self.held_a, self.moving_a.value)
                self.held_b = ordered(low, self.held_b, self.moving_b.value)
                self.moving_a = start(chip_swap, self.held_a, 1)
                self.moving_b = start(chip_swap, self.held_b, 2)

            def t_share(self):
                pieces = [self.held_a, self.moving_a.value, self.held_b, self.moving_b.value]
                self.pieces = pieces + [start(core_swap, p) for p in pieces]

            def joined(self):
                def matrix(n, f):
                    bit = jnp.where(n % 4 < 2, f[2 + images], f[3 + images])
                    return 2 * ((n % 4) // 2) + (bit ^ (n % 2))

                half = width // 2
                placed = ()
                for far in range(2):
                    placed = run(
                        f"qkvjoin{far}",
                        static(last_place_kernel, matrix),
                        (*self.pieces[4 * far : 4 * far + 4], *placed),
                        [whole((half, part))] * 4
                        + [pl.BlockSpec(memory_space=pl.ANY)] * len(placed),
                        [
                            pl.BlockSpec((part, half), lambda w, f: (0, f[1 + images] ^ far)),
                            pl.BlockSpec(
                                (1, half, part),
                                lambda w, f: (
                                    jnp.maximum(matrix(w, f) - 1, 0),
                                    f[1 + images] ^ far,
                                    0,
                                ),
                            ),
                        ],
                        [like((part, width), f32), like((3, width, part), f32)],
                        grid=(4,),
                        input_output_aliases={5: 0, 6: 1} if placed else {},
                    )
                return placed

        def ordered(bit, mine, other):
            return jnp.where(
                bit == 0, jnp.concatenate([mine, other]), jnp.concatenate([other, mine])
            )


        def attend(slot, w):
            qv = biases[slot].value[: 2 * part].reshape(2, 1, part)
            shift = jnp.stack([qv[0], jnp.zeros_like(qv[0]), qv[1]])
            return run(
                f"attend{slot}",
                static(attend_kernel, seq_len, images),
                (normed1, w, shift),
                [
                    whole(shape2),
                    pl.BlockSpec((3, width, lanes), lambda g, f: (0, 0, g)),
                    pl.BlockSpec((3, 1, lanes), lambda g, f: (0, 0, g)),
                ],
                [
                    pl.BlockSpec((3, tokens, lanes), lambda g, f: (0, 0, g)),
                    pl.BlockSpec((tokens, lanes), lambda g, f: (0, g)),
                ],
                [like((3, tokens, part), bf16), like((tokens, part), bf16)],
                grid=(part // lanes,),
            )

        def hide(slot):
            acts[slot], slopes[slot] = run(
                f"hidden{slot}",
                static(hidden_kernel, seq_len, images),
                (normed2, fc1[slot], row(biases[slot].value[2 * part :])),
                [
                    whole(shape2),
                    pl.BlockSpec((width, tile), lambda g, f: (0, g)),
                    pl.BlockSpec((1, tile), lambda g, f: (0, g)),
                ],
                [pl.BlockSpec((tokens, tile), lambda g, f: (0, g))] * 2,
                [like((tokens, hidden), bf16)] * 2,
                grid=(hidden // tile,),
            )

        def ffn():
            block = max(128, 2 * tile // tensor)
            steps = hidden // block

            def at(slot):
                return lambda g: jnp.clip(g - slot * steps, 0, steps - 1)

            across = [
                pl.BlockSpec((tokens, block), lambda g, f, at=at(slot): (0, at(g))) for slot in slots
            ]
            got = run(
                "ffn",
                static(ffn_kernel, seq_len, images, tensor),
                (*acts, *slopes, *fc2, *fc1, top, mid, row(fc2_bias), g2),
                [
                    *across,
                    *across,
                    *[
                        pl.BlockSpec((block, width), lambda g, f, at=at(slot): (at(g), 0))
                        for slot in slots
                    ],
                    *[
                        pl.BlockSpec((width, block), lambda g, f, at=at(slot): (0, at(g)))
                        for slot in slots
                    ],
                    whole(shape2),
                    whole(shape2),
                    whole((1, width)),
                    whole((1, width)),
                ],
                [
                    *across,
                    *[
                        pl.BlockSpec((1, block), lambda g, f, at=at(slot): (0, at(g)))
                        for slot in slots
                    ],
                    whole(shape2),
                    whole(shape2),
                    whole((3, width)),
                ],
                [
                    *[like((tokens, hidden), bf16)] * tensor,
                    *[like((1, hidden), f32)] * tensor,
                    like(shape2, bf16),
                    like(shape2, bf16),
                    like((3, width), f32),
                ],
                grid=(tensor * steps,),
                scratch=[pltpu.VMEM(shape2, f32)] * 2,
                vmem=40 << 20,
            )
            grad_pres[:], pre_sums[:] = got[:tensor], got[tensor : 2 * tensor]
            return got[2 * tensor :]

        def attend_back(slot):
            nonlocal grad_norm1
            first = grad_norm1 is None
            tiles = pl.BlockSpec((3, tokens, lanes), lambda g, f: (0, 0, g))
            grad_projs[slot], grad_norm1, proj_sums[slot] = run(
                f"aback{slot}",
                static(attend_back_kernel, seq_len, images, first),
                (grad_attn, out[slot], projs[slot], qkv[slot]) + (() if first else (grad_norm1,)),
                [
                    whole(shape2),
                    pl.BlockSpec((lanes, width), lambda g, f: (g, 0)),
                    tiles,
                    pl.BlockSpec((3, width, lanes), lambda g, f: (0, 0, g)),
                ]
                + ([] if first else [whole(shape2)]),
                [tiles, whole(shape2), pl.BlockSpec((2, lanes), lambda g, f: (0, g))],
                [like((3, tokens, part), bf16), like(shape2, f32), like((2, part), f32)],
                grid=(part // lanes,),
            )

        acts, slopes = [None] * tensor, [None] * tensor
        grad_pres, pre_sums = [None] * tensor, [None] * tensor
        grad_projs, proj_sums, grad_norm1 = [None] * tensor, [None] * tensor, None


        get_attn = Fetch([w_qkv.reshape(3 * width, part), w_out], False)
        small = jnp.concatenate([qv_bias.reshape(-1), fc1_bias])
        biases = [Box(small)] + [start(peer, small, slot) for slot in others]
        xc, normed1, top, top_sum = run(
            "prep",
            static(prep_kernel, seq_len, images),
            (inputs.reshape(shape2), cotangent.reshape(shape2), keep, g1, b1),
            [whole(shape2), whole(shape2), whole(keep.shape), whole(g1.shape), whole(b1.shape)],
            [whole(shape2), whole(shape2), whole(shape2), whole((1, width))],
            [like(shape2, bf16), like(shape2, bf16), like(shape2, bf16), like((1, width), f32)],
        )
        seen = [attend(0, w_qkv)]
        step()

        get_attn.second()
        get_fc1 = Fetch([w_fc1], True)
        step()

        get_attn.third()
        get_fc1.second()
        qkv, out = [w_qkv], [w_out]
        for w, w_2 in get_attn.full():
            qkv.append(w.value.reshape(3, width, part))
            out.append(w_2)
        for slot in others:
            seen.append(attend(slot, qkv[slot]))
        projs, mixes = [s[0] for s in seen], [s[1] for s in seen]
        mid, normed2 = run(
            "middle",
            static(middle_kernel, seq_len, images, tensor),
            (*mixes, *out, xc, row(out_bias), g2, b2),
            [whole((tokens, part))] * tensor
            + [whole((part, width))] * tensor
            + [whole(shape2), whole((1, width)), whole((1, width)), whole((1, width))],
            [whole(shape2), whole(shape2)],
            [like(shape2, f32), like(shape2, bf16)],
        )
        step()

        get_fc1.third()
        get_fc2 = Fetch([w_fc2], True)
        fc1 = [w_fc1] + [w for w, in get_fc1.full()]
        for slot in slots:
            hide(slot)
        w1 = Reduce(Plain("fc2", acts, [top], TILE))
        w1.k_away()
        step()

        w1.t_core()
        get_fc2.second()
        w1.k_own()
        step()


        w1.t_one()
        get_fc2.third()
        fc2 = [w_fc2] + [w for w, in get_fc2.full()]
        low_out, grad_attn, sums2 = ffn()
        w2 = Reduce(Plain("fc1", [normed2], grad_pres, 256))
        w2.k_away()
        w1.k_mid()
        step()

        w1.t_two()
        w2.t_core()
        w2.k_own()
        step()

        w1.t_z()
        attend_back(0)
        step()

        w2.t_one()
        w1.t_full()
        for slot in others:
            attend_back(slot)
        w3 = Apart(Packed())
        w3.k_away()
        w2.k_mid()
        step()

        w2.t_two()
        w3.t_core()
        w1.t_up()
        w3.k_own()
        step()

        w2.t_z()
        grad_input, sums1 = run(
            "last",
            static(last_kernel, seq_len, images),
            (grad_norm1, xc, grad_attn, g1, keep),
            [whole(shape2), whole(shape2), whole(shape2), whole((1, width)), whole(keep.shape)],
            [whole(shape2), whole((2, width))],
            [like(shape2, bf16), like((2, width), f32)],
        )
        layer_out = run(
            "spread",
            static(spread_kernel, seq_len, images),
            (low_out, keep),
            [whole(shape2), whole(keep.shape)],
            whole(shape2),
            like(shape2, bf16),
        )
        step()

        w3.t_one()
        w1.t_out()
        w3.k_mid()
        step()

        common = jnp.concatenate(
            [
                sums1.value.reshape(-1),
                sums2.value[2],
                sums2.value[0],
                sums2.value[1],
                top_sum.value[0],
            ]
        )
        owned = [
            jnp.concatenate(
                [proj_sums[slot].value.reshape(-1), pre_sums[slot].value.reshape(-1), common]
            )
            for slot in slots
        ]
        vector = owned[0]
        moving = []

        def add(move, *mask):
            nonlocal vector, moving
            for m in moving:
                vector = vector + m.value
            moving = [start(move, vector, *mask)] if move else []

        moving = [start(peer, owned[slot], slot) for slot in others]
        w3.t_two()
        w2.t_full()
        step()

        w3.t_three()
        w2.t_up()
        w1.t_share()
        add(core_swap)
        step()

        w3.t_full()
        w2.t_out()
        add(chip_swap, 1)
        grad_fc2 = w1.joined()
        step()

        w3.t_up()
        w2.t_share()
        add(chip_swap, 2)
        step()

        w3.t_out()
        mask = 4
        while mask < chips:
            add(chip_swap, mask)
            mask *= 2
        grad_fc1 = w2.joined()
        step()

        w3.t_share()
        add(None)
        grad_out, grad_qkv = (g.value for g in w3.joined())
        layer_out = layer_out.value.reshape(inputs.shape)
        grad_input = grad_input.value.reshape(inputs.shape)
        grad_qv_bias = vector[: 2 * part].reshape(2, part)
        grad_fc1_bias = vector[2 * part : 2 * part + hidden]
        rest = vector[2 * part + hidden :].reshape(6, width)
        return (
            layer_out,
            grad_input,
            rest[0],
            rest[1],
            grad_qkv,
            grad_qv_bias,
            grad_out,
            rest[2],
            rest[3],
            rest[4],
            grad_fc1.value,
            grad_fc1_bias,
            grad_fc2.value,
            rest[5],
        )

    return local


def solution(mesh):
    chips, tensor = mesh.shape["dp"] // CORES, mesh.shape["tensor"]
    finer = Mesh(mesh.devices.reshape(chips, CORES, tensor), ("chip", "core", "tensor"))
    rows = ("chip", "core", "tensor")
    return jax.shard_map(
        build(chips, tensor),
        mesh=finer,
        in_specs=(
            P(rows, None, None),
            P(rows, None),
            P(rows, None, None),
            P(),
            P(),
            P(None, None, "tensor"),
            P(None, "tensor"),
            P("tensor", None),
            P(),
            P(),
            P(),
            P(None, "tensor"),
            P("tensor"),
            P("tensor", None),
            P(),
        ),
        out_specs=(
            P(rows, None, None),
            P(rows, None, None),
            P(),
            P(),
            P(None, None, "tensor"),
            P(None, "tensor"),
            P("tensor", None),
            P(),
            P(),
            P(),
            P(None, "tensor"),
            P("tensor"),
            P("tensor", None),
            P(),
        ),
        check_vma=False,
    )
```

```python
import functools

import jax
import jax.numpy as jnp
from jax import lax
from jax.experimental import pallas as pl
from jax.experimental.pallas import tpu as pltpu
from jax.sharding import Mesh, PartitionSpec as P

HD = 64
BUF = 64
EPS = 1e-06
CORES = 2
FAST = 192
LANES = 256
TILE = 512

f32 = jnp.float32
bf16 = jnp.bfloat16
NT = ((1,), (1,))
TN = ((0,), (0,))


def dot(a, b, dims=((1,), (0,))):
    return lax.dot_general(a, b, (dims, ((), ())), preferred_element_type=f32)


def spans(flags, seq_len, body):
    if seq_len <= FAST:
        body(seq_len)
        return

    @pl.when(flags[0] == 1)
    def _():
        body(FAST)

    @pl.when(flags[0] == 0)
    def _():
        body(seq_len)


def whole(shape):
    return pl.BlockSpec(shape, lambda *_: (0,) * len(shape), pipeline_mode=pl.Buffered(1))


def kernel_call(name, body, flags, args, in_specs, out_specs, out_shape, grid=(1,), **kw):
    return pl.pallas_call(
        body,
        name=name,
        grid_spec=pltpu.PrefetchScalarGridSpec(
            num_scalar_prefetch=1,
            grid=grid,
            in_specs=in_specs,
            out_specs=out_specs,
            scratch_shapes=kw.pop("scratch", ()),
        ),
        out_shape=out_shape,
        compiler_params=pltpu.CompilerParams(vmem_limit_bytes=kw.pop("vmem", 28 << 20)),
        cost_estimate=pl.CostEstimate(flops=1000, bytes_accessed=1000, transcendentals=0),
        **kw,
    )(flags, *args)


def picks(keep_row, span):
    seq_len = keep_row.shape[1]
    upto = lax.broadcasted_iota(jnp.int32, (seq_len, seq_len), 0) <= lax.broadcasted_iota(
        jnp.int32, (seq_len, seq_len), 1
    )
    keep_rows = jnp.broadcast_to(keep_row, (16, seq_len))
    rank = dot(keep_rows.astype(bf16), upto.astype(f32).astype(bf16))[0:1]
    place = lax.broadcasted_iota(jnp.int32, (span, seq_len), 0).astype(f32) + 1.0
    hit = jnp.where(place == rank, keep_row, 0.0)
    return hit.astype(bf16)


def norm_parts(values):
    centred = values - jnp.mean(values, axis=-1, keepdims=True)
    inverse = lax.rsqrt(jnp.mean(centred * centred, axis=-1, keepdims=True) + EPS)
    return centred * inverse, inverse


def norm_grad(grad_rows, unit, inverse, gain):
    scaled = grad_rows * gain
    centred = (
        scaled
        - jnp.mean(scaled, axis=-1, keepdims=True)
        - unit * jnp.mean(scaled * unit, axis=-1, keepdims=True)
    )
    return centred * inverse


def col_sum(values):
    return jnp.sum(values, axis=0, keepdims=True)


def prep_kernel(seq_len, images, flags, x, cot, keep, gain, bias, xc, normed, top, top_sum):
    def body(span):
        total = jnp.zeros(top_sum.shape, f32)
        for i in range(images):
            pick = picks(keep[i : i + 1, :], span)
            rows = slice(i * span, (i + 1) * span)
            source = slice(i * seq_len, (i + 1) * seq_len)
            kept = dot(pick, x[source, :])
            xc[rows, :] = kept.astype(bf16)
            normed[rows, :] = (norm_parts(kept)[0] * gain[...] + bias[...]).astype(bf16)
            grad = dot(pick, cot[source, :])
            top[rows, :] = grad.astype(bf16)
            total = total + col_sum(grad)
        top_sum[...] = total

    spans(flags, seq_len, body)


def head_masks(heads):
    lane = lax.broadcasted_iota(jnp.int32, (1, heads * HD), 1)
    return [(lane >= h * HD) & (lane < (h + 1) * HD) for h in range(heads)]


def softmax_rows(q, k, count):
    raw = dot(q, k, NT)
    column = lax.broadcasted_iota(jnp.int32, raw.shape, 1)
    raw = jnp.where(column < count, raw, -1e30)
    raised = jnp.exp(raw - jnp.max(raw, axis=-1, keepdims=True))
    return raised / jnp.sum(raised, axis=-1, keepdims=True)


def attend_kernel(seq_len, images, flags, normed, w, shift, proj, mixed):
    heads = mixed.shape[1] // HD

    def body(span):
        masks = head_masks(heads)
        for c in range(3):
            value = dot(normed[: images * span, :], w[c]) + shift[c]
            proj[c, : images * span, :] = value.astype(bf16)
        for i in range(images):
            rows = slice(i * span, (i + 1) * span)
            count = flags[1 + i]
            q, k, v = proj[0, rows, :], proj[1, rows, :], proj[2, rows, :]
            q = (q.astype(f32) * HD ** (-0.5)).astype(bf16)
            joined = jnp.zeros(q.shape, f32)
            for h in range(heads):
                probs = softmax_rows(jnp.where(masks[h], q, 0), k, count)
                joined = jnp.where(masks[h], dot(probs.astype(bf16), v), joined)
            mixed[rows, :] = joined.astype(bf16)

    spans(flags, seq_len, body)


def middle_kernel(seq_len, images, slots, flags, *refs):
    mixed, w, (xc, out_bias, gain, bias, mid, normed) = (
        refs[:slots],
        refs[slots : 2 * slots],
        refs[2 * slots :],
    )

    def body(span):
        for i in range(images):
            rows = slice(i * span, (i + 1) * span)
            total = xc[rows, :].astype(f32) + out_bias[...]
            for slot in range(slots):
                total = total + dot(mixed[slot][rows, :], w[slot][...])
            mid[rows, :] = total
            normed[rows, :] = (norm_parts(total)[0] * gain[...] + bias[...]).astype(bf16)

    spans(flags, seq_len, body)


def hidden_kernel(seq_len, images, flags, normed, w, bias, act, slope):
    def body(span):
        rows = images * span
        step = rows // 2
        for part in range(2):
            at = slice(part * step, (part + 1) * step)
            pre = dot(normed[at, :], w[...]) + bias[...]
            cdf = 0.5 * (1.0 + lax.erf(pre * 0.7071067811865476))
            act[at, :] = (pre * cdf).astype(bf16)
            slope[at, :] = (cdf + pre * jnp.exp(-0.5 * pre * pre) * 0.3989422804014327).astype(bf16)

    spans(flags, seq_len, body)


def ffn_kernel(seq_len, images, slots, flags, *refs):
    act, slope, w2, w1 = (refs[n * slots : (n + 1) * slots] for n in range(4))
    top, mid, bias, gain = refs[4 * slots : 4 * slots + 4]
    refs = refs[4 * slots + 4 :]
    grad_pre, pre_sums = refs[:slots], refs[slots : 2 * slots]
    low, grad_attn, sums, total, grad_norm = refs[2 * slots :]
    step, steps = pl.program_id(0), pl.num_programs(0)

    def body(span):
        rows = images * span

        @pl.when(step == 0)
        def _():
            total[:rows, :] = mid[:rows, :]
            grad_norm[:rows, :] = jnp.zeros((rows, grad_norm.shape[1]), f32)

        for slot in range(slots):

            @pl.when(step // (steps // slots) == slot)
            def _():
                total[:rows, :] += dot(act[slot][:rows, :], w2[slot][...])
                grad = dot(top[:rows, :], w2[slot][...], NT) * slope[slot][:rows, :].astype(f32)
                grad_pre[slot][:rows, :] = grad.astype(bf16)
                pre_sums[slot][...] = col_sum(grad_pre[slot][:rows, :].astype(f32))
                grad_norm[:rows, :] += dot(grad_pre[slot][:rows, :], w1[slot][...], NT)

        @pl.when(step == steps - 1)
        def _():
            for i in range(images):
                at = slice(i * span, (i + 1) * span)
                low[at, :] = (total[at, :] + bias[...]).astype(bf16)
                unit, inverse = norm_parts(mid[at, :])
                grad = grad_norm[at, :]
                full = top[at, :].astype(f32) + norm_grad(grad, unit, inverse, gain[...])
                grad_attn[at, :] = full.astype(bf16)
                part = [
                    col_sum(grad * unit),
                    col_sum(grad),
                    col_sum(grad_attn[at, :].astype(f32)),
                ]
                for n, row in enumerate(part):
                    sums[n : n + 1, :] = row if i == 0 else sums[n : n + 1, :] + row

    spans(flags, seq_len, body)


def attend_back_kernel(seq_len, images, first, flags, grad_attn, w_out, proj, w, *refs):
    if first:
        grad_proj, grad_norm, sums = refs
        base = None
    else:
        base, grad_proj, grad_norm, sums = refs
    heads = proj.shape[2] // HD
    start = pl.program_id(0) == 0

    def body(span):
        rows_all = images * span
        masks = head_masks(heads)

        @pl.when(start)
        def _():
            if first:
                grad_norm[:rows_all, :] = jnp.zeros((rows_all, grad_norm.shape[1]), f32)
            else:
                grad_norm[:rows_all, :] = base[:rows_all, :]

        for i in range(images):
            rows = slice(i * span, (i + 1) * span)
            count = flags[1 + i]
            grad_mixed = dot(grad_attn[rows, :], w_out[...], NT).astype(bf16)
            q, k, v = proj[0, rows, :], proj[1, rows, :], proj[2, rows, :]
            q_low = (q.astype(f32) * HD ** (-0.5)).astype(bf16)
            dq = jnp.zeros(q.shape, f32)
            dk, dv = dq, dq
            for h in range(heads):
                probs = softmax_rows(jnp.where(masks[h], q_low, 0), k, count)
                grad_prob = dot(jnp.where(masks[h], grad_mixed, 0), v, NT)
                delta = jnp.sum(probs * grad_prob, axis=-1, keepdims=True)
                grad_score = (probs * (grad_prob - delta)).astype(bf16)
                dv = jnp.where(masks[h], dot(probs.astype(bf16), grad_mixed, TN), dv)
                dq = jnp.where(masks[h], dot(grad_score, k), dq)
                dk = jnp.where(masks[h], dot(grad_score, q_low, TN), dk)
            grad_proj[0, rows, :] = (dq * HD ** (-0.5)).astype(bf16)
            grad_proj[1, rows, :] = dk.astype(bf16)
            grad_proj[2, rows, :] = dv.astype(bf16)
        for c in range(3):
            grad_norm[:rows_all, :] += dot(grad_proj[c, :rows_all, :], w[c], NT)
        sums[0:1, :] = col_sum(grad_proj[0, :rows_all, :].astype(f32))
        sums[1:2, :] = col_sum(grad_proj[2, :rows_all, :].astype(f32))

    spans(flags, seq_len, body)


def spread_kernel(seq_len, images, flags, value, keep, out):
    def body(span):
        for i in range(images):
            rows = slice(i * span, (i + 1) * span)
            pick = picks(keep[i : i + 1, :], span)
            out[i * seq_len : (i + 1) * seq_len, :] = dot(pick, value[rows, :], TN).astype(bf16)

    spans(flags, seq_len, body)


def last_kernel(seq_len, images, flags, grad_norm, xc, grad_attn, gain, keep, out, sums):
    def body(span):
        for i in range(images):
            rows = slice(i * span, (i + 1) * span)
            unit, inverse = norm_parts(xc[rows, :].astype(f32))
            grad = grad_norm[rows, :]
            low = grad_attn[rows, :].astype(f32) + norm_grad(grad, unit, inverse, gain[...])
            low = low.astype(bf16)
            pick = picks(keep[i : i + 1, :], span)
            out[i * seq_len : (i + 1) * seq_len, :] = dot(pick, low, TN).astype(bf16)
            part = [col_sum(grad * unit), col_sum(grad)]
            for n, row in enumerate(part):
                sums[n : n + 1, :] = row if i == 0 else sums[n : n + 1, :] + row

    spans(flags, seq_len, body)


def grad_kernel(seq_len, images, slots, flags, *refs):
    left, right, rest = refs[: len(slots)], refs[len(slots) : 2 * len(slots)], refs[2 * len(slots) :]
    out = rest[-1]

    def body(span):
        rows = images * span
        for n in range(len(slots)):
            value = dot(left[n][:rows, :], right[n][:rows, :], TN)
            for came in rest[:-1]:
                value = value + came[n].astype(f32)
            out[n] = value.astype(bf16)

    spans(flags, seq_len, body)


def last_grad_kernel(seq_len, images, first, slots, flags, normed, top, *refs):
    mixed, right, rest = (
        refs[: len(slots)],
        refs[len(slots) : 2 * len(slots)],
        refs[2 * len(slots) :],
    )
    out = rest[-1]

    def finish(n, value):
        for came in rest[:-1]:
            value = value + came[n, 0].astype(f32)
        out[n, 0] = value.astype(bf16)

    def body(span):
        rows = images * span
        which = first + pl.program_id(0)

        @pl.when(which == 0)
        def _():
            for n in range(len(slots)):
                finish(n, dot(top[:rows, :], mixed[n][:rows, :], TN))

        @pl.when(which > 0)
        def _():
            for n in range(len(slots)):
                finish(n, dot(normed[:rows, :], right[n][0, :rows, :], TN))

    spans(flags, seq_len, body)


def assemble_kernel(spots, units, count, flags, *refs):
    pieces, outs, sems = refs[:count], refs[count:-1], refs[-1]
    copies = []
    for piece, places in zip(pieces, spots(flags)):
        begin = 0
        for out in outs:
            rows = out.shape[0] // units
            for c in range(0, out.shape[1], piece.shape[1]):
                for place in places:
                    copy = pltpu.make_async_copy(
                        piece.at[pl.ds(begin, rows), :],
                        out.at[
                            pl.ds(pl.multiple_of(place * rows, 16), rows), pl.ds(c, piece.shape[1])
                        ],
                        sems.at[len(copies)],
                    )
                    copy.start()
                    copies.append(copy)
                    begin += rows
    for copy in copies:
        copy.wait()


def fold_kernel(plan, flags, *refs):
    count = sum(sum(counts) for _, counts, _ in plan)
    ins, outs = list(refs[:count]), list(refs[count:])

    def take(n):
        got = ins[:n]
        del ins[:n]
        return got

    def put(group, at=...):
        total = group[0][at].astype(f32)
        for ref in group[1:]:
            total = total + ref[at].astype(f32)
        return total.astype(bf16)

    for kind, counts, where in plan:
        groups = [take(n) for n in counts]
        shape = groups[0][0].shape
        if kind == "rows":
            size = shape[-2] // 2
            for half in (1 - flags[where], flags[where]):
                at = (pl.ds(pl.multiple_of(half * size, 16), size), slice(None))
                at = (slice(None),) * (len(shape) - 2) + at
                outs.pop(0)[...] = put(groups[0], at)
        elif kind == "slots":
            for slot in range(shape[0]):
                outs.pop(0)[...] = put(groups[0], slot)
        elif kind == "pick":
            sent, held = outs.pop(0), outs.pop(0)
            for bit in range(2):

                @pl.when(flags[where] == bit)
                def _():
                    held[...] = put(groups[bit])
                    sent[...] = put(groups[1 - bit])

        elif kind == "sum":
            outs.pop(0)[...] = put(groups[0])
        elif kind == "order":
            out = outs.pop(0)
            for half, group in zip((flags[where], 1 - flags[where]), groups):
                begin = pl.multiple_of(half * shape[0], 16)
                out[pl.ds(begin, shape[0]), :] = put(group)
        elif kind == "join":
            out = outs.pop(0)
            for n, group in enumerate(groups):
                out[n * shape[0] : (n + 1) * shape[0], :] = put(group)
        else:
            size = shape[0] // 2
            for n in range(2):
                outs.pop(0)[...] = put(groups[0], slice(n * size, (n + 1) * size))


def place_kernel(count, flags, *refs):
    out = refs[count]
    for n in range(count):

        @pl.when(pl.program_id(0) == n)
        def _():
            out[...] = refs[n][...].astype(out.dtype)


def last_place_kernel(matrix, flags, *refs):
    pieces, (out, qkv) = refs[:4], refs[-2:]
    for n in range(4):
        which = matrix(n, flags)

        @pl.when((pl.program_id(0) == n) & (which == 0))
        def _():
            out[...] = pieces[n][...].astype(f32).T

        @pl.when((pl.program_id(0) == n) & (which > 0))
        def _():
            qkv[0] = pieces[n][...].astype(f32)


def swap(value, axis, size, mask):
    return lax.ppermute(value, axis, [(i, i ^ mask) for i in range(size)])


def after(values, *waits):
    return lax.optimization_barrier((values, waits))[0]


def build(chips, tensor):
    def core_swap(value):
        return swap(value, "core", CORES, 1)

    def chip_swap(value, mask):
        return swap(value, "chip", chips, mask)

    def peer(value, slot):
        return swap(value, "tensor", tensor, slot)

    def local(
        inputs,
        keep_mask,
        cotangent,
        ln1_gain,
        ln1_bias,
        w_qkv,
        qv_bias,
        w_out,
        out_bias,
        ln2_gain,
        ln2_bias,
        w_fc1,
        fc1_bias,
        w_fc2,
        fc2_bias,
    ):
        images, seq_len, width = inputs.shape
        tokens = images * seq_len
        part = w_qkv.shape[2]
        hidden = w_fc1.shape[1]
        slots = range(tensor)
        others = range(1, tensor)
        lanes = min(LANES, part)
        tile = min(TILE, hidden)
        core, chip = lax.axis_index("core"), lax.axis_index("chip")
        low, high = chip & 1, (chip >> 1) & 1
        like = jax.ShapeDtypeStruct
        static = functools.partial
        row = lambda v: v.reshape(1, -1)

        keep = jnp.concatenate([jnp.ones((images, BUF), f32), keep_mask.astype(f32)], axis=1)
        counts = BUF + jnp.sum(keep_mask, axis=1)
        place = jnp.stack([core, low, high]).astype(jnp.int32)
        flags = jnp.concatenate([jnp.all(counts <= FAST).astype(jnp.int32)[None], counts, place])
        shape2 = (tokens, width)
        g1, b1, g2, b2 = row(ln1_gain), row(ln1_bias), row(ln2_gain), row(ln2_bias)


        class Box:
            def __init__(self, value):
                self.value = value
                opened.append(self)

        opened = []
        begun = []
        gate = Box(flags)

        def step():
            values = lax.optimization_barrier([box.value for box in opened])
            for box, value in zip(opened, values):
                box.value = value
            opened[:] = [gate]
            begun[:] = [True]

        def run(name, body, args, in_specs, out_specs, out_shape, grid=(1,), **kw):
            args = [a.value if isinstance(a, Box) else a for a in args]
            got = kernel_call(
                name, body, gate.value, args, in_specs, out_specs, out_shape, grid, **kw
            )
            return [Box(g) for g in got] if isinstance(got, (list, tuple)) else Box(got)

        def start(move, value, *mask):
            value = value.value if isinstance(value, Box) else value
            return Box(move(after(value, gate.value) if begun else value, *mask))

        LOW, HIGH = 2 + images, 3 + images

        def fold(*plan):
            ins, outs, steps = [], [], []
            for kind, where, *groups in plan:
                groups = [[g.value if isinstance(g, Box) else g for g in group] for group in groups]
                for group in groups:
                    ins += group
                shape = groups[0][0].shape
                half = (*shape[:-2], shape[-2] // 2, shape[-1])
                outs += {
                    "rows": [half, half],
                    "slots": [shape[1:]] * shape[0],
                    "pick": [shape, shape],
                    "sum": [shape],
                    "order": [(2 * shape[0], *shape[1:])],
                    "join": [(len(groups) * shape[0], *shape[1:])],
                    "cut": [half, half],
                }[kind]
                steps.append((kind, [len(g) for g in groups], where))
            got = run(
                "fold",
                static(fold_kernel, steps),
                ins,
                [whole(v.shape) for v in ins],
                [whole(shape) for shape in outs],
                [like(shape, bf16) for shape in outs],
            )
            return [g.value for g in got]


        class Fetch:
            def __init__(self, shards, split):
                self.split, self.shards = split, shards
                units = self.units = 8 if split else 4
                own = self.places(core, low, high)[0]
                cols = min(w.shape[1] for w in shards)
                parts = []
                for w in shards:
                    rows = w.shape[0] // units
                    for c in range(0, w.shape[1], cols):
                        for place in own:
                            parts.append(
                                lax.dynamic_slice(w, (place * rows, c), (rows, min(cols, w.shape[1])))
                            )
                piece = jnp.concatenate(parts) if len(parts) > 1 else parts[0]
                self.mine = [start(peer, piece, slot) for slot in others]

            def places(self, co, lo, hi):
                if self.split:
                    return [(4 * co + lo, 4 * co + 2 + hi), (4 * co + 1 - lo,), (4 * co + 3 - hi,)]
                return [(2 * co + lo,), (2 * co + 1 - lo,)]

            def second(self):
                self.got = []
                for m in self.mine:
                    if self.split:
                        upper, lower = fold(("cut", 0, [m]))
                        beside = [start(chip_swap, upper, 1), start(chip_swap, lower, 2)]
                    else:
                        beside = [start(chip_swap, m, 1)]
                    self.got.append([m, *beside, start(core_swap, m)])

            def third(self):
                for got in self.got:
                    got += [start(core_swap, g) for g in got[1:-1]]

            def full(self):
                shapes = [w.shape for w in self.shards]

                def spots(f):
                    co, lo, hi = f[1 + images], f[2 + images], f[3 + images]
                    return self.places(co, lo, hi) + self.places(1 - co, lo, hi)

                return [
                    run(
                        "assemble",
                        static(assemble_kernel, spots, self.units, len(got)),
                        got,
                        [pl.BlockSpec(memory_space=pl.ANY)] * len(got),
                        [whole(shape) for shape in shapes],
                        [like(shape, bf16) for shape in shapes],
                        scratch=[pltpu.SemaphoreType.DMA((16,))],
                    )
                    for got in self.got
                ]


        half_of = lambda own: (lambda f: f[1 + images]) if own else (lambda f: 1 - f[1 + images])

        class Plain:
            def __init__(self, name, left, right, block):
                self.name, self.left, self.right, self.block = name, left, right, block

            def make(self, which, own, came, begin=0, share=1):
                pick = lambda v: [v[slot] if len(v) > 1 else v[0] for slot in which]
                left, right = pick(self.left), pick(self.right)
                half_rows = left[0].value.shape[1] // 2
                size = half_rows // share
                block = min(self.block, size)
                first, per_half = begin * size // block, half_rows // block
                cols = right[0].value.shape[1]
                half = half_of(own)
                shape = (len(which), block, cols)
                spots = [
                    pl.BlockSpec(shape, lambda g, f, s=s, r=r: (s, r * (size // block) + g, 0))
                    for _, s, r in came
                ]
                return run(
                    f"{self.name}{which[0]}{'own' if own else 'away'}",
                    static(grad_kernel, seq_len, images, which),
                    (*left, *right, *[c for c, _, _ in came]),
                    [
                        pl.BlockSpec((tokens, block), lambda g, f: (0, half(f) * per_half + first + g))
                        for _ in left
                    ]
                    + [whole((tokens, cols)) for _ in right]
                    + spots,
                    pl.BlockSpec(shape, lambda g, f: (0, g, 0)),
                    like((len(which), size, cols), bf16),
                    grid=(size // block,),
                )

        class Packed:
            name = "qkv"

            def make(self, which, own, came, begin=0, share=1):
                size = 4 // share
                begin, half = begin * size, half_of(own)
                mats = [mixes[slot] for slot in which]
                rights = [grad_projs[slot] for slot in which]
                shape = (len(which), 1, width // 2, part)
                spots = [
                    pl.BlockSpec(shape, lambda g, f, s=s, r=r: (s, r * size + g, 0, 0))
                    for _, s, r in came
                ]
                came = [c for c, _, _ in came]
                return run(
                    f"{self.name}{which[0]}{'own' if own else 'away'}",
                    static(last_grad_kernel, seq_len, images, begin, which),
                    (normed1, grad_attn, *mats, *rights, *came),
                    [pl.BlockSpec((tokens, width // 2), lambda g, f: (0, half(f)))] * 2
                    + [whole((tokens, part)) for _ in mats]
                    + [
                        pl.BlockSpec(
                            (1, tokens, part), lambda g, f: (jnp.maximum(begin + g - 1, 0), 0, 0)
                        )
                        for _ in rights
                    ]
                    + spots,
                    pl.BlockSpec(shape, lambda g, f: (0, g, 0, 0)),
                    like((len(which), size, width // 2, part), bf16),
                    grid=(size,),
                )

        class Reduce:
            def __init__(self, source):
                self.source = source

            def k_away(self):
                self.made = self.source.make([*slots], False, ())

            def t_core(self):
                self.came = start(core_swap, self.made)

            def k_own(self):
                make, came = self.source.make, self.came
                self.first = [make([slot], True, [(came, slot, 0)], 0, 2) for slot in others]
                self.second = make([*slots], True, [(came, 0, 1)], 1, 2)

            def t_one(self):
                self.sent = [start(peer, value, slot) for value, slot in zip(self.first, others)]
                total = self.second.value
                total = total.reshape(tensor, -1, total.shape[-1])
                sent, self.held_b = fold(("rows", LOW, [total]))
                self.moving_b = start(chip_swap, sent, 1)

            def k_mid(self):
                self.total = self.source.make([0], True, [(self.came, 0, 0)], 0, 2)

            def t_two(self):
                cols = self.total.value.shape[-1]
                parts = [v.value.reshape(-1, cols) for v in (self.total, *self.sent)]
                sent, self.held_a, self.held_b, *others_b = fold(
                    ("rows", LOW, parts), ("slots", 0, [self.held_b, self.moving_b])
                )
                self.moving_a = start(chip_swap, sent, 1)
                self.moving_b = [start(peer, v, slot) for v, slot in zip(others_b, others)]

            def t_z(self):
                sent, self.held = fold(
                    ("pick", HIGH, [self.held_a, self.moving_a], [self.held_b, *self.moving_b])
                )
                self.moving = start(chip_swap, sent, 2)

            def t_full(self):
                mask = 4
                while mask < chips:
                    (self.held,) = fold(("sum", 0, [self.held, self.moving]))
                    self.moving = start(chip_swap, self.held, mask)
                    mask *= 2

            def t_up(self):
                (self.held,) = fold(("sum", 0, [self.held, self.moving]))
                self.moving = start(chip_swap, self.held, 2)

            def t_out(self):
                (self.held,) = fold(("order", HIGH, [self.held], [self.moving]))
                self.moving = start(chip_swap, self.held, 1)

            def t_share(self):
                pieces = [self.held, self.moving.value]
                self.pieces = pieces + [start(core_swap, p) for p in pieces]

            def joined(self):
                pieces = self.pieces
                rows, cols = pieces[0].shape
                rows //= 2

                def spot(n):
                    return lambda w, i, f: (jnp.where(w == n, i, jnp.where(w < n, 0, 1)), 0)

                def place(w, i, f):
                    half = f[1 + images] ^ (w // 2)
                    return (half * 4 + i * 2 + (f[2 + images] ^ (w % 2)), 0)

                return run(
                    f"{self.source.name}join",
                    static(place_kernel, 4),
                    pieces,
                    [pl.BlockSpec((rows, cols), spot(n)) for n in range(4)],
                    pl.BlockSpec((rows, cols), place),
                    like((8 * rows, cols), f32),
                    grid=(4, 2),
                )

        class Apart(Reduce):
            def t_one(self):
                self.sent = [start(peer, value, slot) for value, slot in zip(self.first, others)]
                total = self.second.value
                total = total.reshape(tensor, -1, total.shape[-1])
                sent, self.held_b = fold(("rows", HIGH, [total]))
                self.moving_b = start(chip_swap, sent, 2)

            def t_three(self):
                sent_a, self.held_a, sent_b, self.held_b = fold(
                    ("rows", HIGH, [self.held_a, self.moving_a]),
                    ("rows", LOW, [self.held_b, *self.moving_b]),
                )
                self.moving_a = start(chip_swap, sent_a, 2)
                self.moving_b = start(chip_swap, sent_b, 1)

            def t_full(self):
                (self.held,) = fold(
                    ("join", 0, [self.held_a, self.moving_a], [self.held_b, self.moving_b])
                )
                self.moving = start(chip_swap, self.held, 4)
                mask = 8
                while mask < chips:
                    (self.held,) = fold(("sum", 0, [self.held, self.moving]))
                    self.moving = start(chip_swap, self.held, mask)
                    mask *= 2

            def t_up(self):
                self.held_a, self.held_b = fold(("cut", 0, [self.held, self.moving]))
                self.moving_a = start(chip_swap, self.held_a, 2)
                self.moving_b = start(chip_swap, self.held_b, 1)

            def t_out(self):
                self.held_a, self.held_b = fold(
                    ("order", HIGH, [self.held_a], [self.moving_a]),
                    ("order", LOW, [self.held_b], [self.moving_b]),
                )
                self.moving_a = start(chip_swap, self.held_a, 1)
                self.moving_b = start(chip_swap, self.held_b, 2)

            def t_share(self):
                pieces = [self.held_a, self.moving_a.value, self.held_b, self.moving_b.value]
                self.pieces = pieces + [start(core_swap, p) for p in pieces]

            def joined(self):
                def matrix(n, f):
                    bit = jnp.where(n % 4 < 2, f[2 + images], f[3 + images])
                    return 2 * ((n % 4) // 2) + (bit ^ (n % 2))

                half = width // 2
                placed = ()
                for far in range(2):
                    placed = run(
                        f"qkvjoin{far}",
                        static(last_place_kernel, matrix),
                        (*self.pieces[4 * far : 4 * far + 4], *placed),
                        [whole((half, part))] * 4
                        + [pl.BlockSpec(memory_space=pl.ANY)] * len(placed),
                        [
                            pl.BlockSpec((part, half), lambda w, f: (0, f[1 + images] ^ far)),
                            pl.BlockSpec(
                                (1, half, part),
                                lambda w, f: (
                                    jnp.maximum(matrix(w, f) - 1, 0),
                                    f[1 + images] ^ far,
                                    0,
                                ),
                            ),
                        ],
                        [like((part, width), f32), like((3, width, part), f32)],
                        grid=(4,),
                        input_output_aliases={5: 0, 6: 1} if placed else {},
                    )
                return placed


        def attend(slot, w):
            qv = biases[slot].value[: 2 * part].reshape(2, 1, part)
            shift = jnp.stack([qv[0], jnp.zeros_like(qv[0]), qv[1]])
            return run(
                f"attend{slot}",
                static(attend_kernel, seq_len, images),
                (normed1, w, shift),
                [
                    whole(shape2),
                    pl.BlockSpec((3, width, lanes), lambda g, f: (0, 0, g)),
                    pl.BlockSpec((3, 1, lanes), lambda g, f: (0, 0, g)),
                ],
                [
                    pl.BlockSpec((3, tokens, lanes), lambda g, f: (0, 0, g)),
                    pl.BlockSpec((tokens, lanes), lambda g, f: (0, g)),
                ],
                [like((3, tokens, part), bf16), like((tokens, part), bf16)],
                grid=(part // lanes,),
            )

        def hide(slot):
            acts[slot], slopes[slot] = run(
                f"hidden{slot}",
                static(hidden_kernel, seq_len, images),
                (normed2, fc1[slot], row(biases[slot].value[2 * part :])),
                [
                    whole(shape2),
                    pl.BlockSpec((width, tile), lambda g, f: (0, g)),
                    pl.BlockSpec((1, tile), lambda g, f: (0, g)),
                ],
                [pl.BlockSpec((tokens, tile), lambda g, f: (0, g))] * 2,
                [like((tokens, hidden), bf16)] * 2,
                grid=(hidden // tile,),
            )

        def ffn():
            block = max(128, 2 * tile // tensor)
            steps = hidden // block

            def at(slot):
                return lambda g: jnp.clip(g - slot * steps, 0, steps - 1)

            across = [
                pl.BlockSpec((tokens, block), lambda g, f, at=at(slot): (0, at(g))) for slot in slots
            ]
            got = run(
                "ffn",
                static(ffn_kernel, seq_len, images, tensor),
                (*acts, *slopes, *fc2, *fc1, top, mid, row(fc2_bias), g2),
                [
                    *across,
                    *across,
                    *[
                        pl.BlockSpec((block, width), lambda g, f, at=at(slot): (at(g), 0))
                        for slot in slots
                    ],
                    *[
                        pl.BlockSpec((width, block), lambda g, f, at=at(slot): (0, at(g)))
                        for slot in slots
                    ],
                    whole(shape2),
                    whole(shape2),
                    whole((1, width)),
                    whole((1, width)),
                ],
                [
                    *across,
                    *[
                        pl.BlockSpec((1, block), lambda g, f, at=at(slot): (0, at(g)))
                        for slot in slots
                    ],
                    whole(shape2),
                    whole(shape2),
                    whole((3, width)),
                ],
                [
                    *[like((tokens, hidden), bf16)] * tensor,
                    *[like((1, hidden), f32)] * tensor,
                    like(shape2, bf16),
                    like(shape2, bf16),
                    like((3, width), f32),
                ],
                grid=(tensor * steps,),
                scratch=[pltpu.VMEM(shape2, f32)] * 2,
                vmem=40 << 20,
            )
            grad_pres[:], pre_sums[:] = got[:tensor], got[tensor : 2 * tensor]
            return got[2 * tensor :]

        def attend_back(slot):
            nonlocal grad_norm1
            first = grad_norm1 is None
            tiles = pl.BlockSpec((3, tokens, lanes), lambda g, f: (0, 0, g))
            grad_projs[slot], grad_norm1, proj_sums[slot] = run(
                f"aback{slot}",
                static(attend_back_kernel, seq_len, images, first),
                (grad_attn, out[slot], projs[slot], qkv[slot]) + (() if first else (grad_norm1,)),
                [
                    whole(shape2),
                    pl.BlockSpec((lanes, width), lambda g, f: (g, 0)),
                    tiles,
                    pl.BlockSpec((3, width, lanes), lambda g, f: (0, 0, g)),
                ]
                + ([] if first else [whole(shape2)]),
                [tiles, whole(shape2), pl.BlockSpec((2, lanes), lambda g, f: (0, g))],
                [like((3, tokens, part), bf16), like(shape2, f32), like((2, part), f32)],
                grid=(part // lanes,),
            )

        acts, slopes = [None] * tensor, [None] * tensor
        grad_pres, pre_sums = [None] * tensor, [None] * tensor
        grad_projs, proj_sums, grad_norm1 = [None] * tensor, [None] * tensor, None


        get_attn = Fetch([w_qkv.reshape(3 * width, part), w_out], False)
        small = jnp.concatenate([qv_bias.reshape(-1), fc1_bias])
        biases = [Box(small)] + [start(peer, small, slot) for slot in others]
        xc, normed1, top, top_sum = run(
            "prep",
            static(prep_kernel, seq_len, images),
            (inputs.reshape(shape2), cotangent.reshape(shape2), keep, g1, b1),
            [whole(shape2), whole(shape2), whole(keep.shape), whole(g1.shape), whole(b1.shape)],
            [whole(shape2), whole(shape2), whole(shape2), whole((1, width))],
            [like(shape2, bf16), like(shape2, bf16), like(shape2, bf16), like((1, width), f32)],
        )
        seen = [attend(0, w_qkv)]
        step()

        get_attn.second()
        get_fc1 = Fetch([w_fc1], True)
        step()

        get_attn.third()
        get_fc1.second()
        qkv, out = [w_qkv], [w_out]
        for w, w_2 in get_attn.full():
            qkv.append(w.value.reshape(3, width, part))
            out.append(w_2)
        for slot in others:
            seen.append(attend(slot, qkv[slot]))
        projs, mixes = [s[0] for s in seen], [s[1] for s in seen]
        mid, normed2 = run(
            "middle",
            static(middle_kernel, seq_len, images, tensor),
            (*mixes, *out, xc, row(out_bias), g2, b2),
            [whole((tokens, part))] * tensor
            + [whole((part, width))] * tensor
            + [whole(shape2), whole((1, width)), whole((1, width)), whole((1, width))],
            [whole(shape2), whole(shape2)],
            [like(shape2, f32), like(shape2, bf16)],
        )
        step()

        get_fc1.third()
        get_fc2 = Fetch([w_fc2], True)
        fc1 = [w_fc1] + [w for w, in get_fc1.full()]
        for slot in slots:
            hide(slot)
        w1 = Reduce(Plain("fc2", acts, [top], TILE))
        w1.k_away()
        step()

        w1.t_core()
        get_fc2.second()
        w1.k_own()
        step()


        w1.t_one()
        get_fc2.third()
        fc2 = [w_fc2] + [w for w, in get_fc2.full()]
        low_out, grad_attn, sums2 = ffn()
        w2 = Reduce(Plain("fc1", [normed2], grad_pres, 256))
        w2.k_away()
        w1.k_mid()
        step()

        w1.t_two()
        w2.t_core()
        w2.k_own()
        step()

        w1.t_z()
        attend_back(0)
        step()

        w2.t_one()
        w1.t_full()
        for slot in others:
            attend_back(slot)
        w3 = Apart(Packed())
        w3.k_away()
        w2.k_mid()
        step()

        w2.t_two()
        w3.t_core()
        w1.t_up()
        w3.k_own()
        step()

        w2.t_z()
        grad_input, sums1 = run(
            "last",
            static(last_kernel, seq_len, images),
            (grad_norm1, xc, grad_attn, g1, keep),
            [whole(shape2), whole(shape2), whole(shape2), whole((1, width)), whole(keep.shape)],
            [whole(shape2), whole((2, width))],
            [like(shape2, bf16), like((2, width), f32)],
        )
        layer_out = run(
            "spread",
            static(spread_kernel, seq_len, images),
            (low_out, keep),
            [whole(shape2), whole(keep.shape)],
            whole(shape2),
            like(shape2, bf16),
        )
        step()

        w3.t_one()
        w1.t_out()
        w3.k_mid()
        step()

        common = jnp.concatenate(
            [
                sums1.value.reshape(-1),
                sums2.value[2],
                sums2.value[0],
                sums2.value[1],
                top_sum.value[0],
            ]
        )
        owned = [
            jnp.concatenate(
                [proj_sums[slot].value.reshape(-1), pre_sums[slot].value.reshape(-1), common]
            )
            for slot in slots
        ]
        vector = owned[0]
        moving = []

        def add(move, *mask):
            nonlocal vector, moving
            for m in moving:
                vector = vector + m.value
            moving = [start(move, vector, *mask)] if move else []

        moving = [start(peer, owned[slot], slot) for slot in others]
        w3.t_two()
        w2.t_full()
        step()

        w3.t_three()
        w2.t_up()
        w1.t_share()
        add(core_swap)
        step()

        w3.t_full()
        w2.t_out()
        add(chip_swap, 1)
        grad_fc2 = w1.joined()
        step()

        w3.t_up()
        w2.t_share()
        add(chip_swap, 2)
        step()

        w3.t_out()
        mask = 4
        while mask < chips:
            add(chip_swap, mask)
            mask *= 2
        grad_fc1 = w2.joined()
        step()

        w3.t_share()
        add(None)
        grad_out, grad_qkv = (g.value for g in w3.joined())
        layer_out = layer_out.value.reshape(inputs.shape)
        grad_input = grad_input.value.reshape(inputs.shape)
        grad_qv_bias = vector[: 2 * part].reshape(2, part)
        grad_fc1_bias = vector[2 * part : 2 * part + hidden]
        rest = vector[2 * part + hidden :].reshape(6, width)
        return (
            layer_out,
            grad_input,
            rest[0],
            rest[1],
            grad_qkv,
            grad_qv_bias,
            grad_out,
            rest[2],
            rest[3],
            rest[4],
            grad_fc1.value,
            grad_fc1_bias,
            grad_fc2.value,
            rest[5],
        )

    return local


def solution(mesh):
    chips, tensor = mesh.shape["dp"] // CORES, mesh.shape["tensor"]
    finer = Mesh(mesh.devices.reshape(chips, CORES, tensor), ("chip", "core", "tensor"))
    rows = ("chip", "core", "tensor")
    return jax.shard_map(
        build(chips, tensor),
        mesh=finer,
        in_specs=(
            P(rows, None, None),
            P(rows, None),
            P(rows, None, None),
            P(),
            P(),
            P(None, None, "tensor"),
            P(None, "tensor"),
            P("tensor", None),
            P(),
            P(),
            P(),
            P(None, "tensor"),
            P("tensor"),
            P("tensor", None),
            P(),
        ),
        out_specs=(
            P(rows, None, None),
            P(rows, None, None),
            P(),
            P(),
            P(None, None, "tensor"),
            P(None, "tensor"),
            P("tensor", None),
            P(),
            P(),
            P(),
            P(None, "tensor"),
            P("tensor"),
            P("tensor", None),
            P(),
        ),
        check_vma=False,
    )
```

```python
import functools

import jax
import jax.numpy as jnp
from jax import lax
from jax.experimental import pallas as pl
from jax.experimental.pallas import tpu as pltpu
from jax.sharding import Mesh, PartitionSpec as P

HD = 64
BUF = 64
EPS = 1e-06
CORES = 2
FAST = 192
LANES = 256
TILE = 512

f32 = jnp.float32
bf16 = jnp.bfloat16
NT = ((1,), (1,))
TN = ((0,), (0,))


def dot(a, b, dims=((1,), (0,))):
    return lax.dot_general(a, b, (dims, ((), ())), preferred_element_type=f32)


def spans(flags, seq_len, body):
    if seq_len <= FAST:
        body(seq_len)
        return

    @pl.when(flags[0] == 1)
    def _():
        body(FAST)

    @pl.when(flags[0] == 0)
    def _():
        body(seq_len)


def whole(shape):
    return pl.BlockSpec(shape, lambda *_: (0,) * len(shape), pipeline_mode=pl.Buffered(1))


def kernel_call(name, body, flags, args, in_specs, out_specs, out_shape, grid=(1,), **kw):
    return pl.pallas_call(
        body,
        name=name,
        grid_spec=pltpu.PrefetchScalarGridSpec(
            num_scalar_prefetch=1,
            grid=grid,
            in_specs=in_specs,
            out_specs=out_specs,
            scratch_shapes=kw.pop("scratch", ()),
        ),
        out_shape=out_shape,
        compiler_params=pltpu.CompilerParams(vmem_limit_bytes=kw.pop("vmem", 28 << 20)),
        cost_estimate=pl.CostEstimate(flops=1000, bytes_accessed=1000, transcendentals=0),
        **kw,
    )(flags, *args)


def picks(keep_row, span):
    seq_len = keep_row.shape[1]
    upto = lax.broadcasted_iota(jnp.int32, (seq_len, seq_len), 0) <= lax.broadcasted_iota(
        jnp.int32, (seq_len, seq_len), 1
    )
    keep_rows = jnp.broadcast_to(keep_row, (16, seq_len))
    rank = dot(keep_rows.astype(bf16), upto.astype(f32).astype(bf16))[0:1]
    place = lax.broadcasted_iota(jnp.int32, (span, seq_len), 0).astype(f32) + 1.0
    hit = jnp.where(place == rank, keep_row, 0.0)
    return hit.astype(bf16)


def norm_parts(values):
    centred = values - jnp.mean(values, axis=-1, keepdims=True)
    inverse = lax.rsqrt(jnp.mean(centred * centred, axis=-1, keepdims=True) + EPS)
    return centred * inverse, inverse


def norm_grad(grad_rows, unit, inverse, gain):
    scaled = grad_rows * gain
    centred = (
        scaled
        - jnp.mean(scaled, axis=-1, keepdims=True)
        - unit * jnp.mean(scaled * unit, axis=-1, keepdims=True)
    )
    return centred * inverse


def col_sum(values):
    return jnp.sum(values, axis=0, keepdims=True)


def prep_kernel(seq_len, images, flags, x, cot, keep, gain, bias, xc, normed, top, top_sum):
    def body(span):
        total = jnp.zeros(top_sum.shape, f32)
        for i in range(images):
            pick = picks(keep[i : i + 1, :], span)
            rows = slice(i * span, (i + 1) * span)
            source = slice(i * seq_len, (i + 1) * seq_len)
            kept = dot(pick, x[source, :])
            xc[rows, :] = kept.astype(bf16)
            normed[rows, :] = (norm_parts(kept)[0] * gain[...] + bias[...]).astype(bf16)
            grad = dot(pick, cot[source, :])
            top[rows, :] = grad.astype(bf16)
            total = total + col_sum(grad)
        top_sum[...] = total

    spans(flags, seq_len, body)


def head_masks(heads):
    lane = lax.broadcasted_iota(jnp.int32, (1, heads * HD), 1)
    return [(lane >= h * HD) & (lane < (h + 1) * HD) for h in range(heads)]


def softmax_rows(q, k, count):
    raw = dot(q, k, NT)
    column = lax.broadcasted_iota(jnp.int32, raw.shape, 1)
    raw = jnp.where(column < count, raw, -1e30)
    raised = jnp.exp(raw - jnp.max(raw, axis=-1, keepdims=True))
    return raised / jnp.sum(raised, axis=-1, keepdims=True)


def attend_kernel(seq_len, images, flags, normed, w, shift, proj, mixed):
    heads = mixed.shape[1] // HD

    def body(span):
        masks = head_masks(heads)
        for c in range(3):
            value = dot(normed[: images * span, :], w[c]) + shift[c]
            proj[c, : images * span, :] = value.astype(bf16)
        for i in range(images):
            rows = slice(i * span, (i + 1) * span)
            count = flags[1 + i]
            q, k, v = proj[0, rows, :], proj[1, rows, :], proj[2, rows, :]
            q = (q.astype(f32) * HD ** (-0.5)).astype(bf16)
            joined = jnp.zeros(q.shape, f32)
            for h in range(heads):
                probs = softmax_rows(jnp.where(masks[h], q, 0), k, count)
                joined = jnp.where(masks[h], dot(probs.astype(bf16), v), joined)
            mixed[rows, :] = joined.astype(bf16)

    spans(flags, seq_len, body)


def middle_kernel(seq_len, images, slots, flags, *refs):
    mixed, w, (xc, out_bias, gain, bias, mid, normed) = (
        refs[:slots],
        refs[slots : 2 * slots],
        refs[2 * slots :],
    )

    def body(span):
        for i in range(images):
            rows = slice(i * span, (i + 1) * span)
            total = xc[rows, :].astype(f32) + out_bias[...]
            for slot in range(slots):
                total = total + dot(mixed[slot][rows, :], w[slot][...])
            mid[rows, :] = total
            normed[rows, :] = (norm_parts(total)[0] * gain[...] + bias[...]).astype(bf16)

    spans(flags, seq_len, body)


def hidden_kernel(seq_len, images, flags, normed, w, bias, act, slope):
    def body(span):
        rows = images * span
        step = rows // 2
        for part in range(2):
            at = slice(part * step, (part + 1) * step)
            pre = dot(normed[at, :], w[...]) + bias[...]
            cdf = 0.5 * (1.0 + lax.erf(pre * 0.7071067811865476))
            act[at, :] = (pre * cdf).astype(bf16)
            slope[at, :] = (cdf + pre * jnp.exp(-0.5 * pre * pre) * 0.3989422804014327).astype(bf16)

    spans(flags, seq_len, body)


def ffn_kernel(seq_len, images, slots, flags, *refs):
    act, slope, w2, w1 = (refs[n * slots : (n + 1) * slots] for n in range(4))
    top, mid, bias, gain = refs[4 * slots : 4 * slots + 4]
    refs = refs[4 * slots + 4 :]
    grad_pre, pre_sums = refs[:slots], refs[slots : 2 * slots]
    low, grad_attn, sums, total, grad_norm = refs[2 * slots :]
    step, steps = pl.program_id(0), pl.num_programs(0)

    def body(span):
        rows = images * span

        @pl.when(step == 0)
        def _():
            total[:rows, :] = mid[:rows, :]
            grad_norm[:rows, :] = jnp.zeros((rows, grad_norm.shape[1]), f32)

        for slot in range(slots):

            @pl.when(step // (steps // slots) == slot)
            def _():
                total[:rows, :] += dot(act[slot][:rows, :], w2[slot][...])
                grad = dot(top[:rows, :], w2[slot][...], NT) * slope[slot][:rows, :].astype(f32)
                grad_pre[slot][:rows, :] = grad.astype(bf16)
                pre_sums[slot][...] = col_sum(grad_pre[slot][:rows, :].astype(f32))
                grad_norm[:rows, :] += dot(grad_pre[slot][:rows, :], w1[slot][...], NT)

        @pl.when(step == steps - 1)
        def _():
            for i in range(images):
                at = slice(i * span, (i + 1) * span)
                low[at, :] = (total[at, :] + bias[...]).astype(bf16)
                unit, inverse = norm_parts(mid[at, :])
                grad = grad_norm[at, :]
                full = top[at, :].astype(f32) + norm_grad(grad, unit, inverse, gain[...])
                grad_attn[at, :] = full.astype(bf16)
                part = [
                    col_sum(grad * unit),
                    col_sum(grad),
                    col_sum(grad_attn[at, :].astype(f32)),
                ]
                for n, row in enumerate(part):
                    sums[n : n + 1, :] = row if i == 0 else sums[n : n + 1, :] + row

    spans(flags, seq_len, body)


def attend_back_kernel(seq_len, images, first, flags, grad_attn, w_out, proj, w, *refs):
    if first:
        grad_proj, grad_norm, sums = refs
        base = None
    else:
        base, grad_proj, grad_norm, sums = refs
    heads = proj.shape[2] // HD
    start = pl.program_id(0) == 0

    def body(span):
        rows_all = images * span
        masks = head_masks(heads)

        @pl.when(start)
        def _():
            if first:
                grad_norm[:rows_all, :] = jnp.zeros((rows_all, grad_norm.shape[1]), f32)
            else:
                grad_norm[:rows_all, :] = base[:rows_all, :]

        for i in range(images):
            rows = slice(i * span, (i + 1) * span)
            count = flags[1 + i]
            grad_mixed = dot(grad_attn[rows, :], w_out[...], NT).astype(bf16)
            q, k, v = proj[0, rows, :], proj[1, rows, :], proj[2, rows, :]
            q_low = (q.astype(f32) * HD ** (-0.5)).astype(bf16)
            dq = jnp.zeros(q.shape, f32)
            dk, dv = dq, dq
            for h in range(heads):
                probs = softmax_rows(jnp.where(masks[h], q_low, 0), k, count)
                grad_prob = dot(jnp.where(masks[h], grad_mixed, 0), v, NT)
                delta = jnp.sum(probs * grad_prob, axis=-1, keepdims=True)
                grad_score = (probs * (grad_prob - delta)).astype(bf16)
                dv = jnp.where(masks[h], dot(probs.astype(bf16), grad_mixed, TN), dv)
                dq = jnp.where(masks[h], dot(grad_score, k), dq)
                dk = jnp.where(masks[h], dot(grad_score, q_low, TN), dk)
            grad_proj[0, rows, :] = (dq * HD ** (-0.5)).astype(bf16)
            grad_proj[1, rows, :] = dk.astype(bf16)
            grad_proj[2, rows, :] = dv.astype(bf16)
        for c in range(3):
            grad_norm[:rows_all, :] += dot(grad_proj[c, :rows_all, :], w[c], NT)
        sums[0:1, :] = col_sum(grad_proj[0, :rows_all, :].astype(f32))
        sums[1:2, :] = col_sum(grad_proj[2, :rows_all, :].astype(f32))

    spans(flags, seq_len, body)


def spread_kernel(seq_len, images, flags, value, keep, out):
    def body(span):
        for i in range(images):
            rows = slice(i * span, (i + 1) * span)
            pick = picks(keep[i : i + 1, :], span)
            out[i * seq_len : (i + 1) * seq_len, :] = dot(pick, value[rows, :], TN).astype(bf16)

    spans(flags, seq_len, body)


def last_kernel(seq_len, images, flags, grad_norm, xc, grad_attn, gain, keep, out, sums):
    def body(span):
        for i in range(images):
            rows = slice(i * span, (i + 1) * span)
            unit, inverse = norm_parts(xc[rows, :].astype(f32))
            grad = grad_norm[rows, :]
            low = grad_attn[rows, :].astype(f32) + norm_grad(grad, unit, inverse, gain[...])
            low = low.astype(bf16)
            pick = picks(keep[i : i + 1, :], span)
            out[i * seq_len : (i + 1) * seq_len, :] = dot(pick, low, TN).astype(bf16)
            part = [col_sum(grad * unit), col_sum(grad)]
            for n, row in enumerate(part):
                sums[n : n + 1, :] = row if i == 0 else sums[n : n + 1, :] + row

    spans(flags, seq_len, body)


def grad_kernel(seq_len, images, slots, flags, *refs):
    left, right, rest = refs[: len(slots)], refs[len(slots) : 2 * len(slots)], refs[2 * len(slots) :]
    out = rest[-1]

    def body(span):
        rows = images * span
        for n in range(len(slots)):
            value = dot(left[n][:rows, :], right[n][:rows, :], TN)
            for came in rest[:-1]:
                value = value + came[n].astype(f32)
            out[n] = value.astype(bf16)

    spans(flags, seq_len, body)


def last_grad_kernel(seq_len, images, first, slots, flags, normed, top, *refs):
    mixed, right, rest = (
        refs[: len(slots)],
        refs[len(slots) : 2 * len(slots)],
        refs[2 * len(slots) :],
    )
    out = rest[-1]

    def finish(n, value):
        for came in rest[:-1]:
            value = value + came[n, 0].astype(f32)
        out[n, 0] = value.astype(bf16)

    def body(span):
        rows = images * span
        which = first + pl.program_id(0)

        @pl.when(which == 0)
        def _():
            for n in range(len(slots)):
                finish(n, dot(top[:rows, :], mixed[n][:rows, :], TN))

        @pl.when(which > 0)
        def _():
            for n in range(len(slots)):
                finish(n, dot(normed[:rows, :], right[n][0, :rows, :], TN))

    spans(flags, seq_len, body)


def assemble_kernel(spots, units, count, flags, *refs):
    pieces, outs, sems = refs[:count], refs[count:-1], refs[-1]
    copies = []
    for piece, places in zip(pieces, spots(flags)):
        begin = 0
        for out in outs:
            rows = out.shape[0] // units
            for c in range(0, out.shape[1], piece.shape[1]):
                for place in places:
                    copy = pltpu.make_async_copy(
                        piece.at[pl.ds(begin, rows), :],
                        out.at[
                            pl.ds(pl.multiple_of(place * rows, 16), rows), pl.ds(c, piece.shape[1])
                        ],
                        sems.at[len(copies)],
                    )
                    copy.start()
                    copies.append(copy)
                    begin += rows
    for copy in copies:
        copy.wait()


def fold_kernel(plan, flags, *refs):
    count = sum(sum(counts) for _, counts, _ in plan)
    ins, outs = list(refs[:count]), list(refs[count:])

    def take(n):
        got = ins[:n]
        del ins[:n]
        return got

    def put(group, at=...):
        total = group[0][at].astype(f32)
        for ref in group[1:]:
            total = total + ref[at].astype(f32)
        return total.astype(bf16)

    for kind, counts, where in plan:
        groups = [take(n) for n in counts]
        shape = groups[0][0].shape
        if kind == "rows":
            size = shape[-2] // 2
            for half in (1 - flags[where], flags[where]):
                at = (pl.ds(pl.multiple_of(half * size, 16), size), slice(None))
                at = (slice(None),) * (len(shape) - 2) + at
                outs.pop(0)[...] = put(groups[0], at)
        elif kind == "slots":
            for slot in range(shape[0]):
                outs.pop(0)[...] = put(groups[0], slot)
        elif kind == "pick":
            sent, held = outs.pop(0), outs.pop(0)
            for bit in range(2):

                @pl.when(flags[where] == bit)
                def _():
                    held[...] = put(groups[bit])
                    sent[...] = put(groups[1 - bit])

        elif kind == "sum":
            outs.pop(0)[...] = put(groups[0])
        elif kind == "order":
            out = outs.pop(0)
            for half, group in zip((flags[where], 1 - flags[where]), groups):
                begin = pl.multiple_of(half * shape[0], 16)
                out[pl.ds(begin, shape[0]), :] = put(group)
        elif kind == "join":
            out = outs.pop(0)
            for n, group in enumerate(groups):
                out[n * shape[0] : (n + 1) * shape[0], :] = put(group)
        else:
            size = shape[0] // 2
            for n in range(2):
                outs.pop(0)[...] = put(groups[0], slice(n * size, (n + 1) * size))


def place_kernel(count, flags, *refs):
    out = refs[count]
    for n in range(count):

        @pl.when(pl.program_id(0) == n)
        def _():
            out[...] = refs[n][...].astype(out.dtype)


def last_place_kernel(matrix, flags, *refs):
    pieces, (out, qkv) = refs[:4], refs[-2:]
    for n in range(4):
        which = matrix(n, flags)

        @pl.when((pl.program_id(0) == n) & (which == 0))
        def _():
            out[...] = pieces[n][...].astype(f32).T

        @pl.when((pl.program_id(0) == n) & (which > 0))
        def _():
            qkv[0] = pieces[n][...].astype(f32)


def swap(value, axis, size, mask):
    return lax.ppermute(value, axis, [(i, i ^ mask) for i in range(size)])


def after(values, *waits):
    return lax.optimization_barrier((values, waits))[0]


def build(chips, tensor):
    def core_swap(value):
        return swap(value, "core", CORES, 1)

    def chip_swap(value, mask):
        return swap(value, "chip", chips, mask)

    def peer(value, slot):
        return swap(value, "tensor", tensor, slot)

    def local(
        inputs,
        keep_mask,
        cotangent,
        ln1_gain,
        ln1_bias,
        w_qkv,
        qv_bias,
        w_out,
        out_bias,
        ln2_gain,
        ln2_bias,
        w_fc1,
        fc1_bias,
        w_fc2,
        fc2_bias,
    ):
        images, seq_len, width = inputs.shape
        tokens = images * seq_len
        part = w_qkv.shape[2]
        hidden = w_fc1.shape[1]
        slots = range(tensor)
        others = range(1, tensor)
        lanes = min(LANES, part)
        tile = min(TILE, hidden)
        core, chip = lax.axis_index("core"), lax.axis_index("chip")
        low, high = chip & 1, (chip >> 1) & 1
        like = jax.ShapeDtypeStruct
        static = functools.partial
        row = lambda v: v.reshape(1, -1)

        keep = jnp.concatenate([jnp.ones((images, BUF), f32), keep_mask.astype(f32)], axis=1)
        counts = BUF + jnp.sum(keep_mask, axis=1)
        place = jnp.stack([core, low, high]).astype(jnp.int32)
        flags = jnp.concatenate([jnp.all(counts <= FAST).astype(jnp.int32)[None], counts, place])
        shape2 = (tokens, width)
        g1, b1, g2, b2 = row(ln1_gain), row(ln1_bias), row(ln2_gain), row(ln2_bias)


        class Box:
            def __init__(self, value):
                self.value = value
                opened.append(self)

        opened = []
        begun = []
        gate = Box(flags)

        def step():
            values = lax.optimization_barrier([box.value for box in opened])
            for box, value in zip(opened, values):
                box.value = value
            opened[:] = [gate]
            begun[:] = [True]

        def run(name, body, args, in_specs, out_specs, out_shape, grid=(1,), **kw):
            args = [a.value if isinstance(a, Box) else a for a in args]
            got = kernel_call(
                name, body, gate.value, args, in_specs, out_specs, out_shape, grid, **kw
            )
            return [Box(g) for g in got] if isinstance(got, (list, tuple)) else Box(got)

        def start(move, value, *mask):
            value = value.value if isinstance(value, Box) else value
            return Box(move(after(value, gate.value) if begun else value, *mask))

        LOW, HIGH = 2 + images, 3 + images

        def fold(*plan):
            ins, outs, steps = [], [], []
            for kind, where, *groups in plan:
                groups = [[g.value if isinstance(g, Box) else g for g in group] for group in groups]
                for group in groups:
                    ins += group
                shape = groups[0][0].shape
                half = (*shape[:-2], shape[-2] // 2, shape[-1])
                outs += {
                    "rows": [half, half],
                    "slots": [shape[1:]] * shape[0],
                    "pick": [shape, shape],
                    "sum": [shape],
                    "order": [(2 * shape[0], *shape[1:])],
                    "join": [(len(groups) * shape[0], *shape[1:])],
                    "cut": [half, half],
                }[kind]
                steps.append((kind, [len(g) for g in groups], where))
            got = run(
                "fold",
                static(fold_kernel, steps),
                ins,
                [whole(v.shape) for v in ins],
                [whole(shape) for shape in outs],
                [like(shape, bf16) for shape in outs],
            )
            return [g.value for g in got]


        class Fetch:
            def __init__(self, shards, split):
                self.split, self.shards = split, shards
                units = self.units = 8 if split else 4
                own = self.places(core, low, high)[0]
                cols = min(w.shape[1] for w in shards)
                parts = []
                for w in shards:
                    rows = w.shape[0] // units
                    for c in range(0, w.shape[1], cols):
                        for place in own:
                            parts.append(
                                lax.dynamic_slice(w, (place * rows, c), (rows, min(cols, w.shape[1])))
                            )
                piece = jnp.concatenate(parts) if len(parts) > 1 else parts[0]
                self.mine = [start(peer, piece, slot) for slot in others]

            def places(self, co, lo, hi):
                if self.split:
                    return [(4 * co + lo, 4 * co + 2 + hi), (4 * co + 1 - lo,), (4 * co + 3 - hi,)]
                return [(2 * co + lo,), (2 * co + 1 - lo,)]

            def second(self):
                self.got = []
                for m in self.mine:
                    if self.split:
                        upper, lower = fold(("cut", 0, [m]))
                        beside = [start(chip_swap, upper, 1), start(chip_swap, lower, 2)]
                    else:
                        beside = [start(chip_swap, m, 1)]
                    self.got.append([m, *beside, start(core_swap, m)])

            def third(self):
                for got in self.got:
                    got += [start(core_swap, g) for g in got[1:-1]]

            def full(self):
                shapes = [w.shape for w in self.shards]

                def spots(f):
                    co, lo, hi = f[1 + images], f[2 + images], f[3 + images]
                    return self.places(co, lo, hi) + self.places(1 - co, lo, hi)

                return [
                    run(
                        "assemble",
                        static(assemble_kernel, spots, self.units, len(got)),
                        got,
                        [pl.BlockSpec(memory_space=pl.ANY)] * len(got),
                        [whole(shape) for shape in shapes],
                        [like(shape, bf16) for shape in shapes],
                        scratch=[pltpu.SemaphoreType.DMA((16,))],
                    )
                    for got in self.got
                ]

        class FetchLate(Fetch):
            def __init__(self, shard):
                self.split, self.shards, self.units = True, [shard], 8
                self.own = self.places(core, low, high)[0]
                self.pieces = []

            def places(self, co, lo, hi):
                return [(4 * co + lo, 4 * co + 2 + hi)]

            def first(self):
                rows = self.shards[0].shape[0] // 8
                place = self.own[len(self.pieces)]
                piece = lax.dynamic_slice_in_dim(self.shards[0], place * rows, rows, axis=0)
                self.pieces.append([start(peer, piece, slot) for slot in others])

            def second(self):
                self.got = [
                    [a, b, start(chip_swap, a, 1), start(chip_swap, b, 2)]
                    + [start(core_swap, a), start(core_swap, b)]
                    for a, b in zip(*self.pieces)
                ]

            def third(self):
                for got in self.got:
                    got += [start(core_swap, g) for g in got[2:4]]

            def full(self):
                def spots(f):
                    lo, hi = f[2 + images], f[3 + images]
                    return [
                        place
                        for co in (f[1 + images], 1 - f[1 + images])
                        for place in (
                            (4 * co + lo,),
                            (4 * co + 2 + hi,),
                            (4 * co + 1 - lo,),
                            (4 * co + 3 - hi,),
                        )
                    ]

                return [
                    run(
                        "assemble",
                        static(assemble_kernel, spots, 8, 8),
                        got,
                        [pl.BlockSpec(memory_space=pl.ANY)] * 8,
                        [whole(self.shards[0].shape)],
                        [like(self.shards[0].shape, bf16)],
                        scratch=[pltpu.SemaphoreType.DMA((16,))],
                    )
                    for got in self.got
                ]


        half_of = lambda own: (lambda f: f[1 + images]) if own else (lambda f: 1 - f[1 + images])

        class Plain:
            def __init__(self, name, left, right, block):
                self.name, self.left, self.right, self.block = name, left, right, block

            def make(self, which, own, came, begin=0, share=1):
                pick = lambda v: [v[slot] if len(v) > 1 else v[0] for slot in which]
                left, right = pick(self.left), pick(self.right)
                half_rows = left[0].value.shape[1] // 2
                size = half_rows // share
                block = min(self.block, size)
                first, per_half = begin * size // block, half_rows // block
                cols = right[0].value.shape[1]
                half = half_of(own)
                shape = (len(which), block, cols)
                spots = [
                    pl.BlockSpec(shape, lambda g, f, s=s, r=r: (s, r * (size // block) + g, 0))
                    for _, s, r in came
                ]
                return run(
                    f"{self.name}{which[0]}{'own' if own else 'away'}",
                    static(grad_kernel, seq_len, images, which),
                    (*left, *right, *[c for c, _, _ in came]),
                    [
                        pl.BlockSpec((tokens, block), lambda g, f: (0, half(f) * per_half + first + g))
                        for _ in left
                    ]
                    + [whole((tokens, cols)) for _ in right]
                    + spots,
                    pl.BlockSpec(shape, lambda g, f: (0, g, 0)),
                    like((len(which), size, cols), bf16),
                    grid=(size // block,),
                )

        class Packed:
            name = "qkv"

            def make(self, which, own, came, begin=0, share=1):
                size = 4 // share
                begin, half = begin * size, half_of(own)
                mats = [mixes[slot] for slot in which]
                rights = [grad_projs[slot] for slot in which]
                shape = (len(which), 1, width // 2, part)
                spots = [
                    pl.BlockSpec(shape, lambda g, f, s=s, r=r: (s, r * size + g, 0, 0))
                    for _, s, r in came
                ]
                came = [c for c, _, _ in came]
                return run(
                    f"{self.name}{which[0]}{'own' if own else 'away'}",
                    static(last_grad_kernel, seq_len, images, begin, which),
                    (normed1, grad_attn, *mats, *rights, *came),
                    [pl.BlockSpec((tokens, width // 2), lambda g, f: (0, half(f)))] * 2
                    + [whole((tokens, part)) for _ in mats]
                    + [
                        pl.BlockSpec(
                            (1, tokens, part), lambda g, f: (jnp.maximum(begin + g - 1, 0), 0, 0)
                        )
                        for _ in rights
                    ]
                    + spots,
                    pl.BlockSpec(shape, lambda g, f: (0, g, 0, 0)),
                    like((len(which), size, width // 2, part), bf16),
                    grid=(size,),
                )

        class Reduce:
            def __init__(self, source):
                self.source = source

            def k_away(self):
                self.made = self.source.make([*slots], False, ())

            def t_core(self):
                self.came = start(core_swap, self.made)

            def k_own(self):
                make, came = self.source.make, self.came
                self.first = [make([slot], True, [(came, slot, 0)], 0, 2) for slot in others]
                self.second = make([*slots], True, [(came, 0, 1)], 1, 2)

            def t_one(self):
                self.sent = [start(peer, value, slot) for value, slot in zip(self.first, others)]
                total = self.second.value
                total = total.reshape(tensor, -1, total.shape[-1])
                sent, self.held_b = fold(("rows", LOW, [total]))
                self.moving_b = start(chip_swap, sent, 1)

            def k_mid(self):
                self.total = self.source.make([0], True, [(self.came, 0, 0)], 0, 2)

            def t_two(self):
                cols = self.total.value.shape[-1]
                parts = [v.value.reshape(-1, cols) for v in (self.total, *self.sent)]
                sent, self.held_a, self.held_b, *others_b = fold(
                    ("rows", LOW, parts), ("slots", 0, [self.held_b, self.moving_b])
                )
                self.moving_a = start(chip_swap, sent, 1)
                self.moving_b = [start(peer, v, slot) for v, slot in zip(others_b, others)]

            def t_z(self):
                sent, self.held = fold(
                    ("pick", HIGH, [self.held_a, self.moving_a], [self.held_b, *self.moving_b])
                )
                self.moving = start(chip_swap, sent, 2)

            def t_full(self):
                mask = 4
                while mask < chips:
                    (self.held,) = fold(("sum", 0, [self.held, self.moving]))
                    self.moving = start(chip_swap, self.held, mask)
                    mask *= 2

            def t_up(self):
                (self.held,) = fold(("sum", 0, [self.held, self.moving]))
                self.moving = start(chip_swap, self.held, 2)

            def t_out(self):
                (self.held,) = fold(("order", HIGH, [self.held], [self.moving]))
                self.moving = start(chip_swap, self.held, 1)

            def t_share(self):
                pieces = [self.held, self.moving.value]
                self.pieces = pieces + [start(core_swap, p) for p in pieces]

            def joined(self):
                pieces = self.pieces
                rows, cols = pieces[0].shape
                rows //= 2

                def spot(n):
                    return lambda w, i, f: (jnp.where(w == n, i, jnp.where(w < n, 0, 1)), 0)

                def place(w, i, f):
                    half = f[1 + images] ^ (w // 2)
                    return (half * 4 + i * 2 + (f[2 + images] ^ (w % 2)), 0)

                return run(
                    f"{self.source.name}join",
                    static(place_kernel, 4),
                    pieces,
                    [pl.BlockSpec((rows, cols), spot(n)) for n in range(4)],
                    pl.BlockSpec((rows, cols), place),
                    like((8 * rows, cols), f32),
                    grid=(4, 2),
                )

        class Apart(Reduce):
            def t_one(self):
                self.sent = [start(peer, value, slot) for value, slot in zip(self.first, others)]
                total = self.second.value
                total = total.reshape(tensor, -1, total.shape[-1])
                sent, self.held_b = fold(("rows", HIGH, [total]))
                self.moving_b = start(chip_swap, sent, 2)

            def t_three(self):
                sent_a, self.held_a, sent_b, self.held_b = fold(
                    ("rows", HIGH, [self.held_a, self.moving_a]),
                    ("rows", LOW, [self.held_b, *self.moving_b]),
                )
                self.moving_a = start(chip_swap, sent_a, 2)
                self.moving_b = start(chip_swap, sent_b, 1)

            def t_full(self):
                (self.held,) = fold(
                    ("join", 0, [self.held_a, self.moving_a], [self.held_b, self.moving_b])
                )
                self.moving = start(chip_swap, self.held, 4)
                mask = 8
                while mask < chips:
                    (self.held,) = fold(("sum", 0, [self.held, self.moving]))
                    self.moving = start(chip_swap, self.held, mask)
                    mask *= 2

            def t_up(self):
                self.held_a, self.held_b = fold(("cut", 0, [self.held, self.moving]))
                self.moving_a = start(chip_swap, self.held_a, 2)
                self.moving_b = start(chip_swap, self.held_b, 1)

            def t_out(self):
                self.held_a, self.held_b = fold(
                    ("order", HIGH, [self.held_a], [self.moving_a]),
                    ("order", LOW, [self.held_b], [self.moving_b]),
                )
                self.moving_a = start(chip_swap, self.held_a, 1)
                self.moving_b = start(chip_swap, self.held_b, 2)

            def t_share(self):
                pieces = [self.held_a, self.moving_a.value, self.held_b, self.moving_b.value]
                self.pieces = pieces + [start(core_swap, p) for p in pieces]

            def joined(self):
                def matrix(n, f):
                    bit = jnp.where(n % 4 < 2, f[2 + images], f[3 + images])
                    return 2 * ((n % 4) // 2) + (bit ^ (n % 2))

                half = width // 2
                placed = ()
                for far in range(2):
                    placed = run(
                        f"qkvjoin{far}",
                        static(last_place_kernel, matrix),
                        (*self.pieces[4 * far : 4 * far + 4], *placed),
                        [whole((half, part))] * 4
                        + [pl.BlockSpec(memory_space=pl.ANY)] * len(placed),
                        [
                            pl.BlockSpec((part, half), lambda w, f: (0, f[1 + images] ^ far)),
                            pl.BlockSpec(
                                (1, half, part),
                                lambda w, f: (
                                    jnp.maximum(matrix(w, f) - 1, 0),
                                    f[1 + images] ^ far,
                                    0,
                                ),
                            ),
                        ],
                        [like((part, width), f32), like((3, width, part), f32)],
                        grid=(4,),
                        input_output_aliases={5: 0, 6: 1} if placed else {},
                    )
                return placed


        def attend(slot, w):
            qv = biases[slot].value[: 2 * part].reshape(2, 1, part)
            shift = jnp.stack([qv[0], jnp.zeros_like(qv[0]), qv[1]])
            return run(
                f"attend{slot}",
                static(attend_kernel, seq_len, images),
                (normed1, w, shift),
                [
                    whole(shape2),
                    pl.BlockSpec((3, width, lanes), lambda g, f: (0, 0, g)),
                    pl.BlockSpec((3, 1, lanes), lambda g, f: (0, 0, g)),
                ],
                [
                    pl.BlockSpec((3, tokens, lanes), lambda g, f: (0, 0, g)),
                    pl.BlockSpec((tokens, lanes), lambda g, f: (0, g)),
                ],
                [like((3, tokens, part), bf16), like((tokens, part), bf16)],
                grid=(part // lanes,),
            )

        def hide(slot):
            acts[slot], slopes[slot] = run(
                f"hidden{slot}",
                static(hidden_kernel, seq_len, images),
                (normed2, fc1[slot], row(biases[slot].value[2 * part :])),
                [
                    whole(shape2),
                    pl.BlockSpec((width, tile), lambda g, f: (0, g)),
                    pl.BlockSpec((1, tile), lambda g, f: (0, g)),
                ],
                [pl.BlockSpec((tokens, tile), lambda g, f: (0, g))] * 2,
                [like((tokens, hidden), bf16)] * 2,
                grid=(hidden // tile,),
            )

        def ffn():
            block = max(128, 2 * tile // tensor)
            steps = hidden // block

            def at(slot):
                return lambda g: jnp.clip(g - slot * steps, 0, steps - 1)

            across = [
                pl.BlockSpec((tokens, block), lambda g, f, at=at(slot): (0, at(g))) for slot in slots
            ]
            got = run(
                "ffn",
                static(ffn_kernel, seq_len, images, tensor),
                (*acts, *slopes, *fc2, *fc1, top, mid, row(fc2_bias), g2),
                [
                    *across,
                    *across,
                    *[
                        pl.BlockSpec((block, width), lambda g, f, at=at(slot): (at(g), 0))
                        for slot in slots
                    ],
                    *[
                        pl.BlockSpec((width, block), lambda g, f, at=at(slot): (0, at(g)))
                        for slot in slots
                    ],
                    whole(shape2),
                    whole(shape2),
                    whole((1, width)),
                    whole((1, width)),
                ],
                [
                    *across,
                    *[
                        pl.BlockSpec((1, block), lambda g, f, at=at(slot): (0, at(g)))
                        for slot in slots
                    ],
                    whole(shape2),
                    whole(shape2),
                    whole((3, width)),
                ],
                [
                    *[like((tokens, hidden), bf16)] * tensor,
                    *[like((1, hidden), f32)] * tensor,
                    like(shape2, bf16),
                    like(shape2, bf16),
                    like((3, width), f32),
                ],
                grid=(tensor * steps,),
                scratch=[pltpu.VMEM(shape2, f32)] * 2,
                vmem=40 << 20,
            )
            grad_pres[:], pre_sums[:] = got[:tensor], got[tensor : 2 * tensor]
            return got[2 * tensor :]

        def attend_back(slot):
            nonlocal grad_norm1
            first = grad_norm1 is None
            tiles = pl.BlockSpec((3, tokens, lanes), lambda g, f: (0, 0, g))
            grad_projs[slot], grad_norm1, proj_sums[slot] = run(
                f"aback{slot}",
                static(attend_back_kernel, seq_len, images, first),
                (grad_attn, out[slot], projs[slot], qkv[slot]) + (() if first else (grad_norm1,)),
                [
                    whole(shape2),
                    pl.BlockSpec((lanes, width), lambda g, f: (g, 0)),
                    tiles,
                    pl.BlockSpec((3, width, lanes), lambda g, f: (0, 0, g)),
                ]
                + ([] if first else [whole(shape2)]),
                [tiles, whole(shape2), pl.BlockSpec((2, lanes), lambda g, f: (0, g))],
                [like((3, tokens, part), bf16), like(shape2, f32), like((2, part), f32)],
                grid=(part // lanes,),
            )

        acts, slopes = [None] * tensor, [None] * tensor
        grad_pres, pre_sums = [None] * tensor, [None] * tensor
        grad_projs, proj_sums, grad_norm1 = [None] * tensor, [None] * tensor, None


        get_attn = Fetch([w_qkv.reshape(3 * width, part), w_out], False)
        small = jnp.concatenate([qv_bias.reshape(-1), fc1_bias])
        biases = [Box(small)] + [start(peer, small, slot) for slot in others]
        xc, normed1, top, top_sum = run(
            "prep",
            static(prep_kernel, seq_len, images),
            (inputs.reshape(shape2), cotangent.reshape(shape2), keep, g1, b1),
            [whole(shape2), whole(shape2), whole(keep.shape), whole(g1.shape), whole(b1.shape)],
            [whole(shape2), whole(shape2), whole(shape2), whole((1, width))],
            [like(shape2, bf16), like(shape2, bf16), like(shape2, bf16), like((1, width), f32)],
        )
        seen = [attend(0, w_qkv)]
        step()

        get_attn.second()
        get_fc1 = Fetch([w_fc1], True)
        step()

        get_attn.third()
        get_fc1.second()
        get_fc2 = FetchLate(w_fc2)
        get_fc2.first()
        qkv, out = [w_qkv], [w_out]
        for w, w_2 in get_attn.full():
            qkv.append(w.value.reshape(3, width, part))
            out.append(w_2)
        for slot in others:
            seen.append(attend(slot, qkv[slot]))
        projs, mixes = [s[0] for s in seen], [s[1] for s in seen]
        mid, normed2 = run(
            "middle",
            static(middle_kernel, seq_len, images, tensor),
            (*mixes, *out, xc, row(out_bias), g2, b2),
            [whole((tokens, part))] * tensor
            + [whole((part, width))] * tensor
            + [whole(shape2), whole((1, width)), whole((1, width)), whole((1, width))],
            [whole(shape2), whole(shape2)],
            [like(shape2, f32), like(shape2, bf16)],
        )
        step()

        get_fc1.third()
        get_fc2.first()
        fc1 = [w_fc1] + [w for w, in get_fc1.full()]
        for slot in slots:
            hide(slot)
        w1 = Reduce(Plain("fc2", acts, [top], TILE))
        w1.k_away()
        step()

        w1.t_core()
        get_fc2.second()
        w1.k_own()
        step()


        w1.t_one()
        get_fc2.third()
        fc2 = [w_fc2] + [w for w, in get_fc2.full()]
        low_out, grad_attn, sums2 = ffn()
        w2 = Reduce(Plain("fc1", [normed2], grad_pres, 256))
        w2.k_away()
        w1.k_mid()
        step()

        w1.t_two()
        w2.t_core()
        w2.k_own()
        step()

        w1.t_z()
        attend_back(0)
        step()

        w2.t_one()
        w1.t_full()
        for slot in others:
            attend_back(slot)
        w3 = Apart(Packed())
        w3.k_away()
        w2.k_mid()
        step()

        w2.t_two()
        w3.t_core()
        w1.t_up()
        w3.k_own()
        step()

        w2.t_z()
        grad_input, sums1 = run(
            "last",
            static(last_kernel, seq_len, images),
            (grad_norm1, xc, grad_attn, g1, keep),
            [whole(shape2), whole(shape2), whole(shape2), whole((1, width)), whole(keep.shape)],
            [whole(shape2), whole((2, width))],
            [like(shape2, bf16), like((2, width), f32)],
        )
        layer_out = run(
            "spread",
            static(spread_kernel, seq_len, images),
            (low_out, keep),
            [whole(shape2), whole(keep.shape)],
            whole(shape2),
            like(shape2, bf16),
        )
        w3.t_one()
        w1.t_out()
        w3.k_mid()
        step()

        common = jnp.concatenate(
            [
                sums1.value.reshape(-1),
                sums2.value[2],
                sums2.value[0],
                sums2.value[1],
                top_sum.value[0],
            ]
        )
        owned = [
            jnp.concatenate(
                [proj_sums[slot].value.reshape(-1), pre_sums[slot].value.reshape(-1), common]
            )
            for slot in slots
        ]
        vector = owned[0]
        moving = []

        def add(move, *mask):
            nonlocal vector, moving
            for m in moving:
                vector = vector + m.value
            moving = [start(move, vector, *mask)] if move else []

        moving = [start(peer, owned[slot], slot) for slot in others]
        w3.t_two()
        w2.t_full()
        step()

        w3.t_three()
        w2.t_up()
        w1.t_share()
        add(core_swap)
        step()

        w3.t_full()
        w2.t_out()
        add(chip_swap, 1)
        grad_fc2 = w1.joined()
        step()

        w3.t_up()
        w2.t_share()
        add(chip_swap, 2)
        step()

        w3.t_out()
        mask = 4
        while mask < chips:
            add(chip_swap, mask)
            mask *= 2
        grad_fc1 = w2.joined()
        step()

        w3.t_share()
        add(None)
        grad_out, grad_qkv = (g.value for g in w3.joined())
        layer_out = layer_out.value.reshape(inputs.shape)
        grad_input = grad_input.value.reshape(inputs.shape)
        grad_qv_bias = vector[: 2 * part].reshape(2, part)
        grad_fc1_bias = vector[2 * part : 2 * part + hidden]
        rest = vector[2 * part + hidden :].reshape(6, width)
        return (
            layer_out,
            grad_input,
            rest[0],
            rest[1],
            grad_qkv,
            grad_qv_bias,
            grad_out,
            rest[2],
            rest[3],
            rest[4],
            grad_fc1.value,
            grad_fc1_bias,
            grad_fc2.value,
            rest[5],
        )

    return local


def solution(mesh):
    chips, tensor = mesh.shape["dp"] // CORES, mesh.shape["tensor"]
    finer = Mesh(mesh.devices.reshape(chips, CORES, tensor), ("chip", "core", "tensor"))
    rows = ("chip", "core", "tensor")
    return jax.shard_map(
        build(chips, tensor),
        mesh=finer,
        in_specs=(
            P(rows, None, None),
            P(rows, None),
            P(rows, None, None),
            P(),
            P(),
            P(None, None, "tensor"),
            P(None, "tensor"),
            P("tensor", None),
            P(),
            P(),
            P(),
            P(None, "tensor"),
            P("tensor"),
            P("tensor", None),
            P(),
        ),
        out_specs=(
            P(rows, None, None),
            P(rows, None, None),
            P(),
            P(),
            P(None, None, "tensor"),
            P(None, "tensor"),
            P("tensor", None),
            P(),
            P(),
            P(),
            P(None, "tensor"),
            P("tensor"),
            P("tensor", None),
            P(),
        ),
        check_vma=False,
    )
```
